32 devices in a mesh: section: 2 (over x), dp: 4 (over y, core), tensor: 4 (over z).
Axes of the slice: x: 2, y: 2, z: 4, core: 2. Of those that a mesh axis runs over, the one named last changes fastest.
Arguments:
- tokens: bfloat16 [8, 704, 768], P('dp', 'tensor'), may hold values from -6 to 6
- segment_ids: int32 [8, 704], P('dp'), may hold values from 0 to 3, as said below
- cotangent: bfloat16 [8, 704, 768], P('dp', 'tensor'), may hold values from -6 to 6
- norm_gain1: float32 [2, 768], P('section'), may hold values from 0.5 to 1.5
- w_in: bfloat16 [2, 768, 3, 768], P('section', None, None, 'tensor'), may hold values from -0.21875 to 0.21875
- short_taps: float32 [2, 3, 3, 768], P('section', None, None, 'tensor'), may hold values from -4 to 4
- cond_taps: float32 [2, 3, 768], P('section', None, 'tensor'), may hold values from -4 to 4
- spectrum: float32 [2, 2, 705, 768], P('section', None, None, 'tensor'), may hold values from -6 to 6
- spectral_gain: float32 [2, 2, 768], P('section', None, 'tensor'), may hold values from 0.3 to 3
- w_out: bfloat16 [2, 768, 768], P('section', 'tensor'), may hold values from -0.4375 to 0.4375
- norm_gain2: float32 [2, 768], P('section'), may hold values from 0.5 to 1.5
- w_gate_up: bfloat16 [2, 768, 2, 3072], P('section', None, None, 'tensor'), may hold values from -0.21875 to 0.21875
- w_down: bfloat16 [2, 3072, 768], P('section', 'tensor'), may hold values from -0.15625 to 0.15625
Outputs:
- layer_out: float32 [2, 8, 704, 768], P('section', 'dp', 'tensor')
- grad_in: float32 [2, 8, 704, 768], P('section', 'dp', 'tensor')
- grad_norm_gain1: float32 [2, 768], P('section')
- grad_w_in: float32 [2, 768, 3, 768], P('section', None, None, 'tensor')
- grad_short_taps: float32 [2, 3, 3, 768], P('section', None, None, 'tensor')
- grad_cond_taps: float32 [2, 3, 768], P('section', None, 'tensor')
- grad_spectrum: float32 [2, 2, 705, 768], P('section', None, None, 'tensor')
- grad_spectral_gain: float32 [2, 2, 768], P('section', None, 'tensor')
- grad_w_out: float32 [2, 768, 768], P('section', 'tensor')
- grad_norm_gain2: float32 [2, 768], P('section')
- grad_w_gate_up: float32 [2, 768, 2, 3072], P('section', None, None, 'tensor')
- grad_w_down: float32 [2, 3072, 768], P('section', 'tensor')
The draws below stay inside these ranges and needn't reach their ends.
Inputs may be any that keep to these rules, and one draw needn't show every extreme that they name: `segment_ids`: in each pack the ids never fall along the rows, and each of the 4 ids holds one or more rows.
All inputs are finite; a program needn't handle non-finite values.
Results may differ from the reference program's by a relative error of at most 0.022.
The reference program's roundings to bfloat16 on the way count: a program that leaves them out, or rounds other values in their place, can miss the bound.
Values may be sent and summed in bfloat16 or wider, within the bound.
No kernel may reach another device: no remote copies, remote signals or barrier semaphores. Data moves between devices by JAX's collectives and lax.ppermute only.
A program may use at most 192 MiB of HBM per device.

```python
import math
import jax
import jax.numpy as jnp
from jax import lax

D = 768
FF = 3072
L = 704
SEGS = 4
FREQ = 705
PACKS = 8
LAYERS = 2


def draw_segment_ids(key, part):
    pack_keys = jax.random.split(key, PACKS)

    def one_pack(pack_key):
        order = jax.random.permutation(pack_key, L - 1)
        cuts = order[:SEGS - 1].astype(jnp.int32) + 1
        places = jnp.arange(L, dtype=jnp.int32)
        return jnp.sum((places[:, None] >= cuts[None, :]).astype(jnp.int32), axis=1)
    return jax.vmap(one_pack)(pack_keys).astype(jnp.int32)


def block_levels(key, shape, cuts, smallest, high):
    level = 1.0
    for axis_at, blocks in cuts:
        heights = jax.random.uniform(jax.random.fold_in(jax.random.fold_in(key, 6), axis_at), (blocks,), jnp.float32, smallest / len(cuts), high / len(cuts))
        level = level * jnp.repeat(jnp.exp(heights), shape[axis_at] // blocks).reshape((-1,) + (1,) * (len(shape) - 1 - axis_at))
    return level


def normal_values(stream_key, dims, width, reach, cuts=(), held_as=jnp.bfloat16):
    entries = jax.random.normal(stream_key, dims, jnp.float32) * width
    if len(cuts) > 0:
        entries = block_levels(stream_key, dims, cuts, -0.22, 0.18) * entries
    return jnp.clip(entries, min=-reach, max=reach).astype(held_as)


def setup_inputs(seed: int = 0) -> dict:
    splits = jax.random.split(jax.random.key(seed), 14)
    tokens = normal_values(splits[0], (PACKS, L, D), 1.0, 6.0, ((0, 4), (1, 4)))
    segment_ids = draw_segment_ids(jax.random.fold_in(splits[13], 71), 0)
    cotangent = normal_values(splits[2], (PACKS, L, D), 1.0, 6.0, ((0, 4), (1, 4)))
    norm_gain1 = jnp.clip(1.0 + 0.1 * jax.random.normal(splits[3], (LAYERS, D), jnp.float32), 0.5, 1.5)
    w_in = normal_values(splits[4], (LAYERS, D, 3, D), D ** -0.5, 0.21875, ((0, 2), (3, 4)))
    short_taps = normal_values(splits[5], (LAYERS, 3, 3, D), 0.7, 4.0, ((0, 2), (3, 4)), jnp.float32)
    cond_taps = normal_values(splits[6], (LAYERS, 3, D), 0.7, 4.0, ((0, 2), (2, 4)), jnp.float32)
    spectrum = normal_values(splits[7], (LAYERS, 2, FREQ, D), 1.0, 6.0, ((0, 2), (3, 4)), jnp.float32)
    spectral_gain = jnp.clip(jnp.exp(math.log(3.0) - 2.3025851 * jax.random.uniform(splits[8], (LAYERS, 2, D), jnp.float32) ** block_levels(splits[8], (LAYERS, 2, D), ((0, 2), (2, 4)), -0.2, 0.2)), 0.3, 3.0)
    w_out = normal_values(splits[9], (LAYERS, D, D), (D // 4) ** -0.5, 0.4375, ((0, 2), (1, 4)))
    norm_gain2 = jnp.clip(1.0 + 0.1 * jax.random.normal(splits[10], (LAYERS, D), jnp.float32), 0.5, 1.5)
    w_gate_up = normal_values(splits[11], (LAYERS, D, 2, FF), D ** -0.5, 0.21875, ((0, 2), (3, 4)))
    w_down = normal_values(splits[12], (LAYERS, FF, D), (FF // 2) ** -0.5, 0.15625, ((0, 2), (1, 4)))
    return dict(tokens=tokens, segment_ids=segment_ids, cotangent=cotangent, norm_gain1=norm_gain1, w_in=w_in, short_taps=short_taps, cond_taps=cond_taps, spectrum=spectrum, spectral_gain=spectral_gain, w_out=w_out, norm_gain2=norm_gain2, w_gate_up=w_gate_up, w_down=w_down)


@jax.custom_vjp
def low(v):
    return lax.optimization_barrier(v.astype(jnp.bfloat16)).astype(jnp.float32)

@jax.custom_vjp
def low_back(v):
    return v

def low_keep(v):
    return (low(v), None)

def low_pass(kept, grad):
    return (grad,)

def back_keep(v):
    return (v, None)

def back_low(kept, grad):
    return (low(grad),)
low.defvjp(low_keep, low_pass)
low_back.defvjp(back_keep, back_low)

def layer_norm(values, gain):
    row_mean = lax.optimization_barrier(jnp.mean(values, axis=-1, keepdims=True))
    centred = values - row_mean
    variance = lax.optimization_barrier(jnp.mean(centred * centred, axis=-1, keepdims=True))
    return centred * lax.rsqrt(variance + 1e-05) * gain

def neighbours(segments, dtype):
    equal = (segments[1:] == segments[:-1]).astype(dtype)
    blank = jnp.zeros((1,), dtype)
    return (jnp.concatenate([blank, equal]), jnp.concatenate([equal, blank]))

def masked_short(values, taps, same_prev, same_next):
    blank = jnp.zeros((1, values.shape[1]), values.dtype)
    before = jnp.concatenate([blank, values[:-1]], axis=0) * same_prev[:, None]
    after = jnp.concatenate([values[1:], blank], axis=0) * same_next[:, None]
    return taps[0] * before + taps[1] * values + taps[2] * after

def orchid_mix(proj, short_taps, cond_taps, spectrum, spectral_gain, segments):
    pack_len = proj.shape[0]
    channels = proj.shape[2]
    same_prev, same_next = neighbours(segments, proj.dtype)
    shorted = masked_short(proj.reshape(pack_len, 3 * channels), short_taps.reshape(3, 3 * channels), same_prev, same_next)
    query = shorted[:, :channels]
    key_part = shorted[:, channels:2 * channels]
    value_part = shorted[:, 2 * channels:]
    condition = masked_short(key_part, cond_taps, same_prev, same_next)
    period = 2 * pack_len
    cond_hat = jnp.fft.rfft(condition, n=period, axis=0)
    scale_in = spectral_gain[0] / math.sqrt(pack_len)
    filt_re = spectrum[0] + spectral_gain[1] * jnp.tanh(scale_in * jnp.real(cond_hat))
    filt_im = spectrum[1] + spectral_gain[1] * jnp.tanh(scale_in * jnp.imag(cond_hat))
    masks = (segments[:, None] == jnp.arange(SEGS, dtype=jnp.int32)[None, :]).astype(proj.dtype)
    pieces = masks[:, :, None] * value_part[:, None, :]
    piece_hat = jnp.fft.rfft(pieces, n=period, axis=0)
    product = piece_hat * lax.complex(filt_re, filt_im)[:, None, :]
    conv = jnp.fft.irfft(product, n=period, axis=0)[:pack_len]
    mixed = lax.optimization_barrier(jnp.sum(conv * masks[:, :, None], axis=1))
    return query * mixed

def layer(layer_input, params, segments):
    gain_one, w_in, short_taps, cond_taps, spectrum, spectral_gain, w_out, gain_two, w_gate_up, w_down = params
    highest = lax.Precision.HIGHEST
    normed = low(layer_norm(layer_input, gain_one))
    proj = low_back(jnp.einsum('ld,dke->lke', normed, w_in, precision=highest))
    mixed = low(orchid_mix(proj, short_taps, cond_taps, spectrum, spectral_gain, segments))
    hidden = layer_input + low_back(jnp.dot(mixed, w_out, precision=highest))
    normed_two = low(layer_norm(hidden, gain_two))
    gate = low_back(jnp.dot(normed_two, w_gate_up[:, 0], precision=highest))
    up_part = low_back(jnp.dot(normed_two, w_gate_up[:, 1], precision=highest))
    act = low(jax.nn.silu(gate) * up_part)
    return hidden + low_back(jnp.dot(act, w_down, precision=highest))

def run_section(inputs, params, segment_ids):
    checked = jax.checkpoint(layer)

    def one_pack(state, item):
        return (state, checked(item[0], params, item[1]))
    start = jnp.zeros((), jnp.float32)
    return lax.scan(one_pack, start, (inputs, segment_ids))[1]

def reference(tokens, segment_ids, cotangent, norm_gain1, w_in, short_taps, cond_taps, spectrum, spectral_gain, w_out, norm_gain2, w_gate_up, w_down):
    stacked = (norm_gain1, w_in.astype(jnp.float32), short_taps, cond_taps, spectrum, spectral_gain, w_out.astype(jnp.float32), norm_gain2, w_gate_up.astype(jnp.float32), w_down.astype(jnp.float32))
    first = tuple((array[0] for array in stacked))
    second = tuple((array[1] for array in stacked))

    def section_fn(inputs, params):
        return run_section(inputs, params, segment_ids)
    start_rows = tokens.astype(jnp.float32)
    middle, pull_first = jax.vjp(section_fn, start_rows, first)
    final, pull_second = jax.vjp(section_fn, middle, second)
    grad_middle, grads_second = pull_second(cotangent.astype(jnp.float32))
    grad_start, grads_first = pull_first(grad_middle)
    grads = tuple((jnp.stack([one_grad, two_grad]) for one_grad, two_grad in zip(grads_first, grads_second)))
    layer_out = jnp.stack([middle, final])
    grad_in = jnp.stack([grad_start, grad_middle])
    return (layer_out, grad_in, grads[0], grads[1], grads[2], grads[3], grads[4], grads[5], grads[6], grads[7], grads[8], grads[9])
```

```python
from functools import partial
import math

import jax
import jax.numpy as jnp
from jax import lax
from jax.sharding import Mesh
from jax.sharding import PartitionSpec as P

SEGS = 4

high = lax.Precision.HIGH

ALL_AXES = ("section", "dq", "core", "th", "tl")


def permute(values, axes, mapping):
    sizes = [lax.axis_size(a) for a in axes]
    pairs = []
    total = math.prod(sizes)
    for source in range(total):
        place = []
        rest = source
        for size in reversed(sizes):
            place.append(rest % size)
            rest //= size
        place = tuple(reversed(place))
        target = mapping(*place)
        if target is None:
            continue
        flat = 0
        for size, at in zip(sizes, target):
            flat = flat * size + at
        pairs.append((source, flat))
    return lax.ppermute(values, axes if len(axes) > 1 else axes[0], pairs)


def swap_core(values):
    return permute(values, ("core",), lambda c: (1 - c,))


def swap_section(values):
    return permute(values, ("section",), lambda s: (1 - s,))


def shift(values, axis, by):
    size = lax.axis_size(axis)
    return permute(values, (axis,), lambda j: ((j + by) % size,))


def transposed(values):
    return permute(values, ("core", "th"), lambda c, h: (h, c))


def gather_rows(rows):
    peers = lax.axis_size("tl")
    blocks = [rows] + [shift(rows, "tl", k) for k in range(1, peers)]
    others = [swap_core(block) for block in blocks]
    return jnp.concatenate(blocks + others, axis=0)


def scatter_rows(partial_rows):
    peers = lax.axis_size("tl")
    count = partial_rows.shape[0] // (2 * peers)
    blocks = partial_rows.reshape(2, peers, count, partial_rows.shape[1])
    total = None
    for k in list(range(1, peers)) + [0]:
        block = blocks[0, k] + swap_core(blocks[1, k])
        if k:
            block = shift(block, "tl", -k)
        total = block if total is None else total + block
    return total


def reorder(rows, core, low):
    peers = lax.axis_size("tl")
    count = rows.shape[0] // (2 * peers)
    blocks = rows.reshape(2, peers, count, rows.shape[1])
    picked = []
    for c in range(2):
        for t in range(peers):
            picked.append(blocks[jnp.bitwise_xor(core, c), (low - t) % peers])
    return jnp.concatenate(picked, axis=0)


def layer_norm(values, gain):
    row_mean = jnp.mean(values, axis=-1, keepdims=True)
    centred = values - row_mean
    variance = jnp.mean(centred * centred, axis=-1, keepdims=True)
    return centred * lax.rsqrt(variance + 1e-05) * gain


def neighbours(segments):
    equal = (segments[1:] == segments[:-1]).astype(jnp.float32)
    blank = jnp.zeros((1,), jnp.float32)
    return (jnp.concatenate([blank, equal]), jnp.concatenate([equal, blank]))


def masked_short(values, taps, same_prev, same_next):
    blank = jnp.zeros((1, values.shape[1]), values.dtype)
    before = jnp.concatenate([blank, values[:-1]], axis=0) * same_prev[:, None]
    after = jnp.concatenate([values[1:], blank], axis=0) * same_next[:, None]
    return taps[0] * before + taps[1] * values + taps[2] * after


def spectral_tables(pack_len):
    period = 2 * pack_len
    freq_index = lax.broadcasted_iota(jnp.int32, (pack_len + 1, pack_len), 0)
    place_index = lax.broadcasted_iota(jnp.int32, (pack_len + 1, pack_len), 1)
    angle = (freq_index * place_index % period).astype(jnp.float32) * (2.0 * math.pi / period)
    cosine = jnp.cos(angle)
    sine = jnp.sin(angle)
    forward_table = jnp.concatenate([cosine, -sine], axis=0)
    freq_column = freq_index[:, :1]
    column_weight = jnp.where((freq_column == 0) | (freq_column == pack_len), 1.0, 2.0) / period
    inverse_table = jnp.concatenate([cosine * column_weight, -sine * column_weight], axis=0).T
    return (forward_table, inverse_table)


def orchid_mix(proj, short_taps, cond_taps, spectrum, spectral_gain, segments, tables):
    forward_table, inverse_table = tables
    pack_len = proj.shape[0]
    channels = proj.shape[1] // 3
    freqs = pack_len + 1
    same_prev, same_next = neighbours(segments)
    shorted = masked_short(proj, short_taps, same_prev, same_next)
    query = shorted[:, :channels]
    key_part = shorted[:, channels : 2 * channels]
    value_part = shorted[:, 2 * channels :]
    condition = masked_short(key_part, cond_taps, same_prev, same_next)
    cond_hat = jnp.dot(forward_table, condition, precision=high)
    scale_in = spectral_gain[0] / math.sqrt(pack_len)
    filt_re = spectrum[0] + spectral_gain[1] * jnp.tanh(scale_in * cond_hat[:freqs])
    filt_im = spectrum[1] + spectral_gain[1] * jnp.tanh(scale_in * cond_hat[freqs:])
    masks = (segments[:, None] == jnp.arange(SEGS, dtype=jnp.int32)[None, :]).astype(jnp.float32)
    pieces = (masks[:, :, None] * value_part[:, None, :]).reshape(pack_len, SEGS * channels)
    piece_hat = jnp.dot(forward_table, pieces, precision=high).reshape(2, freqs, SEGS, channels)
    real_part = piece_hat[0] * filt_re[:, None, :] - piece_hat[1] * filt_im[:, None, :]
    imag_part = piece_hat[0] * filt_im[:, None, :] + piece_hat[1] * filt_re[:, None, :]
    joined = jnp.concatenate([real_part, imag_part], axis=0).reshape(2 * freqs, SEGS * channels)
    conv = jnp.dot(inverse_table, joined, precision=high).reshape(pack_len, SEGS, channels)
    mixed = jnp.sum(conv * masks[:, :, None], axis=1)
    return query * mixed


def glu_act(both_parts):
    half_width = both_parts.shape[1] // 2
    return jax.nn.silu(both_parts[:, :half_width]) * both_parts[:, half_width:]


def dot32(spec, a, b):
    return jnp.einsum(spec, a, b, preferred_element_type=jnp.float32)


def forward_layer(rows, segments, params, tables, place):
    w_in, short_taps, cond_taps, spectrum, spectral_gain, w_out, gate_up, down, gain1, gain2 = params
    core, low = place
    normed, norm_pull = jax.vjp(layer_norm, rows, gain1)
    gathered = reorder(gather_rows(normed.astype(jnp.bfloat16)), core, low)
    proj = dot32("ld,dc->lc", gathered, w_in)
    mixer = partial(orchid_mix, segments=segments, tables=tables)
    mixed, mix_pull = jax.vjp(mixer, proj, short_taps, cond_taps, spectrum, spectral_gain)
    mixed_low = mixed.astype(jnp.bfloat16)
    hidden = rows + scatter_rows(dot32("lc,cd->ld", reorder(mixed_low, core, low), w_out))
    normed_two, norm_pull_two = jax.vjp(layer_norm, hidden, gain2)
    gathered_two = gather_rows(normed_two.astype(jnp.bfloat16))
    act, act_pull = jax.vjp(glu_act, dot32("ld,df->lf", gathered_two, gate_up))
    act_low = act.astype(jnp.bfloat16)
    result = hidden + scatter_rows(dot32("lf,fd->ld", act_low, down))
    return result, (norm_pull, gathered, mixed_low, mix_pull, norm_pull_two, gathered_two, act_pull, act_low)


def backward_layer(grad_out, params, saved, place):
    w_in, short_taps, cond_taps, spectrum, spectral_gain, w_out, gate_up, down, gain1, gain2 = params
    norm_pull, gathered, mixed_low, mix_pull, norm_pull_two, gathered_two, act_pull, act_low = saved
    core, low = place
    grad_rows = gather_rows(grad_out.astype(jnp.bfloat16))
    grad_act = dot32("ld,fd->lf", grad_rows, down)
    grad_both = act_pull(grad_act)[0].astype(jnp.bfloat16)
    grad_normed_two = scatter_rows(dot32("lf,df->ld", grad_both, gate_up))
    grad_down = dot32("lf,ld->fd", act_low, grad_rows)
    grad_gate_up = dot32("ld,lf->df", gathered_two, grad_both)
    grad_hidden_part, grad_gain2 = norm_pull_two(grad_normed_two)
    grad_hidden = grad_out + grad_hidden_part
    mix_rows = reorder(gather_rows(grad_hidden.astype(jnp.bfloat16)), core, low)
    grad_mixed = dot32("ld,cd->lc", mix_rows, w_out)
    grad_w_out = dot32("lc,ld->cd", mixed_low, mix_rows)
    grad_proj, grad_short, grad_cond, grad_spectrum, grad_spectral = mix_pull(grad_mixed)
    grad_proj_low = grad_proj.astype(jnp.bfloat16)
    grad_normed = scatter_rows(dot32("lc,dc->ld", reorder(grad_proj_low, core, low), w_in))
    grad_w_in = dot32("ld,lc->dc", gathered, grad_proj_low)
    grad_input_part, grad_gain1 = norm_pull(grad_normed)
    large = (grad_w_in, grad_spectrum, grad_w_out, grad_gate_up, grad_down)
    small = (grad_short, grad_cond, grad_spectral)
    return grad_hidden + grad_input_part, large, small, (grad_gain1, grad_gain2)


def parts_of(values):
    unit = 32 * lax.axis_size("dq")
    rows = values.shape[0]
    padded = -(-rows // unit) * unit
    if padded != rows:
        values = jnp.pad(values, ((0, padded - rows), (0, 0)))
    return values.reshape(lax.axis_size("dq"), padded // lax.axis_size("dq"), values.shape[1])


def join_dq(part, dq, mapping_ok=None):
    peers = lax.axis_size("dq")
    got = [part]
    for k in range(1, peers):
        if mapping_ok is None:
            got.append(shift(part, "dq", k))
        else:
            got.append(
                permute(
                    part,
                    ("dq", "core", "th"),
                    lambda d, c, h: ((d + k) % peers, c, h) if mapping_ok(c, h) else None,
                )
            )
    stack = jnp.stack(got)
    return jnp.concatenate([stack[(dq - d) % peers] for d in range(peers)], axis=0)


def fetch(own, place5):
    section, dq, core, high_part, low = place5
    rows = own.shape[0]
    parts = parts_of(own)
    own_part = parts[dq]
    crossed = lambda c, h: c != h
    moved_part = permute(
        own_part, ("core", "th"), lambda c, h: (h, c) if c != h else None
    )
    stays = core == high_part
    part = jnp.where(stays, own_part, moved_part)
    other_part = swap_section(part)
    moved = join_dq(moved_part, dq, crossed)[:rows]
    mine = jnp.where(stays, own, moved)
    other = join_dq(other_part, dq)[:rows]
    first = section == 0
    return jnp.where(first, mine, other), jnp.where(first, other, mine)


def reduce_large(first, second, place5):
    section, dq, core, high_part, low = place5
    low_type = jnp.bfloat16
    rows = first.shape[0]
    peers = lax.axis_size("dq")

    def over_dq(grad):
        parts = parts_of(grad)
        total = parts[dq]
        for k in range(1, peers):
            total = total + shift(parts[(dq + k) % peers].astype(low_type), "dq", k).astype(
                jnp.float32
            )
        return total

    first, second = over_dq(first), over_dq(second)
    is_first = section == 0
    total = jnp.where(is_first, first, second) + swap_section(
        jnp.where(is_first, second, first).astype(low_type)
    ).astype(jnp.float32)
    other = permute(
        total.astype(low_type), ("core", "th"), lambda c, h: (c, 1 - h) if c != h else None
    )
    total = (total + other.astype(jnp.float32)).astype(low_type)
    half = total.shape[0] // 2
    halves = total.reshape(2, half, total.shape[1])
    got = permute(total, ("core", "th"), lambda c, h: (1 - c, h) if c == h else None)
    total = jnp.where(core == high_part, total, got)
    mine = total.reshape(2, half, total.shape[1])[core]
    joined = [mine] + [shift(mine, "dq", k) for k in range(1, peers)]
    stack = jnp.stack(joined)
    across = swap_core(stack)
    both = jnp.stack([stack, across])
    ordered = []
    for d in range(peers):
        for c in range(2):
            ordered.append(both[jnp.bitwise_xor(core, c), (dq - d) % peers])
    return jnp.concatenate(ordered, axis=0)[:rows].astype(jnp.float32)


def reduce_small(values):
    for k in range(1, 2):
        values = values + swap_section(values)
    total = values
    for k in range(1, lax.axis_size("dq")):
        total = total + shift(values, "dq", k)
    total = total + permute(total, ("th",), lambda h: (1 - h,))
    return total


def per_device(
    tokens,
    segment_ids,
    cotangent,
    norm_gain1,
    w_in,
    short_taps,
    cond_taps,
    spectrum,
    spectral_gain,
    w_out,
    norm_gain2,
    w_gate_up,
    w_down,
):
    slots, row_count, width = tokens.shape
    pack_len = segment_ids.shape[1]
    channels = w_in.shape[3]
    hidden_cols = w_gate_up.shape[3]
    place5 = tuple(lax.axis_index(a) for a in ALL_AXES)
    section, dq, core, high_part, low = place5
    place = (core, low)
    packs = slots // 2

    tables = spectral_tables(pack_len)

    def own_slots(array):
        return lax.dynamic_slice_in_dim(array, section * packs, packs, 0)

    rows_in = transposed(own_slots(tokens))
    ids_both = jnp.stack([segment_ids, permute(segment_ids.astype(jnp.float32), ("core",), lambda c: (1 - c,)).astype(jnp.int32)])
    segments = own_slots(ids_both[jnp.bitwise_xor(core, high_part)])

    freqs = spectrum.shape[2]
    flat = {
        "w_in": w_in[0].reshape(width, 3 * channels),
        "spectrum": spectrum[0].reshape(2 * freqs, channels),
        "w_out": w_out[0],
        "gate_up": w_gate_up[0].reshape(width, 2 * hidden_cols),
        "down": w_down[0],
    }
    taps = jnp.concatenate(
        [short_taps[0].reshape(9, channels), cond_taps[0], spectral_gain[0]], axis=0
    )
    taps_t = transposed(taps)
    taps_o = swap_section(taps_t)
    gains = jnp.concatenate([norm_gain1, norm_gain2], axis=0)
    gains_o = swap_section(gains)
    first = section == 0
    taps_l = (jnp.where(first, taps_t, taps_o), jnp.where(first, taps_o, taps_t))
    gains_l = (jnp.where(first, gains, gains_o), jnp.where(first, gains_o, gains))
    fetched = {name: fetch(flat[name], place5) for name in ("w_in", "spectrum", "w_out", "gate_up", "down")}
    cot_in = transposed(own_slots(cotangent))

    def params_of(layer):
        t = taps_l[layer]
        short = t[:9].reshape(3, 3, channels).reshape(3, 3 * channels)
        return (
            fetched["w_in"][layer],
            short,
            t[9:12],
            fetched["spectrum"][layer].reshape(2, freqs, channels),
            t[12:14],
            fetched["w_out"][layer],
            fetched["gate_up"][layer],
            fetched["down"][layer],
            gains_l[layer][0],
            gains_l[layer][1],
        )

    params = (params_of(0), params_of(1))
    results = [[], []]
    saved = [[], []]
    for pack in range(packs):
        state = rows_in[pack].astype(jnp.float32)
        for layer in range(2):
            state, kept = forward_layer(state, segments[pack], params[layer], tables, place)
            results[layer].append(state)
            saved[layer].append(kept)
    grads_in = [[], []]
    large_sum = [None, None]
    small_sum = [None, None]
    gain_sum = [None, None]

    def add(old, new):
        return new if old is None else jax.tree.map(jnp.add, old, new)

    for pack in range(packs):
        state = cot_in[pack].astype(jnp.float32)
        for layer in (1, 0):
            state, large, small, gain = backward_layer(
                state, params[layer], saved[layer][pack], place
            )
            grads_in[layer].append(state)
            large_sum[layer] = add(large_sum[layer], large)
            small_sum[layer] = add(small_sum[layer], small)
            gain_sum[layer] = add(gain_sum[layer], gain)

    def deliver(by_layer):
        zero, one = jnp.stack(by_layer[0]), jnp.stack(by_layer[1])
        keep = transposed(jnp.where(first, zero, one))
        given = permute(
            jnp.where(first, one, zero),
            ("section", "core", "th"),
            lambda s, c, h: (1 - s, h, c),
        )
        lead = jnp.where(first, keep, given)
        trail = jnp.where(first, given, keep)
        return jnp.concatenate([lead, trail], axis=0)

    layer_out = deliver(results)
    grad_in = deliver(grads_in)

    names = ("w_in", "spectrum", "w_out", "gate_up", "down")
    large_first = dict(zip(names, large_sum[0]))
    large_second = dict(zip(names, large_sum[1]))
    for d in (large_first, large_second):
        d["spectrum"] = d["spectrum"].reshape(2 * freqs, channels)
    reduced = {n: reduce_large(large_first[n], large_second[n], place5) for n in names}

    def small_pack(small):
        short, cond, spectral = small
        return jnp.concatenate([short.reshape(9, channels), cond, spectral], axis=0)

    small_both = jnp.stack([small_pack(small_sum[0]), small_pack(small_sum[1])])
    small_both = transposed(reduce_small(small_both))
    small_mine = small_both[section]
    gain_both = jnp.stack([jnp.stack(gain_sum[0]), jnp.stack(gain_sum[1])])
    gain_both = lax.psum(gain_both, ALL_AXES)
    gain_mine = gain_both[section]
    return (
        layer_out[None],
        grad_in[None],
        gain_mine[0][None],
        reduced["w_in"].reshape(1, width, 3, channels),
        small_mine[:9].reshape(1, 3, 3, channels),
        small_mine[9:12][None],
        reduced["spectrum"].reshape(1, 2, freqs, channels),
        small_mine[12:14][None],
        reduced["w_out"][None],
        gain_mine[1][None],
        reduced["gate_up"].reshape(1, width, 2, hidden_cols),
        reduced["down"][None],
    )


def solution(mesh):
    sections, dps, tensors = (mesh.shape[a] for a in ("section", "dp", "tensor"))
    devices = mesh.devices.reshape(sections, dps // 2, 2, 2, tensors // 2)
    fine = Mesh(devices, ALL_AXES)
    dp = ("dq", "core")
    tensor = ("th", "tl")
    return jax.shard_map(
        per_device,
        mesh=fine,
        in_specs=(
            P(dp, tensor, None),
            P(dp, None),
            P(dp, tensor, None),
            P("section", None),
            P("section", None, None, tensor),
            P("section", None, None, tensor),
            P("section", None, tensor),
            P("section", None, None, tensor),
            P("section", None, tensor),
            P("section", tensor, None),
            P("section", None),
            P("section", None, None, tensor),
            P("section", tensor, None),
        ),
        out_specs=(
            P("section", dp, tensor, None),
            P("section", dp, tensor, None),
            P("section", None),
            P("section", None, None, tensor),
            P("section", None, None, tensor),
            P("section", None, tensor),
            P("section", None, None, tensor),
            P("section", None, tensor),
            P("section", tensor, None),
            P("section", None),
            P("section", None, None, tensor),
            P("section", tensor, None),
        ),
        check_vma=False,
    )
```

```python
from functools import partial
import math

import jax
import jax.numpy as jnp
import numpy as np
from jax import lax
from jax.experimental import pallas as pl
from jax.experimental.pallas import tpu as pltpu
from jax.sharding import Mesh
from jax.sharding import PartitionSpec as P

SEGS = 4

FTILE = 256
HTILE = 384
PEAK = 1.0e9
VMEM_LIMIT = 56 * 1024 * 1024

ALL_AXES = ("section", "dq", "core", "th", "tl")


def permute(values, axes, mapping):
    sizes = [lax.axis_size(a) for a in axes]
    pairs = []
    total = math.prod(sizes)
    for source in range(total):
        place = []
        rest = source
        for size in reversed(sizes):
            place.append(rest % size)
            rest //= size
        place = tuple(reversed(place))
        target = mapping(*place)
        if target is None:
            continue
        flat = 0
        for size, at in zip(sizes, target):
            flat = flat * size + at
        pairs.append((source, flat))
    return lax.ppermute(values, axes if len(axes) > 1 else axes[0], pairs)


def swap_core(values):
    return permute(values, ("core",), lambda c: (1 - c,))


def swap_section(values):
    return permute(values, ("section",), lambda s: (1 - s,))


def shift(values, axis, by):
    size = lax.axis_size(axis)
    return permute(values, (axis,), lambda j: ((j + by) % size,))


def transposed(values):
    return permute(values, ("core", "th"), lambda c, h: (h, c))


def chip_blocks(rows):
    return [rows] + [shift(rows, "tl", k) for k in range(1, lax.axis_size("tl"))]


def both_cores(blocks):
    return blocks + [swap_core(block) for block in blocks]


def gather_rows(rows):
    return both_cores(chip_blocks(rows))


def core_sums(blocks):
    peers = lax.axis_size("tl")
    order = list(range(1, peers)) + [0]
    sums = {k: blocks[k] + swap_core(blocks[peers + k]) for k in order}
    return [sums[k] for k in range(peers)]


def sent_sums(sums):
    return [shift(sums[k], "tl", -k) for k in range(1, len(sums))]


def add_sums(sums, moved):
    total = sums[0]
    for term in moved:
        total = total + term.astype(jnp.float32)
    return total


def chip_sums(sums):
    return add_sums(sums, sent_sums(sums))


def after(values, *events):
    return lax.optimization_barrier((values, events))[0]


class Line:
    def __init__(self):
        self.events = ()

    def take(self, values):
        return after(values, self.events)

    def mark(self, *events):
        self.events = events


def layer_norm(values, gain):
    row_mean = jnp.mean(values, axis=-1, keepdims=True)
    centred = values - row_mean
    variance = jnp.mean(centred * centred, axis=-1, keepdims=True)
    return centred * lax.rsqrt(variance + 1e-05) * gain


def neighbours(segments):
    equal = (segments[1:] == segments[:-1]).astype(jnp.float32)
    blank = jnp.zeros((1,), jnp.float32)
    return (jnp.concatenate([blank, equal]), jnp.concatenate([equal, blank]))


def table_size(pack_len):
    return -(-(pack_len + 1) // FTILE) * FTILE


def split(values):
    upper = values.astype(jnp.bfloat16)
    lower = (values - upper.astype(jnp.float32)).astype(jnp.bfloat16)
    return upper, lower


def mm(a, b):
    return jnp.dot(a, b, preferred_element_type=jnp.float32)


def mm_t(a, b):
    return lax.dot_general(a, b, (((1,), (1,)), ((), ())), preferred_element_type=jnp.float32)


def mm3(upper, lower, b_upper, b_lower):
    return mm(upper, b_upper) + (mm(upper, b_lower) + mm(lower, b_upper))


STEP = 32


def tables_kernel(coarse_cos, coarse_sin, fine_cos, fine_sin, cos_hi, cos_lo, sin_hi, sin_lo):
    def body(p, carry):
        cc = coarse_cos[pl.ds(p, 1), :]
        cs = coarse_sin[pl.ds(p, 1), :]
        rows = pl.ds(pl.multiple_of(p * STEP, STEP), STEP)
        upper, lower = split(cc * fine_cos[...] - cs * fine_sin[...])
        cos_hi[rows, :] = upper
        cos_lo[rows, :] = lower
        upper, lower = split(cs * fine_cos[...] + cc * fine_sin[...])
        sin_hi[rows, :] = upper
        sin_lo[rows, :] = lower
        return carry

    lax.fori_loop(0, cos_hi.shape[0] // STEP, body, 0)


def spectral_tables(pack_len):
    size = table_size(pack_len)
    period = 2 * pack_len
    column = np.arange(size, dtype=np.int64)[None, :]
    coarse = (np.arange(size // STEP, dtype=np.int64)[:, None] * STEP * column) % period
    fine = (np.arange(STEP, dtype=np.int64)[:, None] * column) % period
    to_angle = 2.0 * np.pi / period
    small = [f(x * to_angle).astype(np.float32) for x in (coarse, fine) for f in (np.cos, np.sin)]
    return pl.pallas_call(
        tables_kernel,
        out_shape=[jax.ShapeDtypeStruct((size, size), jnp.bfloat16)] * 4,
        cost_estimate=pl.CostEstimate(flops=int(4 * PEAK), bytes_accessed=0, transcendentals=0),
        name="tables",
    )(*small)


def row_before(values):
    return pltpu.roll(values, 1, 0)


def row_after(values):
    return pltpu.roll(values, values.shape[0] - 1, 0)


def freq_weight(pack_len, step, shape):
    f = lax.broadcasted_iota(jnp.int32, shape, 0) + step * FTILE
    edge = (f == 0) | (f == pack_len)
    weight = jnp.where(edge, 1.0, 2.0) / (2.0 * pack_len)
    return f <= pack_len, jnp.where(f <= pack_len, weight, 0.0)


def join(whole_rows, parts, places):
    for k, part in enumerate(parts):
        count = part.shape[0]
        at = pl.ds(pl.multiple_of(places[k] * count, 8), count)
        whole_rows[at, :] = part[...]


def mixer_kernel(nb, np_, order, places, *refs):
    rows = refs[:nb]
    w_parts, s_parts = refs[nb : nb + np_], refs[nb + np_ : nb + 2 * np_]
    refs = refs[nb + 2 * np_ :]
    (taps, cols, ch_r, cl_r, sh_r, sl_r, ch_c, cl_c, sh_c, sl_c) = refs[:10]
    parts = refs[10 : nb + 10]
    (gathered, mix, proj, long, cond_hat, piece_hat) = refs[nb + 10 : nb + 16]
    x_hi, x_lo, acc, query, w_in_out, spectrum = refs[nb + 16 :]
    step = pl.program_id(0)
    count = rows[0].shape[0]
    pack_len = proj.shape[0]
    width = mix.shape[2]
    scale = 1.0 / math.sqrt(pack_len)

    @pl.when(step == 0)
    def _():
        join(w_in_out, w_parts, places)
        for j in range(nb):
            gathered[j] = rows[j][...]
            at = pl.ds(pl.multiple_of(order[j] * count, 8), count)
            proj[at, :] = mm_t(rows[j][...], w_in_out[: 3 * width, :])
        prev = cols[:, 0:1]
        nxt = cols[:, 1:2]

        def short(values, w0, w1, w2):
            return w0 * (row_before(values) * prev) + w1 * values + w2 * (row_after(values) * nxt)

        def one(k):
            return short(
                proj[:, k * width : (k + 1) * width],
                taps[0, k : k + 1, :],
                taps[0, 3 + k : 4 + k, :],
                taps[0, 6 + k : 7 + k, :],
            )

        query[...] = one(0)
        condition = short(one(1), taps[0, 9:10, :], taps[0, 10:11, :], taps[0, 11:12, :])
        value = one(2)
        x_hi[pack_len:, :] = jnp.zeros((x_hi.shape[0] - pack_len, x_hi.shape[1]), jnp.bfloat16)
        x_lo[pack_len:, :] = jnp.zeros((x_hi.shape[0] - pack_len, x_hi.shape[1]), jnp.bfloat16)
        pieces = [value * cols[:, 2 + g : 3 + g] for g in range(SEGS)] + [condition]
        for g, piece in enumerate(pieces):
            upper, lower = split(piece)
            x_hi[:pack_len, g * width : (g + 1) * width] = upper
            x_lo[:pack_len, g * width : (g + 1) * width] = lower
        acc[...] = jnp.zeros_like(acc)

    wide = SEGS * width
    hat_re = mm3(ch_r[...], cl_r[...], x_hi[...], x_lo[...])
    hat_im = -mm3(sh_r[...], sl_r[...], x_hi[...], x_lo[...])
    v_re, v_im = hat_re[:, :wide], hat_im[:, :wide]
    c_re, c_im = hat_re[:, wide:], hat_im[:, wide:]
    cond_hat[0] = c_re
    cond_hat[1] = c_im
    piece_hat[0] = v_re
    piece_hat[1] = v_im
    gain_in = taps[0, 12:13, :] * scale
    gain_out = taps[0, 13:14, :]
    inside, weight = freq_weight(pack_len, step, c_re.shape)
    join(spectrum, s_parts, places)
    s_re = jnp.transpose(spectrum[:width, :])
    s_im = jnp.transpose(spectrum[width:, :])
    f_re = jnp.where(inside, s_re + gain_out * jnp.tanh(gain_in * c_re), 0.0) * weight
    f_im = jnp.where(inside, s_im + gain_out * jnp.tanh(gain_in * c_im), 0.0) * weight
    f_re = jnp.concatenate([f_re] * SEGS, axis=1)
    f_im = jnp.concatenate([f_im] * SEGS, axis=1)
    p_hi, p_lo = split(v_re * f_re - v_im * f_im)
    m_hi, m_lo = split(-(v_re * f_im + v_im * f_re))
    acc[...] += mm3(ch_c[...], cl_c[...], p_hi, p_lo) + mm3(sh_c[...], sl_c[...], m_hi, m_lo)

    @pl.when(step == pl.num_programs(0) - 1)
    def _():
        total = acc[:, :width] * cols[:, 2:3]
        for g in range(1, SEGS):
            total = total + acc[:, g * width : (g + 1) * width] * cols[:, 2 + g : 3 + g]
        long[...] = total
        query[...] = query[...] * total
        for j in range(nb):
            at = pl.ds(pl.multiple_of(order[j] * count, 8), count)
            mixed = query[at, :].astype(jnp.bfloat16)
            mix[j] = mixed
            parts[j][...] = mm(mixed, w_in_out[3 * width :, :])


def table_specs(size, pack_len):
    row = pl.BlockSpec((FTILE, size), lambda i: (i, 0))
    col = pl.BlockSpec((pack_len, FTILE), lambda i: (0, i))
    return [row] * 4 + [col] * 4


def whole(shape):
    zeros = (0,) * len(shape)
    return pl.BlockSpec(shape, lambda i: zeros)


def of_layer(layer, shape):
    rest = (0,) * len(shape)
    return pl.BlockSpec((1,) + shape, lambda i: (layer,) + rest)


SMEM = pl.BlockSpec(memory_space=pltpu.SMEM)


def part_specs(w_in_out, spectra):
    return [whole(p.shape) for p in w_in_out] + [
        pl.BlockSpec((p.shape[0], FTILE), lambda i: (0, i)) for p in spectra
    ]


def part_scratch(w_in_out, spectra):
    peers = len(w_in_out)
    return [
        pltpu.VMEM((peers * w_in_out[0].shape[0], w_in_out[0].shape[1]), jnp.bfloat16),
        pltpu.VMEM((peers * spectra[0].shape[0], FTILE), jnp.float32),
    ]


def mixer_forward(blocks, w_in_out, taps, cols, spectra, tables, order, places):
    layer = 0
    pack_len = cols.shape[0]
    nb = len(blocks)
    count, model = blocks[0].shape
    width = taps.shape[2]
    size = tables[0].shape[0]
    f32, low = jnp.float32, jnp.bfloat16
    out = pl.pallas_call(
        partial(mixer_kernel, nb, len(w_in_out)),
        grid=(size // FTILE,),
        in_specs=[SMEM, SMEM]
        + [whole((count, model))] * nb
        + part_specs(w_in_out, spectra)
        + [of_layer(layer, taps.shape[1:]), whole(cols.shape)]
        + table_specs(size, pack_len),
        out_specs=[whole((count, model))] * nb
        + [
            whole((nb, count, model)),
            whole((nb, count, width)),
            whole((pack_len, 3 * width)),
            whole((pack_len, width)),
            pl.BlockSpec((2, FTILE, width), lambda i: (0, i, 0)),
            pl.BlockSpec((2, FTILE, SEGS * width), lambda i: (0, i, 0)),
        ],
        out_shape=[jax.ShapeDtypeStruct((count, model), f32)] * nb
        + [
            jax.ShapeDtypeStruct((nb, count, model), low),
            jax.ShapeDtypeStruct((nb, count, width), low),
            jax.ShapeDtypeStruct((pack_len, 3 * width), f32),
            jax.ShapeDtypeStruct((pack_len, width), f32),
            jax.ShapeDtypeStruct((2, size, width), f32),
            jax.ShapeDtypeStruct((2, size, SEGS * width), f32),
        ],
        scratch_shapes=[
            pltpu.VMEM((size, (SEGS + 1) * width), low),
            pltpu.VMEM((size, (SEGS + 1) * width), low),
            pltpu.VMEM((pack_len, SEGS * width), f32),
            pltpu.VMEM((pack_len, width), f32),
        ]
        + part_scratch(w_in_out, spectra),
        compiler_params=pltpu.CompilerParams(vmem_limit_bytes=VMEM_LIMIT),
        cost_estimate=pl.CostEstimate(flops=int(26 * PEAK), bytes_accessed=0, transcendentals=0),
        name="mixer_forward",
    )(order, places, *blocks, *w_in_out, *spectra, taps, cols, *tables, *tables)
    return out[:nb], out[nb].reshape(pack_len, model), out[nb + 1].reshape(pack_len, width), out[nb + 2 :]


def mixer_grad_kernel(nb, np_, order, places, *refs):
    grads = refs[:nb]
    w_parts, s_parts = refs[nb : nb + np_], refs[nb + np_ : nb + 2 * np_]
    refs = refs[nb + 2 * np_ :]
    (taps, cols, proj, long, cond_hat, piece_hat) = refs[:6]
    (ch_r, cl_r, sh_r, sl_r, ch_c, cl_c, sh_c, sl_c) = refs[6:14]
    partials = refs[14 : nb + 14]
    gathered, proj_grad, grad_spectrum, grad_taps = refs[nb + 14 : nb + 18]
    x_hi, x_lo, acc, query_grad, full, w_in_out, spectrum = refs[nb + 18 :]
    step = pl.program_id(0)
    count = grads[0].shape[0]
    pack_len = proj.shape[0]
    width = long.shape[1]
    wide = SEGS * width
    scale = 1.0 / math.sqrt(pack_len)

    def short(values, w0, w1, w2):
        return (
            w0 * (row_before(values) * cols[:, 0:1])
            + w1 * values
            + w2 * (row_after(values) * cols[:, 1:2])
        )

    @pl.when(step == 0)
    def _():
        join(w_in_out, w_parts, places)
        for j in range(nb):
            gathered[j] = grads[j][...]
            at = pl.ds(pl.multiple_of(order[j] * count, 8), count)
            query_grad[at, :] = mm_t(grads[j][...], w_in_out[3 * width :, :])
        query = short(proj[:, :width], taps[0, 0:1, :], taps[0, 3:4, :], taps[0, 6:7, :])
        mix_grad = query_grad[...]
        long_grad = mix_grad * query
        query_grad[...] = mix_grad * long[...]
        x_hi[pack_len:, :] = jnp.zeros((x_hi.shape[0] - pack_len, wide), jnp.bfloat16)
        x_lo[pack_len:, :] = jnp.zeros((x_hi.shape[0] - pack_len, wide), jnp.bfloat16)
        for g in range(SEGS):
            upper, lower = split(long_grad * cols[:, 2 + g : 3 + g])
            x_hi[:pack_len, g * width : (g + 1) * width] = upper
            x_lo[:pack_len, g * width : (g + 1) * width] = lower
        acc[...] = jnp.zeros_like(acc)
        grad_taps[...] = jnp.zeros_like(grad_taps)

    c_re, c_im = cond_hat[0], cond_hat[1]
    inside, weight = freq_weight(pack_len, step, c_re.shape)
    w4 = jnp.concatenate([weight] * SEGS, axis=1)
    b_re = mm3(ch_r[...], cl_r[...], x_hi[...], x_lo[...]) * w4
    b_im = mm3(sh_r[...], sl_r[...], x_hi[...], x_lo[...]) * (-w4)
    v_re, v_im = piece_hat[0], piece_hat[1]

    def over_segments(values):
        total = values[:, :width]
        for g in range(1, SEGS):
            total = total + values[:, g * width : (g + 1) * width]
        return total

    h_re = over_segments(v_re * b_re + v_im * b_im)
    h_im = over_segments(v_re * b_im - v_im * b_re)
    grad_spectrum[0] = jnp.transpose(h_re).astype(jnp.bfloat16)
    grad_spectrum[1] = jnp.transpose(h_im).astype(jnp.bfloat16)
    gain_in = taps[0, 12:13, :] * scale
    gain_out = taps[0, 13:14, :]
    t_re = jnp.tanh(gain_in * c_re)
    t_im = jnp.tanh(gain_in * c_im)
    join(spectrum, s_parts, places)
    f_re = jnp.where(inside, jnp.transpose(spectrum[:width, :]) + gain_out * t_re, 0.0)
    f_im = jnp.where(inside, jnp.transpose(spectrum[width:, :]) + gain_out * t_im, 0.0)
    a_re = h_re * gain_out * (1.0 - t_re * t_re)
    a_im = h_im * gain_out * (1.0 - t_im * t_im)
    grad_taps[12:13, :] += jnp.sum(a_re * c_re + a_im * c_im, axis=0, keepdims=True) * scale
    grad_taps[13:14, :] += jnp.sum(h_re * t_re + h_im * t_im, axis=0, keepdims=True)
    f_re = jnp.concatenate([f_re] * SEGS, axis=1)
    f_im = jnp.concatenate([f_im] * SEGS, axis=1)
    p = jnp.concatenate([f_re * b_re + f_im * b_im, a_re * gain_in], axis=1)
    m = jnp.concatenate([f_im * b_re - f_re * b_im, -(a_im * gain_in)], axis=1)
    p_hi, p_lo = split(p)
    m_hi, m_lo = split(m)
    acc[...] += mm3(ch_c[...], cl_c[...], p_hi, p_lo) + mm3(sh_c[...], sl_c[...], m_hi, m_lo)

    @pl.when(step == pl.num_programs(0) - 1)
    def _():
        prev = cols[:, 0:1]
        nxt = cols[:, 1:2]
        value_grad = acc[:, :width] * cols[:, 2:3]
        for g in range(1, SEGS):
            value_grad = value_grad + acc[:, g * width : (g + 1) * width] * cols[:, 2 + g : 3 + g]

        def column_sum(values):
            return jnp.sum(values, axis=0, keepdims=True)

        def adjoint(values, grad, row, stride):
            w0 = taps[0, row : row + 1, :]
            w1 = taps[0, row + stride : row + stride + 1, :]
            w2 = taps[0, row + 2 * stride : row + 2 * stride + 1, :]
            from_prev = prev * grad
            from_next = nxt * grad
            grad_taps[row : row + 1, :] = column_sum(row_before(values) * from_prev)
            grad_taps[row + stride : row + stride + 1, :] = column_sum(values * grad)
            grad_taps[row + 2 * stride : row + 2 * stride + 1, :] = column_sum(
                row_after(values) * from_next
            )
            return w1 * grad + w0 * row_after(from_prev) + w2 * row_before(from_next)

        key_proj = proj[:, width : 2 * width]
        key_part = short(key_proj, taps[0, 1:2, :], taps[0, 4:5, :], taps[0, 7:8, :])
        key_grad = adjoint(key_part, acc[:, wide:], 9, 1)
        parts = [query_grad[...], key_grad, value_grad]
        for j in range(3):
            full[:, j * width : (j + 1) * width] = adjoint(
                proj[:, j * width : (j + 1) * width], parts[j], j, 3
            )
        for j in range(nb):
            at = pl.ds(pl.multiple_of(order[j] * count, 8), count)
            low = full[at, :].astype(jnp.bfloat16)
            proj_grad[j] = low
            partials[j][...] = mm(low, w_in_out[: 3 * width, :])


def mixer_backward(blocks, w_in_out, taps, cols, kept, spectra, tables, order, places):
    layer = 0
    proj, long, cond_hat, piece_hat = kept
    pack_len = cols.shape[0]
    nb = len(blocks)
    count, model = blocks[0].shape
    width = taps.shape[2]
    size = tables[0].shape[0]
    f32, low = jnp.float32, jnp.bfloat16
    freq = pl.BlockSpec((2, FTILE, width), lambda i: (0, i, 0))
    out = pl.pallas_call(
        partial(mixer_grad_kernel, nb, len(w_in_out)),
        grid=(size // FTILE,),
        in_specs=[SMEM, SMEM]
        + [whole((count, model))] * nb
        + part_specs(w_in_out, spectra)
        + [
            of_layer(layer, taps.shape[1:]),
            whole(cols.shape),
            whole(proj.shape),
            whole(long.shape),
            freq,
            pl.BlockSpec((2, FTILE, SEGS * width), lambda i: (0, i, 0)),
        ]
        + table_specs(size, pack_len),
        out_specs=[whole((count, model))] * nb
        + [
            whole((nb, count, model)),
            whole((nb, count, 3 * width)),
            pl.BlockSpec((2, width, FTILE), lambda i: (0, 0, i)),
            whole(taps.shape[1:]),
        ],
        out_shape=[jax.ShapeDtypeStruct((count, model), f32)] * nb
        + [
            jax.ShapeDtypeStruct((nb, count, model), low),
            jax.ShapeDtypeStruct((nb, count, 3 * width), low),
            jax.ShapeDtypeStruct((2, width, size), low),
            jax.ShapeDtypeStruct(taps.shape[1:], f32),
        ],
        scratch_shapes=[
            pltpu.VMEM((size, SEGS * width), low),
            pltpu.VMEM((size, SEGS * width), low),
            pltpu.VMEM((pack_len, (SEGS + 1) * width), f32),
            pltpu.VMEM((pack_len, width), f32),
            pltpu.VMEM((pack_len, 3 * width), f32),
        ]
        + part_scratch(w_in_out, spectra),
        compiler_params=pltpu.CompilerParams(vmem_limit_bytes=VMEM_LIMIT),
        cost_estimate=pl.CostEstimate(flops=int(30 * PEAK), bytes_accessed=0, transcendentals=0),
        name="mixer_backward",
    )(
        order, places, *blocks, *w_in_out, *spectra, taps, cols, proj, long, cond_hat, piece_hat,
        *tables, *tables,
    )
    rows, proj_grad, grad_spectrum, grad_taps = out[nb:]
    return (
        out[:nb],
        rows.reshape(pack_len, model),
        proj_grad.reshape(pack_len, 3 * width),
        grad_spectrum.reshape(2 * width, size),
        grad_taps,
    )


def glu_kernel(nb, np_, places, *refs):
    rows = refs[:nb]
    gu_parts, down_parts = refs[nb : nb + np_], refs[nb + np_ : nb + 2 * np_]
    refs = refs[nb + 2 * np_ :]
    parts = refs[:nb]
    gathered, gate, up, act, total, gate_up, down_w = refs[nb:]
    step = pl.program_id(0)
    count, model = rows[0].shape
    tile = gate.shape[1]
    join(gate_up, gu_parts, places)

    @pl.when(step == 0)
    def _():
        join(down_w, down_parts, places)
        for j in range(nb):
            gathered[j * count : (j + 1) * count, :] = rows[j][...]

    gates = mm(gathered[...], gate_up[:model, :])
    ups = mm(gathered[...], gate_up[model:, :])
    gate[...] = gates
    up[...] = ups
    low = (gates * jax.nn.sigmoid(gates) * ups).astype(jnp.bfloat16)
    act[...] = low
    grown = mm(low, down_w[pl.ds(pl.multiple_of(step * tile, tile), tile), :])

    @pl.when(step == 0)
    def _():
        total[...] = grown

    @pl.when(step > 0)
    def _():
        total[...] += grown

    @pl.when(step == pl.num_programs(0) - 1)
    def _():
        for j in range(nb):
            parts[j][...] = total[j * count : (j + 1) * count, :]


def glu_specs(gate_up, down, tile):
    return [pl.BlockSpec((p.shape[0], tile), lambda i: (0, i)) for p in gate_up] + [
        whole(p.shape) for p in down
    ]


def glu_scratch(gate_up, down, tile):
    peers = len(down)
    return [
        pltpu.VMEM((peers * gate_up[0].shape[0], tile), jnp.bfloat16),
        pltpu.VMEM((peers * down[0].shape[0], down[0].shape[1]), jnp.bfloat16),
    ]


def glu_forward(blocks, gate_up, down, places):
    nb = len(blocks)
    count, model = blocks[0].shape
    hidden = len(down) * down[0].shape[0]
    tile = min(HTILE, hidden)
    length = nb * count
    f32, low = jnp.float32, jnp.bfloat16
    column = pl.BlockSpec((length, tile), lambda i: (0, i))
    out = pl.pallas_call(
        partial(glu_kernel, nb, len(down)),
        grid=(hidden // tile,),
        in_specs=[SMEM] + [whole((count, model))] * nb + glu_specs(gate_up, down, tile),
        out_specs=[whole((count, model))] * nb + [whole((length, model))] + [column] * 3,
        out_shape=[jax.ShapeDtypeStruct((count, model), f32)] * nb
        + [
            jax.ShapeDtypeStruct((length, model), low),
            jax.ShapeDtypeStruct((length, hidden), f32),
            jax.ShapeDtypeStruct((length, hidden), f32),
            jax.ShapeDtypeStruct((length, hidden), low),
        ],
        scratch_shapes=[pltpu.VMEM((length, model), f32)] + glu_scratch(gate_up, down, tile),
        compiler_params=pltpu.CompilerParams(vmem_limit_bytes=VMEM_LIMIT),
        cost_estimate=pl.CostEstimate(flops=int(9 * PEAK), bytes_accessed=0, transcendentals=0),
        name="glu_forward",
    )(places, *blocks, *gate_up, *down)
    return out[:nb], out[nb:]


def glu_grad_kernel(nb, np_, places, *refs):
    rows = refs[:nb]
    gate, up = refs[nb : nb + 2]
    gu_parts, down_parts = refs[nb + 2 : nb + 2 + np_], refs[nb + 2 + np_ : nb + 2 + 2 * np_]
    refs = refs[nb + 2 + 2 * np_ :]
    parts = refs[:nb]
    gathered, gate_grad, up_grad, total, gate_up, down_w = refs[nb:]
    step = pl.program_id(0)
    count, model = rows[0].shape
    tile = gate.shape[1]
    join(gate_up, gu_parts, places)

    @pl.when(step == 0)
    def _():
        join(down_w, down_parts, places)
        for j in range(nb):
            gathered[j * count : (j + 1) * count, :] = rows[j][...]

    act_grad = mm_t(gathered[...], down_w[pl.ds(pl.multiple_of(step * tile, tile), tile), :])
    gates = gate[...]
    s = jax.nn.sigmoid(gates)
    low_gate = (act_grad * up[...] * (s * (1.0 + gates * (1.0 - s)))).astype(jnp.bfloat16)
    low_up = (act_grad * (gates * s)).astype(jnp.bfloat16)
    gate_grad[...] = low_gate
    up_grad[...] = low_up
    grown = mm_t(low_gate, gate_up[:model, :]) + mm_t(low_up, gate_up[model:, :])

    @pl.when(step == 0)
    def _():
        total[...] = grown

    @pl.when(step > 0)
    def _():
        total[...] += grown

    @pl.when(step == pl.num_programs(0) - 1)
    def _():
        for j in range(nb):
            parts[j][...] = total[j * count : (j + 1) * count, :]


def glu_backward(blocks, gate, up, gate_up, down, places):
    nb = len(blocks)
    count, model = blocks[0].shape
    hidden = len(down) * down[0].shape[0]
    tile = min(HTILE, hidden)
    length = nb * count
    f32, low = jnp.float32, jnp.bfloat16
    column = pl.BlockSpec((length, tile), lambda i: (0, i))
    out = pl.pallas_call(
        partial(glu_grad_kernel, nb, len(down)),
        grid=(hidden // tile,),
        in_specs=[SMEM] + [whole((count, model))] * nb + [column] * 2 + glu_specs(gate_up, down, tile),
        out_specs=[whole((count, model))] * nb + [whole((length, model))] + [column] * 2,
        out_shape=[jax.ShapeDtypeStruct((count, model), f32)] * nb
        + [
            jax.ShapeDtypeStruct((length, model), low),
            jax.ShapeDtypeStruct((length, hidden), low),
            jax.ShapeDtypeStruct((length, hidden), low),
        ],
        scratch_shapes=[pltpu.VMEM((length, model), f32)] + glu_scratch(gate_up, down, tile),
        compiler_params=pltpu.CompilerParams(vmem_limit_bytes=VMEM_LIMIT),
        cost_estimate=pl.CostEstimate(flops=int(9.5 * PEAK), bytes_accessed=0, transcendentals=0),
        name="glu_backward",
    )(places, *blocks, gate, up, *gate_up, *down)
    return out[:nb], out[nb:]


def dot32(spec, a, b):
    return jnp.einsum(spec, a, b, preferred_element_type=jnp.float32)


def low(values):
    return values.astype(jnp.bfloat16)


def add(old, new):
    return new if old is None else old + new


def exchange_dq(grad):
    peers = lax.axis_size("dq")
    dq = lax.axis_index("dq")
    parts = low(grad).reshape(peers, grad.shape[0] // peers, grad.shape[1])
    moved = [shift(parts[(dq + k) % peers], "dq", k) for k in range(1, peers)]
    return parts[dq], moved


def total_dq(own, moved):
    total = own.astype(jnp.float32)
    for term in moved:
        total = total + term.astype(jnp.float32)
    return total


def to_section(total, target):
    source = 1 - target
    return permute(low(total), ("section",), lambda s: (target,) if s == source else None)


def own_part(own):
    count = own.shape[0] // lax.axis_size("dq")
    return lax.dynamic_slice_in_dim(own, lax.axis_index("dq") * count, count, 0)


def join_parts(part):
    return [part] + [shift(part, "dq", k) for k in range(1, lax.axis_size("dq"))]


def to_holder(total):
    return permute(low(total), ("core", "th"), lambda c, h: (c, 1 - h) if c != h else None)


def quarters(total, other):
    core, high_part = lax.axis_index("core"), lax.axis_index("th")
    total = low(total + other.astype(jnp.float32))
    halves = total.reshape(2, total.shape[0] // 2, total.shape[1])
    got = permute(halves[1 - core], ("core", "th"), lambda c, h: (1 - c, h) if c == h else None)
    quarter = jnp.where(core == high_part, halves[core], got)
    peers = lax.axis_size("dq")
    joined = [quarter] + [shift(quarter, "dq", k) for k in range(1, peers)]
    return joined + [swap_core(block) for block in joined]


def quarter_places():
    core, dq, peers = lax.axis_index("core"), lax.axis_index("dq"), lax.axis_size("dq")
    return jnp.stack(
        [
            (dq - k) % peers * 2 + jnp.bitwise_xor(core, c)
            for c in range(2)
            for k in range(peers)
        ]
    ).astype(jnp.int32)


def assemble_kernel(counts, finish, places, *refs):
    taken = 0
    n_out = len(refs) - sum(counts) - len(counts)
    outs = refs[sum(counts) : sum(counts) + n_out]
    joined = refs[sum(counts) + n_out :]
    for buffer, nb in zip(joined, counts):
        for j in range(nb):
            block = refs[taken + j]
            rows = block.shape[0]
            at = pl.ds(pl.multiple_of(places[j] * rows, 8), rows)
            buffer[at, :] = block[...].astype(jnp.float32)
        taken += nb
    finish(joined, outs)


def assemble(messages, finish, out_shapes):
    counts = [len(blocks) for blocks in messages]
    vmem = pl.BlockSpec(memory_space=pltpu.VMEM)
    return pl.pallas_call(
        partial(assemble_kernel, counts, finish),
        in_specs=[pl.BlockSpec(memory_space=pltpu.SMEM)] + [vmem] * sum(counts),
        out_specs=[vmem] * len(out_shapes),
        out_shape=[jax.ShapeDtypeStruct(s, jnp.float32) for s in out_shapes],
        scratch_shapes=[
            pltpu.VMEM((len(blocks) * blocks[0].shape[0], blocks[0].shape[1]), jnp.float32)
            for blocks in messages
        ],
        compiler_params=pltpu.CompilerParams(vmem_limit_bytes=VMEM_LIMIT),
        cost_estimate=pl.CostEstimate(flops=int(4 * PEAK), bytes_accessed=0, transcendentals=0),
        name="assemble",
    )(quarter_places(), *[block for blocks in messages for block in blocks])


def pack(arrays):
    if len({a.shape[1] for a in arrays}) == 1:
        return [jnp.concatenate(arrays, axis=0)]
    return list(arrays)


def row_reader(buffers):
    state = [0, 0]

    def take(rows):
        at, offset = state
        if offset + rows > buffers[at].shape[0]:
            at, offset = at + 1, 0
        state[0], state[1] = at, offset + rows
        return buffers[at][offset : offset + rows, :]

    return take


def per_device(
    tokens,
    segment_ids,
    cotangent,
    norm_gain1,
    w_in,
    short_taps,
    cond_taps,
    spectrum,
    spectral_gain,
    w_out,
    norm_gain2,
    w_gate_up,
    w_down,
):
    slots, row_count, width = tokens.shape
    pack_len = segment_ids.shape[1]
    channels = w_in.shape[3]
    hidden_cols = w_gate_up.shape[3]
    place5 = tuple(lax.axis_index(a) for a in ALL_AXES)
    section, dq, core, high_part, along = place5
    packs = slots // 2
    peers = lax.axis_size("tl")
    order = jnp.stack(
        [jnp.bitwise_xor(core, c) * peers + (along - t) % peers for c in range(2) for t in range(peers)]
    ).astype(jnp.int32)

    tables = spectral_tables(pack_len)

    def own_slots(array):
        return lax.dynamic_slice_in_dim(array, section * packs, packs, 0)

    freqs = spectrum.shape[2]
    dqs = lax.axis_size("dq")
    places = jnp.stack([(dq - k) % dqs for k in range(dqs)]).astype(jnp.int32)
    w_in_t = jnp.transpose(w_in[0], (1, 2, 0)).reshape(3 * channels, width)
    spectrum_t = jnp.transpose(spectrum[0], (0, 2, 1)).reshape(2 * channels, freqs)
    io_own = own_part(jnp.concatenate([w_in_t, w_out[0]], axis=0))
    sp_own = own_part(spectrum_t)
    per = 2 * width // dqs
    gu_own = lax.dynamic_slice(
        w_gate_up[0], (dq * per % width, dq * 2 // dqs, 0), (per, 1, hidden_cols)
    ).reshape(per, hidden_cols)
    dn_own = own_part(w_down[0])
    rows_in = after(transposed(own_slots(tokens)), gu_own, dn_own)
    first_wave = (transposed(io_own), transposed(sp_own))
    swapped = permute(segment_ids.astype(jnp.float32), ("core",), lambda c: (1 - c,))
    ids_both = jnp.stack([segment_ids, swapped.astype(jnp.int32)])
    segments = own_slots(ids_both[jnp.bitwise_xor(core, high_part)])
    first = section == 0
    own_taps = jnp.concatenate(
        [
            short_taps[0].reshape(9, channels),
            cond_taps[0],
            spectral_gain[0],
            jnp.zeros((2, channels), jnp.float32),
        ],
        axis=0,
    )
    own_taps = transposed(own_taps)
    own_gains = jnp.concatenate([norm_gain1, norm_gain2], axis=0)

    def both_layers(own):
        other = swap_section(own)
        return jnp.stack([jnp.where(first, own, other), jnp.where(first, other, own)])

    taps = both_layers(own_taps)
    gains = both_layers(own_gains)

    def columns(ids):
        prev, nxt = neighbours(ids)
        masks = [(ids == g).astype(jnp.float32) for g in range(SEGS)]
        return jnp.stack([prev, nxt] + masks + [jnp.zeros_like(prev)] * 2, axis=1)

    cols = [columns(segments[index]) for index in range(packs)]
    line = Line()

    def by_layer(part, other):
        return jnp.where(first, part, other), jnp.where(first, other, part)

    w_io, spectra, gate_up, down = [None, None], [None, None], [None, None], [None, None]
    results = [[], []]
    saved = [[], []]
    late = []
    for index in range(packs):
        state = rows_in[index].astype(jnp.float32)
        for layer in range(2):
            opening = index == 0 and layer == 0
            normed, norm_pull = jax.vjp(layer_norm, state, gains[layer, 0])
            blocks = gather_rows(low(normed))
            if opening:
                line.mark(blocks)
                io_part, sp_part = line.take(first_wave)
                io_other, sp_other = swap_section(io_part), swap_section(sp_part)
                held = after((gu_own, dn_own), io_part, sp_part)
                gu_moved, dn_moved = transposed(held[0]), transposed(held[1])
                sp_both = by_layer(sp_part, sp_other)
                spectra[0] = join_parts(sp_both[0])
                io_both = by_layer(io_part, io_other)
                w_io[0] = join_parts(io_both[0])
                line.mark(io_both[0], sp_both[0])
                gu_part, dn_part = line.take((gu_moved, dn_moved))
                gu_other, dn_other = swap_section(gu_part), swap_section(dn_part)
                blocks = after(blocks, gu_part, dn_part)
            parts, gathered, mix, kept = mixer_forward(
                blocks, w_io[layer], taps[layer : layer + 1], cols[index], spectra[layer], tables,
                order, places,
            )
            if opening:
                gu_both = by_layer(gu_part, after(gu_other, parts))
                parts = after(parts, gu_both[0])
            sums_of = core_sums(parts)
            if opening:
                gate_up[0] = join_parts(gu_both[0])
                dn_both = by_layer(dn_part, after(dn_other, sums_of))
                down[0] = join_parts(dn_both[0])
            if layer == 1:
                cot_blocks = both_cores(after(cot_chip, sums_of))
            hidden = state + chip_sums(sums_of)
            normed_two, norm_pull_two = jax.vjp(layer_norm, hidden, gains[layer, 1])
            blocks = gather_rows(low(normed_two))
            if opening:
                io_part, sp_part = after((io_both[1], sp_both[1]), blocks)
                w_io[1] = join_parts(io_part)
                spectra[1] = join_parts(sp_part)
            parts, (gathered_two, gate, up, act) = glu_forward(
                blocks, gate_up[layer], down[layer], places
            )
            saved[layer].append(
                (norm_pull, gathered, mix, kept, norm_pull_two, gathered_two, gate, up, act)
            )
            if layer == 0:
                sums_of = core_sums(parts)
                if opening:
                    gu_part, dn_part = after((gu_both[1], dn_both[1]), sums_of)
                    gate_up[1] = join_parts(gu_part)
                    down[1] = join_parts(dn_part)
                    cot_in = transposed(own_slots(after(cotangent, sums_of)))
                state = hidden + chip_sums(sums_of)
                results[0].append(state)
                cot_chip = chip_blocks(after(cot_in[index], state))
            else:
                late.append((hidden, parts, cot_blocks))

    def deliver(zero, one):
        keep = transposed(jnp.where(first, zero, one))
        given = permute(
            jnp.where(first, one, zero),
            ("section", "core", "th"),
            lambda s, c, h: (1 - s, h, c),
        )
        return keep, given

    def ordered(keep, given):
        lead = jnp.where(first, keep, given)
        trail = jnp.where(first, given, keep)
        return jnp.concatenate([lead, trail], axis=0).astype(jnp.float32)

    sums = [{}, {}]

    def collect(layer, terms, last):
        for name, term in terms.items():
            total = term if name not in sums[layer] else sums[layer][name] + term
            sums[layer][name] = low(total) if last else total.astype(jnp.float32)

    def glu_terms(layer, kept, sums_of, grad_rows, gate_grad, up_grad, last):
        act, rows_two, grad_rows, gate_grad, up_grad = after(
            (kept[8], kept[5], grad_rows, gate_grad, up_grad), sums_of
        )
        half = width // 2
        terms = {
            "down": dot32("lf,ld->fd", act, grad_rows),
            "gate_a": dot32("ld,lf->df", rows_two[:, :half], gate_grad),
            "gate_b": dot32("ld,lf->df", rows_two[:, half:], gate_grad),
            "up": dot32("ld,lf->df", rows_two, up_grad),
        }
        collect(layer, terms, last)

    def mix_terms(layer, kept, sums_of, mix_rows, proj_grad, spectrum_grad, last):
        mix, mix_rows, proj_grad, rows_one = after((kept[2], mix_rows, proj_grad, kept[1]), sums_of)
        terms = {
            "w_in": dot32("lc,ld->cd", proj_grad, rows_one),
            "w_out": dot32("lc,ld->cd", mix, mix_rows),
            "spectrum": spectrum_grad,
        }
        collect(layer, terms, last)

    contents = (("down", "gate_a"), ("gate_b", "up"), ("w_in", "w_out", "spectrum"))
    own = [{}, {}]
    moved = [{}, {}]
    crossed = [{}, {}]

    def send_dq(layer, *messages):
        for m in messages:
            arrays = pack([sums[layer][name] for name in contents[m]])
            sent = [exchange_dq(a) for a in arrays]
            own[layer][m] = [s[0] for s in sent]
            moved[layer][m] = [s[1] for s in sent]

    def send_section(layer, m, *events):
        terms = after(moved[layer][m], *events)
        own[layer][m] = [total_dq(o, t) for o, t in zip(own[layer][m], terms)]
        crossed[layer][m] = [to_section(o, layer) for o in own[layer][m]]

    small_sum = [None, None]
    gain_sum = [None, None]
    grads_in = [[], []]
    for index in range(packs):
        last = index == packs - 1
        state = cot_in[index].astype(jnp.float32)
        kept = saved[1][index]
        late_hidden, late_parts, cot_blocks = late[index]
        parts, (grad_rows, gate_grad, up_grad) = glu_backward(
            cot_blocks, kept[6], kept[7], gate_up[1], down[1], places
        )
        sums_of = core_sums(parts)
        glu_terms(1, kept, sums_of, grad_rows, gate_grad, up_grad, last)
        if last:
            send_dq(1, 0, 1)
        grad_part, gain_two = kept[4](chip_sums(sums_of))
        hidden_grad = state + grad_part
        blocks = gather_rows(low(hidden_grad))
        late_sums = core_sums(after(late_parts, blocks))
        parts, mix_rows, proj_grad, spectrum_grad, tap_grad = mixer_backward(
            blocks, w_io[1], taps[1:2], cols[index], kept[3], spectra[1], tables, order, places
        )
        sums_of = core_sums(parts)
        mix_terms(1, kept, sums_of, mix_rows, proj_grad, spectrum_grad, last)
        moved_sums = sent_sums(sums_of)
        late_moved = sent_sums(after(late_sums, sums_of))
        if last:
            send_section(1, 0, sums_of)
            send_section(1, 1, sums_of)
            send_dq(1, 2)
            moved_sums = after(moved_sums, own[1][1], own[1][2])
        grad_part, gain_one = kept[0](add_sums(sums_of, moved_sums))
        state = hidden_grad + grad_part
        small_sum[1] = add(small_sum[1], tap_grad)
        gain_sum[1] = add(gain_sum[1], jnp.stack([gain_one, gain_two]))
        grads_in[1].append(state)
        kept = saved[0][index]
        blocks = gather_rows(low(state))
        results[1].append(late_hidden + add_sums(late_sums, after(late_moved, blocks)))
        parts, (grad_rows, gate_grad, up_grad) = glu_backward(
            blocks, kept[6], kept[7], gate_up[0], down[0], places
        )
        sums_of = core_sums(parts)
        glu_terms(0, kept, sums_of, grad_rows, gate_grad, up_grad, last)
        moved_sums = sent_sums(sums_of)
        if last:
            send_dq(0, 0, 1)
            out_sent = deliver(
                low(after(jnp.stack(results[0]), sums_of)), low(after(jnp.stack(results[1]), sums_of))
            )
            moved_sums = after(moved_sums, own[0][1])
            send_section(1, 2, moved_sums)
            moved_sums = after(moved_sums, own[1][2])
        grad_part, gain_two = kept[4](add_sums(sums_of, moved_sums))
        hidden_grad = state + grad_part
        chip = chip_blocks(low(hidden_grad))
        if last:
            send_section(0, 0, hidden_grad)
            chip = after(chip, own[0][0])
        blocks = both_cores(chip)
        if last:
            send_section(0, 1, blocks)
            blocks = after(blocks, own[0][1])
        parts, mix_rows, proj_grad, spectrum_grad, tap_grad = mixer_backward(
            blocks, w_io[0], taps[0:1], cols[index], kept[3], spectra[0], tables, order, places
        )
        sums_of = core_sums(parts)
        mix_terms(0, kept, sums_of, mix_rows, proj_grad, spectrum_grad, last)
        moved_sums = sent_sums(sums_of)
        small_sum[0] = add(small_sum[0], tap_grad)
        if last:
            break
        grad_part, gain_one = kept[0](add_sums(sums_of, moved_sums))
        grads_in[0].append(hidden_grad + grad_part)
        gain_sum[0] = add(gain_sum[0], jnp.stack([gain_one, gain_two]))

    send_dq(0, 2)
    line.mark(own[0][2])
    total = {}
    held = {}

    def send_holder(m):
        terms = line.take((crossed[0][m], crossed[1][m]))
        total[m] = [
            jnp.where(first, o, p) + jnp.where(first, t, u).astype(jnp.float32)
            for o, p, t, u in zip(own[0][m], own[1][m], *terms)
        ]
        line.mark(total[m])
        held[m] = [to_holder(t) for t in total[m]]

    joined = {}

    def send_quarters(m):
        terms = line.take(held[m])
        joined[m] = [quarters(t, o) for t, o in zip(total[m], terms)]
        line.mark([j[0] for j in joined[m]])

    send_holder(0)
    grad_part, gain_one = kept[0](add_sums(sums_of, line.take(moved_sums)))
    state = hidden_grad + grad_part
    grads_in[0].append(state)
    gain_sum[0] = add(gain_sum[0], jnp.stack([gain_one, gain_two]))
    line.mark(state)
    grad_sent = deliver(low(jnp.stack(grads_in[0])), low(jnp.stack(grads_in[1])))
    small = [
        jnp.concatenate(
            [jnp.pad(small_sum[k], ((0, 0), (0, width - channels))), gain_sum[k]], axis=0
        )
        for k in range(2)
    ]
    small_other = swap_section(jnp.where(first, small[1], small[0]))
    send_holder(1)
    send_section(0, 2, line.events)
    line.mark(own[0][2])
    mine = jnp.where(first, small[0], small[1]) + line.take(small_other)
    moved_small = [shift(mine, "dq", k) for k in range(1, lax.axis_size("dq"))]
    line.mark(mine)
    send_quarters(0)
    sum_dq = mine
    for term in line.take(moved_small):
        sum_dq = sum_dq + term
    moved_small = permute(sum_dq, ("th",), lambda h: (1 - h,))
    line.mark(sum_dq)
    layer_out = ordered(*line.take(out_sent))
    line.mark(layer_out)
    send_holder(2)
    mine = sum_dq + line.take(moved_small)
    rows_of = own_taps.shape[0]
    tap_grads = transposed(mine[:rows_of, :channels])
    gain_grads = mine[rows_of:]
    gain_other = swap_core(gain_grads)
    line.mark(mine)
    send_quarters(1)
    gain_grads = gain_grads + line.take(gain_other)
    gain_moved = [shift(gain_grads, "tl", k) for k in range(1, peers)]
    line.mark(gain_grads)
    grad_in = ordered(*line.take(grad_sent))
    line.mark(grad_in)
    send_quarters(2)
    gain_total = gain_grads
    for term in line.take(gain_moved):
        gain_total = gain_total + term

    def finish_wide(buffers, outs):
        take = row_reader(buffers)
        outs[0][...] = take(hidden_cols)
        outs[1][: width // 2, 0, :] = take(width // 2)
        outs[1][width // 2 :, 0, :] = take(width // 2)
        outs[1][:, 1, :] = take(width)

    def finish_rest(buffers, outs):
        take = row_reader(buffers)
        outs[0][...] = take(3 * channels)
        outs[1][...] = take(channels)
        outs[2][...] = take(2 * channels)[:, :freqs]

    grad_down, grad_gate_up = assemble(
        line.take(joined[0] + joined[1]), finish_wide, [(hidden_cols, width), (width, 2, hidden_cols)]
    )
    grad_w_in, grad_w_out, grad_spectrum = assemble(
        after(joined[2], grad_down),
        finish_rest,
        [(3 * channels, width), (channels, width), (2 * channels, freqs)],
    )
    grad_spectrum = grad_spectrum.reshape(2, channels, freqs)
    return (
        layer_out[None],
        grad_in[None],
        gain_total[0:1],
        jnp.transpose(grad_w_in.reshape(3, channels, width), (2, 0, 1))[None],
        tap_grads[:9].reshape(1, 3, 3, channels),
        tap_grads[9:12][None],
        jnp.transpose(grad_spectrum, (0, 2, 1))[None],
        tap_grads[12:14][None],
        grad_w_out[None],
        gain_total[1:2],
        grad_gate_up[None],
        grad_down[None],
    )


def solution(mesh):
    sections, dps, tensors = (mesh.shape[a] for a in ("section", "dp", "tensor"))
    devices = mesh.devices.reshape(sections, dps // 2, 2, 2, tensors // 2)
    fine = Mesh(devices, ALL_AXES)
    dp = ("dq", "core")
    tensor = ("th", "tl")
    return jax.shard_map(
        per_device,
        mesh=fine,
        in_specs=(
            P(dp, tensor, None),
            P(dp, None),
            P(dp, tensor, None),
            P("section", None),
            P("section", None, None, tensor),
            P("section", None, None, tensor),
            P("section", None, tensor),
            P("section", None, None, tensor),
            P("section", None, tensor),
            P("section", tensor, None),
            P("section", None),
            P("section", None, None, tensor),
            P("section", tensor, None),
        ),
        out_specs=(
            P("section", dp, tensor, None),
            P("section", dp, tensor, None),
            P("section", None),
            P("section", None, None, tensor),
            P("section", None, None, tensor),
            P("section", None, tensor),
            P("section", None, None, tensor),
            P("section", None, tensor),
            P("section", tensor, None),
            P("section", None),
            P("section", None, None, tensor),
            P("section", tensor, None),
        ),
        check_vma=False,
    )
```

```python
from functools import partial
import math

import jax
import jax.numpy as jnp
import numpy as np
from jax import lax
from jax.experimental import pallas as pl
from jax.experimental.pallas import tpu as pltpu
from jax.sharding import Mesh
from jax.sharding import PartitionSpec as P

SEGS = 4

FTILE = 256
HTILE = 384
PEAK = 1.0e9
MIB = 1024 * 1024

ALL_AXES = ("section", "dq", "core", "th", "tl")


def permute(values, axes, mapping):
    sizes = [lax.axis_size(a) for a in axes]
    pairs = []
    total = math.prod(sizes)
    for source in range(total):
        place = []
        rest = source
        for size in reversed(sizes):
            place.append(rest % size)
            rest //= size
        place = tuple(reversed(place))
        target = mapping(*place)
        if target is None:
            continue
        flat = 0
        for size, at in zip(sizes, target):
            flat = flat * size + at
        pairs.append((source, flat))
    return lax.ppermute(values, axes if len(axes) > 1 else axes[0], pairs)


def swap_core(values):
    return permute(values, ("core",), lambda c: (1 - c,))


def swap_section(values):
    return permute(values, ("section",), lambda s: (1 - s,))


def shift(values, axis, by):
    size = lax.axis_size(axis)
    return permute(values, (axis,), lambda j: ((j + by) % size,))


def transposed(values):
    return permute(values, ("core", "th"), lambda c, h: (h, c))


def chip_blocks(rows):
    return [rows] + [shift(rows, "tl", k) for k in range(1, lax.axis_size("tl"))]


def both_cores(blocks):
    return blocks + [swap_core(block) for block in blocks]


def gather_rows(rows):
    return both_cores(chip_blocks(rows))


def core_sums(blocks):
    peers = lax.axis_size("tl")
    order = list(range(1, peers)) + [0]
    sums = {k: blocks[k] + swap_core(blocks[peers + k]) for k in order}
    return [sums[k] for k in range(peers)]


def sent_sums(sums):
    return [shift(sums[k], "tl", -k) for k in range(1, len(sums))]


def add_sums(sums, moved):
    total = sums[0]
    for term in moved:
        total = total + term.astype(jnp.float32)
    return total


def chip_sums(sums):
    return add_sums(sums, sent_sums(sums))


def after(values, *events):
    return lax.optimization_barrier((values, events))[0]


def tie(*values):
    return lax.optimization_barrier(values)


class Line:
    def __init__(self):
        self.events = ()

    def take(self, values):
        return after(values, self.events)

    def mark(self, *events):
        self.events = events


def layer_norm(values, gain):
    row_mean = jnp.mean(values, axis=-1, keepdims=True)
    centred = values - row_mean
    variance = jnp.mean(centred * centred, axis=-1, keepdims=True)
    return centred * lax.rsqrt(variance + 1e-05) * gain


def neighbours(segments):
    equal = (segments[1:] == segments[:-1]).astype(jnp.float32)
    blank = jnp.zeros((1,), jnp.float32)
    return (jnp.concatenate([blank, equal]), jnp.concatenate([equal, blank]))


def table_size(pack_len):
    return -(-(pack_len + 1) // FTILE) * FTILE


def split(values):
    upper = values.astype(jnp.bfloat16)
    lower = (values - upper.astype(jnp.float32)).astype(jnp.bfloat16)
    return upper, lower


def mm(a, b):
    return jnp.dot(a, b, preferred_element_type=jnp.float32)


def mm_t(a, b):
    return lax.dot_general(a, b, (((1,), (1,)), ((), ())), preferred_element_type=jnp.float32)


def mm3(upper, lower, b_upper, b_lower):
    return mm(upper, b_upper) + (mm(upper, b_lower) + mm(lower, b_upper))


STEP = 32


def tables_kernel(coarse_cos, coarse_sin, fine_cos, fine_sin, cos_hi, cos_lo, sin_hi, sin_lo):
    def body(p, carry):
        cc = coarse_cos[pl.ds(p, 1), :]
        cs = coarse_sin[pl.ds(p, 1), :]
        rows = pl.ds(pl.multiple_of(p * STEP, STEP), STEP)
        upper, lower = split(cc * fine_cos[...] - cs * fine_sin[...])
        cos_hi[rows, :] = upper
        cos_lo[rows, :] = lower
        upper, lower = split(cs * fine_cos[...] + cc * fine_sin[...])
        sin_hi[rows, :] = upper
        sin_lo[rows, :] = lower
        return carry

    lax.fori_loop(0, cos_hi.shape[0] // STEP, body, 0)


def spectral_tables(pack_len):
    size = table_size(pack_len)
    period = 2 * pack_len
    column = np.arange(size, dtype=np.int64)[None, :]
    coarse = (np.arange(size // STEP, dtype=np.int64)[:, None] * STEP * column) % period
    fine = (np.arange(STEP, dtype=np.int64)[:, None] * column) % period
    to_angle = 2.0 * np.pi / period
    small = [f(x * to_angle).astype(np.float32) for x in (coarse, fine) for f in (np.cos, np.sin)]
    return pl.pallas_call(
        tables_kernel,
        out_shape=[jax.ShapeDtypeStruct((size, size), jnp.bfloat16)] * 4,
        cost_estimate=pl.CostEstimate(flops=int(4 * PEAK), bytes_accessed=0, transcendentals=0),
        name="tables",
    )(*small)


def row_before(values):
    return pltpu.roll(values, 1, 0)


def row_after(values):
    return pltpu.roll(values, values.shape[0] - 1, 0)


def freq_weight(pack_len, step, shape):
    f = lax.broadcasted_iota(jnp.int32, shape, 0) + step * FTILE
    edge = (f == 0) | (f == pack_len)
    weight = jnp.where(edge, 1.0, 2.0) / (2.0 * pack_len)
    return f <= pack_len, jnp.where(f <= pack_len, weight, 0.0)


def join(whole_rows, parts, places):
    for k, part in enumerate(parts):
        count = part.shape[0]
        at = pl.ds(pl.multiple_of(places[k] * count, 8), count)
        whole_rows[at, :] = part[...]


def mixer_kernel(nb, np_, order, places, *refs):
    rows = refs[:nb]
    w_parts, s_parts = refs[nb : nb + np_], refs[nb + np_ : nb + 2 * np_]
    refs = refs[nb + 2 * np_ :]
    (taps, cols, ch_r, cl_r, sh_r, sl_r, ch_c, cl_c, sh_c, sl_c) = refs[:10]
    parts = refs[10 : nb + 10]
    (gathered, mix, proj, long, cond_hat, piece_hat) = refs[nb + 10 : nb + 16]
    x_hi, x_lo, acc, query, w_in_out, spectrum = refs[nb + 16 :]
    step = pl.program_id(0)
    count = rows[0].shape[0]
    pack_len = proj.shape[0]
    width = mix.shape[2]
    scale = 1.0 / math.sqrt(pack_len)

    @pl.when(step == 0)
    def _():
        join(w_in_out, w_parts, places)
        for j in range(nb):
            gathered[j] = rows[j][...]
            at = pl.ds(pl.multiple_of(order[j] * count, 8), count)
            proj[at, :] = mm_t(rows[j][...], w_in_out[: 3 * width, :])
        prev = cols[:, 0:1]
        nxt = cols[:, 1:2]

        def short(values, w0, w1, w2):
            return w0 * (row_before(values) * prev) + w1 * values + w2 * (row_after(values) * nxt)

        def one(k):
            return short(
                proj[:, k * width : (k + 1) * width],
                taps[0, k : k + 1, :],
                taps[0, 3 + k : 4 + k, :],
                taps[0, 6 + k : 7 + k, :],
            )

        query[...] = one(0)
        condition = short(one(1), taps[0, 9:10, :], taps[0, 10:11, :], taps[0, 11:12, :])
        value = one(2)
        x_hi[pack_len:, :] = jnp.zeros((x_hi.shape[0] - pack_len, x_hi.shape[1]), jnp.bfloat16)
        x_lo[pack_len:, :] = jnp.zeros((x_hi.shape[0] - pack_len, x_hi.shape[1]), jnp.bfloat16)
        pieces = [value * cols[:, 2 + g : 3 + g] for g in range(SEGS)] + [condition]
        for g, piece in enumerate(pieces):
            upper, lower = split(piece)
            x_hi[:pack_len, g * width : (g + 1) * width] = upper
            x_lo[:pack_len, g * width : (g + 1) * width] = lower
        acc[...] = jnp.zeros_like(acc)

    wide = SEGS * width
    hat_re = mm3(ch_r[...], cl_r[...], x_hi[...], x_lo[...])
    hat_im = -mm3(sh_r[...], sl_r[...], x_hi[...], x_lo[...])
    v_re, v_im = hat_re[:, :wide], hat_im[:, :wide]
    c_re, c_im = hat_re[:, wide:], hat_im[:, wide:]
    cond_hat[0] = c_re
    cond_hat[1] = c_im
    piece_hat[0] = v_re
    piece_hat[1] = v_im
    gain_in = taps[0, 12:13, :] * scale
    gain_out = taps[0, 13:14, :]
    inside, weight = freq_weight(pack_len, step, c_re.shape)
    join(spectrum, s_parts, places)
    s_re = jnp.transpose(spectrum[:width, :])
    s_im = jnp.transpose(spectrum[width:, :])
    f_re = jnp.where(inside, s_re + gain_out * jnp.tanh(gain_in * c_re), 0.0) * weight
    f_im = jnp.where(inside, s_im + gain_out * jnp.tanh(gain_in * c_im), 0.0) * weight
    f_re = jnp.concatenate([f_re] * SEGS, axis=1)
    f_im = jnp.concatenate([f_im] * SEGS, axis=1)
    p_hi, p_lo = split(v_re * f_re - v_im * f_im)
    m_hi, m_lo = split(-(v_re * f_im + v_im * f_re))
    acc[...] += mm3(ch_c[...], cl_c[...], p_hi, p_lo) + mm3(sh_c[...], sl_c[...], m_hi, m_lo)

    @pl.when(step == pl.num_programs(0) - 1)
    def _():
        total = acc[:, :width] * cols[:, 2:3]
        for g in range(1, SEGS):
            total = total + acc[:, g * width : (g + 1) * width] * cols[:, 2 + g : 3 + g]
        long[...] = total
        query[...] = query[...] * total
        for j in range(nb):
            at = pl.ds(pl.multiple_of(order[j] * count, 8), count)
            mixed = query[at, :].astype(jnp.bfloat16)
            mix[j] = mixed
            parts[j][...] = mm(mixed, w_in_out[3 * width :, :])


def table_specs(size, pack_len):
    row = pl.BlockSpec((FTILE, size), lambda i: (i, 0))
    col = pl.BlockSpec((pack_len, FTILE), lambda i: (0, i))
    return [row] * 4 + [col] * 4


def whole(shape):
    zeros = (0,) * len(shape)
    return pl.BlockSpec(shape, lambda i: zeros)


def of_layer(layer, shape):
    rest = (0,) * len(shape)
    return pl.BlockSpec((1,) + shape, lambda i: (layer,) + rest)


SMEM = pl.BlockSpec(memory_space=pltpu.SMEM)


def part_specs(w_in_out, spectra):
    return [whole(p.shape) for p in w_in_out] + [
        pl.BlockSpec((p.shape[0], FTILE), lambda i: (0, i)) for p in spectra
    ]


def part_scratch(w_in_out, spectra):
    peers = len(w_in_out)
    return [
        pltpu.VMEM((peers * w_in_out[0].shape[0], w_in_out[0].shape[1]), jnp.bfloat16),
        pltpu.VMEM((peers * spectra[0].shape[0], FTILE), jnp.float32),
    ]


def mixer_forward(blocks, w_in_out, taps, cols, spectra, tables, order, places):
    layer = 0
    pack_len = cols.shape[0]
    nb = len(blocks)
    count, model = blocks[0].shape
    width = taps.shape[2]
    size = tables[0].shape[0]
    f32, low = jnp.float32, jnp.bfloat16
    out = pl.pallas_call(
        partial(mixer_kernel, nb, len(w_in_out)),
        grid=(size // FTILE,),
        in_specs=[SMEM, SMEM]
        + [whole((count, model))] * nb
        + part_specs(w_in_out, spectra)
        + [of_layer(layer, taps.shape[1:]), whole(cols.shape)]
        + table_specs(size, pack_len),
        out_specs=[whole((count, model))] * nb
        + [
            whole((nb, count, model)),
            whole((nb, count, width)),
            whole((pack_len, 3 * width)),
            whole((pack_len, width)),
            pl.BlockSpec((2, FTILE, width), lambda i: (0, i, 0)),
            pl.BlockSpec((2, FTILE, SEGS * width), lambda i: (0, i, 0)),
        ],
        out_shape=[jax.ShapeDtypeStruct((count, model), f32)] * nb
        + [
            jax.ShapeDtypeStruct((nb, count, model), low),
            jax.ShapeDtypeStruct((nb, count, width), low),
            jax.ShapeDtypeStruct((pack_len, 3 * width), f32),
            jax.ShapeDtypeStruct((pack_len, width), f32),
            jax.ShapeDtypeStruct((2, size, width), f32),
            jax.ShapeDtypeStruct((2, size, SEGS * width), f32),
        ],
        scratch_shapes=[
            pltpu.VMEM((size, (SEGS + 1) * width), low),
            pltpu.VMEM((size, (SEGS + 1) * width), low),
            pltpu.VMEM((pack_len, SEGS * width), f32),
            pltpu.VMEM((pack_len, width), f32),
        ]
        + part_scratch(w_in_out, spectra),
        compiler_params=pltpu.CompilerParams(vmem_limit_bytes=36 * MIB),
        cost_estimate=pl.CostEstimate(flops=int(26 * PEAK), bytes_accessed=0, transcendentals=0),
        name="mixer_forward",
    )(order, places, *blocks, *w_in_out, *spectra, taps, cols, *tables, *tables)
    return out[:nb], out[nb].reshape(pack_len, model), out[nb + 1].reshape(pack_len, width), out[nb + 2 :]


def mixer_grad_kernel(nb, np_, order, places, *refs):
    grads = refs[:nb]
    w_parts, s_parts = refs[nb : nb + np_], refs[nb + np_ : nb + 2 * np_]
    refs = refs[nb + 2 * np_ :]
    (taps, cols, proj, long, cond_hat, piece_hat) = refs[:6]
    (ch_r, cl_r, sh_r, sl_r, ch_c, cl_c, sh_c, sl_c) = refs[6:14]
    partials = refs[14 : nb + 14]
    gathered, proj_grad, grad_spectrum, grad_taps = refs[nb + 14 : nb + 18]
    x_hi, x_lo, acc, query_grad, full, w_in_out, spectrum = refs[nb + 18 :]
    step = pl.program_id(0)
    count = grads[0].shape[0]
    pack_len = proj.shape[0]
    width = long.shape[1]
    wide = SEGS * width
    scale = 1.0 / math.sqrt(pack_len)

    def short(values, w0, w1, w2):
        return (
            w0 * (row_before(values) * cols[:, 0:1])
            + w1 * values
            + w2 * (row_after(values) * cols[:, 1:2])
        )

    @pl.when(step == 0)
    def _():
        join(w_in_out, w_parts, places)
        for j in range(nb):
            gathered[j] = grads[j][...]
            at = pl.ds(pl.multiple_of(order[j] * count, 8), count)
            query_grad[at, :] = mm_t(grads[j][...], w_in_out[3 * width :, :])
        query = short(proj[:, :width], taps[0, 0:1, :], taps[0, 3:4, :], taps[0, 6:7, :])
        mix_grad = query_grad[...]
        long_grad = mix_grad * query
        query_grad[...] = mix_grad * long[...]
        x_hi[pack_len:, :] = jnp.zeros((x_hi.shape[0] - pack_len, wide), jnp.bfloat16)
        x_lo[pack_len:, :] = jnp.zeros((x_hi.shape[0] - pack_len, wide), jnp.bfloat16)
        for g in range(SEGS):
            upper, lower = split(long_grad * cols[:, 2 + g : 3 + g])
            x_hi[:pack_len, g * width : (g + 1) * width] = upper
            x_lo[:pack_len, g * width : (g + 1) * width] = lower
        acc[...] = jnp.zeros_like(acc)
        grad_taps[...] = jnp.zeros_like(grad_taps)

    c_re, c_im = cond_hat[0], cond_hat[1]
    inside, weight = freq_weight(pack_len, step, c_re.shape)
    w4 = jnp.concatenate([weight] * SEGS, axis=1)
    b_re = mm3(ch_r[...], cl_r[...], x_hi[...], x_lo[...]) * w4
    b_im = mm3(sh_r[...], sl_r[...], x_hi[...], x_lo[...]) * (-w4)
    v_re, v_im = piece_hat[0], piece_hat[1]

    def over_segments(values):
        total = values[:, :width]
        for g in range(1, SEGS):
            total = total + values[:, g * width : (g + 1) * width]
        return total

    h_re = over_segments(v_re * b_re + v_im * b_im)
    h_im = over_segments(v_re * b_im - v_im * b_re)
    grad_spectrum[0] = jnp.transpose(h_re).astype(jnp.bfloat16)
    grad_spectrum[1] = jnp.transpose(h_im).astype(jnp.bfloat16)
    gain_in = taps[0, 12:13, :] * scale
    gain_out = taps[0, 13:14, :]
    t_re = jnp.tanh(gain_in * c_re)
    t_im = jnp.tanh(gain_in * c_im)
    join(spectrum, s_parts, places)
    f_re = jnp.where(inside, jnp.transpose(spectrum[:width, :]) + gain_out * t_re, 0.0)
    f_im = jnp.where(inside, jnp.transpose(spectrum[width:, :]) + gain_out * t_im, 0.0)
    a_re = h_re * gain_out * (1.0 - t_re * t_re)
    a_im = h_im * gain_out * (1.0 - t_im * t_im)
    grad_taps[12:13, :] += jnp.sum(a_re * c_re + a_im * c_im, axis=0, keepdims=True) * scale
    grad_taps[13:14, :] += jnp.sum(h_re * t_re + h_im * t_im, axis=0, keepdims=True)
    f_re = jnp.concatenate([f_re] * SEGS, axis=1)
    f_im = jnp.concatenate([f_im] * SEGS, axis=1)
    p = jnp.concatenate([f_re * b_re + f_im * b_im, a_re * gain_in], axis=1)
    m = jnp.concatenate([f_im * b_re - f_re * b_im, -(a_im * gain_in)], axis=1)
    p_hi, p_lo = split(p)
    m_hi, m_lo = split(m)
    acc[...] += mm3(ch_c[...], cl_c[...], p_hi, p_lo) + mm3(sh_c[...], sl_c[...], m_hi, m_lo)

    @pl.when(step == pl.num_programs(0) - 1)
    def _():
        prev = cols[:, 0:1]
        nxt = cols[:, 1:2]
        value_grad = acc[:, :width] * cols[:, 2:3]
        for g in range(1, SEGS):
            value_grad = value_grad + acc[:, g * width : (g + 1) * width] * cols[:, 2 + g : 3 + g]

        def column_sum(values):
            return jnp.sum(values, axis=0, keepdims=True)

        def adjoint(values, grad, row, stride):
            w0 = taps[0, row : row + 1, :]
            w1 = taps[0, row + stride : row + stride + 1, :]
            w2 = taps[0, row + 2 * stride : row + 2 * stride + 1, :]
            from_prev = prev * grad
            from_next = nxt * grad
            grad_taps[row : row + 1, :] = column_sum(row_before(values) * from_prev)
            grad_taps[row + stride : row + stride + 1, :] = column_sum(values * grad)
            grad_taps[row + 2 * stride : row + 2 * stride + 1, :] = column_sum(
                row_after(values) * from_next
            )
            return w1 * grad + w0 * row_after(from_prev) + w2 * row_before(from_next)

        key_proj = proj[:, width : 2 * width]
        key_part = short(key_proj, taps[0, 1:2, :], taps[0, 4:5, :], taps[0, 7:8, :])
        key_grad = adjoint(key_part, acc[:, wide:], 9, 1)
        parts = [query_grad[...], key_grad, value_grad]
        for j in range(3):
            full[:, j * width : (j + 1) * width] = adjoint(
                proj[:, j * width : (j + 1) * width], parts[j], j, 3
            )
        for j in range(nb):
            at = pl.ds(pl.multiple_of(order[j] * count, 8), count)
            low = full[at, :].astype(jnp.bfloat16)
            proj_grad[j] = low
            partials[j][...] = mm(low, w_in_out[: 3 * width, :])


def mixer_backward(blocks, w_in_out, taps, cols, kept, spectra, tables, order, places):
    layer = 0
    proj, long, cond_hat, piece_hat = kept
    pack_len = cols.shape[0]
    nb = len(blocks)
    count, model = blocks[0].shape
    width = taps.shape[2]
    size = tables[0].shape[0]
    f32, low = jnp.float32, jnp.bfloat16
    freq = pl.BlockSpec((2, FTILE, width), lambda i: (0, i, 0))
    out = pl.pallas_call(
        partial(mixer_grad_kernel, nb, len(w_in_out)),
        grid=(size // FTILE,),
        in_specs=[SMEM, SMEM]
        + [whole((count, model))] * nb
        + part_specs(w_in_out, spectra)
        + [
            of_layer(layer, taps.shape[1:]),
            whole(cols.shape),
            whole(proj.shape),
            whole(long.shape),
            freq,
            pl.BlockSpec((2, FTILE, SEGS * width), lambda i: (0, i, 0)),
        ]
        + table_specs(size, pack_len),
        out_specs=[whole((count, model))] * nb
        + [
            whole((nb, count, model)),
            whole((nb, count, 3 * width)),
            pl.BlockSpec((2, width, FTILE), lambda i: (0, 0, i)),
            whole(taps.shape[1:]),
        ],
        out_shape=[jax.ShapeDtypeStruct((count, model), f32)] * nb
        + [
            jax.ShapeDtypeStruct((nb, count, model), low),
            jax.ShapeDtypeStruct((nb, count, 3 * width), low),
            jax.ShapeDtypeStruct((2, width, size), low),
            jax.ShapeDtypeStruct(taps.shape[1:], f32),
        ],
        scratch_shapes=[
            pltpu.VMEM((size, SEGS * width), low),
            pltpu.VMEM((size, SEGS * width), low),
            pltpu.VMEM((pack_len, (SEGS + 1) * width), f32),
            pltpu.VMEM((pack_len, width), f32),
            pltpu.VMEM((pack_len, 3 * width), f32),
        ]
        + part_scratch(w_in_out, spectra),
        compiler_params=pltpu.CompilerParams(vmem_limit_bytes=37 * MIB),
        cost_estimate=pl.CostEstimate(flops=int(30 * PEAK), bytes_accessed=0, transcendentals=0),
        name="mixer_backward",
    )(
        order, places, *blocks, *w_in_out, *spectra, taps, cols, proj, long, cond_hat, piece_hat,
        *tables, *tables,
    )
    rows, proj_grad, grad_spectrum, grad_taps = out[nb:]
    return (
        out[:nb],
        rows.reshape(pack_len, model),
        proj_grad.reshape(pack_len, 3 * width),
        grad_spectrum.reshape(2 * width, size),
        grad_taps,
    )


def glu_kernel(nb, np_, places, *refs):
    rows = refs[:nb]
    gu_parts, down_parts = refs[nb : nb + np_], refs[nb + np_ : nb + 2 * np_]
    refs = refs[nb + 2 * np_ :]
    parts = refs[:nb]
    gathered, gate, up, act, total, gate_up, down_w = refs[nb:]
    step = pl.program_id(0)
    count, model = rows[0].shape
    tile = gate.shape[1]
    join(gate_up, gu_parts, places)

    @pl.when(step == 0)
    def _():
        join(down_w, down_parts, places)
        for j in range(nb):
            gathered[j * count : (j + 1) * count, :] = rows[j][...]

    gates = mm(gathered[...], gate_up[:model, :])
    ups = mm(gathered[...], gate_up[model:, :])
    gate[...] = gates
    up[...] = ups
    low = (gates * jax.nn.sigmoid(gates) * ups).astype(jnp.bfloat16)
    act[...] = low
    grown = mm(low, down_w[pl.ds(pl.multiple_of(step * tile, tile), tile), :])

    @pl.when(step == 0)
    def _():
        total[...] = grown

    @pl.when(step > 0)
    def _():
        total[...] += grown

    @pl.when(step == pl.num_programs(0) - 1)
    def _():
        for j in range(nb):
            parts[j][...] = total[j * count : (j + 1) * count, :]


def glu_specs(gate_up, down, tile):
    return [pl.BlockSpec((p.shape[0], tile), lambda i: (0, i)) for p in gate_up] + [
        whole(p.shape) for p in down
    ]


def glu_scratch(gate_up, down, tile):
    peers = len(down)
    return [
        pltpu.VMEM((peers * gate_up[0].shape[0], tile), jnp.bfloat16),
        pltpu.VMEM((peers * down[0].shape[0], down[0].shape[1]), jnp.bfloat16),
    ]


def glu_forward(blocks, gate_up, down, places):
    nb = len(blocks)
    count, model = blocks[0].shape
    hidden = len(down) * down[0].shape[0]
    tile = min(HTILE, hidden)
    length = nb * count
    f32, low = jnp.float32, jnp.bfloat16
    column = pl.BlockSpec((length, tile), lambda i: (0, i))
    out = pl.pallas_call(
        partial(glu_kernel, nb, len(down)),
        grid=(hidden // tile,),
        in_specs=[SMEM] + [whole((count, model))] * nb + glu_specs(gate_up, down, tile),
        out_specs=[whole((count, model))] * nb + [whole((length, model))] + [column] * 3,
        out_shape=[jax.ShapeDtypeStruct((count, model), f32)] * nb
        + [
            jax.ShapeDtypeStruct((length, model), low),
            jax.ShapeDtypeStruct((length, hidden), f32),
            jax.ShapeDtypeStruct((length, hidden), f32),
            jax.ShapeDtypeStruct((length, hidden), low),
        ],
        scratch_shapes=[pltpu.VMEM((length, model), f32)] + glu_scratch(gate_up, down, tile),
        compiler_params=pltpu.CompilerParams(vmem_limit_bytes=28 * MIB),
        cost_estimate=pl.CostEstimate(flops=int(9 * PEAK), bytes_accessed=0, transcendentals=0),
        name="glu_forward",
    )(places, *blocks, *gate_up, *down)
    return out[:nb], out[nb:]


def glu_grad_kernel(nb, np_, places, *refs):
    rows = refs[:nb]
    gate, up = refs[nb : nb + 2]
    gu_parts, down_parts = refs[nb + 2 : nb + 2 + np_], refs[nb + 2 + np_ : nb + 2 + 2 * np_]
    refs = refs[nb + 2 + 2 * np_ :]
    parts = refs[:nb]
    gathered, gate_grad, up_grad, total, gate_up, down_w = refs[nb:]
    step = pl.program_id(0)
    count, model = rows[0].shape
    tile = gate.shape[1]
    join(gate_up, gu_parts, places)

    @pl.when(step == 0)
    def _():
        join(down_w, down_parts, places)
        for j in range(nb):
            gathered[j * count : (j + 1) * count, :] = rows[j][...]

    act_grad = mm_t(gathered[...], down_w[pl.ds(pl.multiple_of(step * tile, tile), tile), :])
    gates = gate[...]
    s = jax.nn.sigmoid(gates)
    low_gate = (act_grad * up[...] * (s * (1.0 + gates * (1.0 - s)))).astype(jnp.bfloat16)
    low_up = (act_grad * (gates * s)).astype(jnp.bfloat16)
    gate_grad[...] = low_gate
    up_grad[...] = low_up
    grown = mm_t(low_gate, gate_up[:model, :]) + mm_t(low_up, gate_up[model:, :])

    @pl.when(step == 0)
    def _():
        total[...] = grown

    @pl.when(step > 0)
    def _():
        total[...] += grown

    @pl.when(step == pl.num_programs(0) - 1)
    def _():
        for j in range(nb):
            parts[j][...] = total[j * count : (j + 1) * count, :]


def glu_backward(blocks, gate, up, gate_up, down, places):
    nb = len(blocks)
    count, model = blocks[0].shape
    hidden = len(down) * down[0].shape[0]
    tile = min(HTILE, hidden)
    length = nb * count
    f32, low = jnp.float32, jnp.bfloat16
    column = pl.BlockSpec((length, tile), lambda i: (0, i))
    out = pl.pallas_call(
        partial(glu_grad_kernel, nb, len(down)),
        grid=(hidden // tile,),
        in_specs=[SMEM] + [whole((count, model))] * nb + [column] * 2 + glu_specs(gate_up, down, tile),
        out_specs=[whole((count, model))] * nb + [whole((length, model))] + [column] * 2,
        out_shape=[jax.ShapeDtypeStruct((count, model), f32)] * nb
        + [
            jax.ShapeDtypeStruct((length, model), low),
            jax.ShapeDtypeStruct((length, hidden), low),
            jax.ShapeDtypeStruct((length, hidden), low),
        ],
        scratch_shapes=[pltpu.VMEM((length, model), f32)] + glu_scratch(gate_up, down, tile),
        compiler_params=pltpu.CompilerParams(vmem_limit_bytes=28 * MIB),
        cost_estimate=pl.CostEstimate(flops=int(9.5 * PEAK), bytes_accessed=0, transcendentals=0),
        name="glu_backward",
    )(places, *blocks, gate, up, *gate_up, *down)
    return out[:nb], out[nb:]


def dot32(spec, a, b):
    return jnp.einsum(spec, a, b, preferred_element_type=jnp.float32)


def low(values):
    return values.astype(jnp.bfloat16)


def add(old, new):
    return new if old is None else old + new


def exchange_dq(grad):
    peers = lax.axis_size("dq")
    dq = lax.axis_index("dq")
    parts = low(grad).reshape(peers, grad.shape[0] // peers, grad.shape[1])
    moved = [shift(parts[(dq + k) % peers], "dq", k) for k in range(1, peers)]
    return parts[dq], moved


def total_dq(own, moved):
    total = own.astype(jnp.float32)
    for term in moved:
        total = total + term.astype(jnp.float32)
    return total


def to_section(total, target):
    source = 1 - target
    return permute(low(total), ("section",), lambda s: (target,) if s == source else None)


def own_part(own):
    count = own.shape[0] // lax.axis_size("dq")
    return lax.dynamic_slice_in_dim(own, lax.axis_index("dq") * count, count, 0)


def join_parts(part):
    return [part] + [shift(part, "dq", k) for k in range(1, lax.axis_size("dq"))]


def to_holder(total):
    return permute(low(total), ("core", "th"), lambda c, h: (c, 1 - h) if c != h else None)


def holder_total(total, other):
    return low(total + other.astype(jnp.float32))


def from_holder(values):
    return permute(values, ("core", "th"), lambda c, h: (1 - c, h) if c == h else None)


def join_holders(total):
    peers = lax.axis_size("dq")
    held = [total]
    for k in range(1, peers):
        held.append(
            permute(
                total,
                ("dq", "core", "th"),
                lambda d, c, h: ((d + k) % peers, c, h) if c == h else None,
            )
        )
    return held, [from_holder(part) for part in held]


def assemble_kernel(counts, finish, places, *refs):
    taken = 0
    n_in = 2 * sum(counts)
    n_out = len(refs) - n_in - len(counts)
    outs = refs[n_in : n_in + n_out]
    joined = refs[n_in + n_out :]
    holds = places[len(places) - 1] == 1
    for buffer, nb in zip(joined, counts):
        for j in range(nb):
            held, given = refs[taken + j], refs[taken + nb + j]
            rows = held.shape[0]
            at = pl.ds(pl.multiple_of(places[j] * rows, 8), rows)
            buffer[at, :] = jnp.where(
                holds, held[...].astype(jnp.float32), given[...].astype(jnp.float32)
            )
        taken += 2 * nb
    finish(joined, outs)


def assemble(messages, places, finish, out_shapes):
    counts = [len(held) for held, given in messages]
    vmem = pl.BlockSpec(memory_space=pltpu.VMEM)
    holds = (lax.axis_index("core") == lax.axis_index("th")).astype(jnp.int32)
    return pl.pallas_call(
        partial(assemble_kernel, counts, finish),
        in_specs=[SMEM] + [vmem] * (2 * sum(counts)),
        out_specs=[vmem] * len(out_shapes),
        out_shape=[jax.ShapeDtypeStruct(s, jnp.float32) for s in out_shapes],
        scratch_shapes=[
            pltpu.VMEM((len(held) * held[0].shape[0], held[0].shape[1]), jnp.float32)
            for held, given in messages
        ],
        compiler_params=pltpu.CompilerParams(vmem_limit_bytes=40 * MIB),
        cost_estimate=pl.CostEstimate(flops=int(4 * PEAK), bytes_accessed=0, transcendentals=0),
        name="assemble",
    )(jnp.append(places, holds), *[p for held, given in messages for p in held + given])


def pack(arrays):
    if len({a.shape[1] for a in arrays}) == 1:
        return [jnp.concatenate(arrays, axis=0)]
    return list(arrays)


def row_reader(buffers):
    state = [0, 0]

    def take(rows):
        at, offset = state
        if offset + rows > buffers[at].shape[0]:
            at, offset = at + 1, 0
        state[0], state[1] = at, offset + rows
        return buffers[at][offset : offset + rows, :]

    return take


def per_device(
    tokens,
    segment_ids,
    cotangent,
    norm_gain1,
    w_in,
    short_taps,
    cond_taps,
    spectrum,
    spectral_gain,
    w_out,
    norm_gain2,
    w_gate_up,
    w_down,
):
    slots, row_count, width = tokens.shape
    pack_len = segment_ids.shape[1]
    channels = w_in.shape[3]
    hidden_cols = w_gate_up.shape[3]
    place5 = tuple(lax.axis_index(a) for a in ALL_AXES)
    section, dq, core, high_part, along = place5
    packs = slots // 2
    peers = lax.axis_size("tl")
    order = jnp.stack(
        [jnp.bitwise_xor(core, c) * peers + (along - t) % peers for c in range(2) for t in range(peers)]
    ).astype(jnp.int32)

    tables = spectral_tables(pack_len)

    def own_slots(array):
        return lax.dynamic_slice_in_dim(array, section * packs, packs, 0)

    freqs = spectrum.shape[2]
    dqs = lax.axis_size("dq")
    places = jnp.stack([(dq - k) % dqs for k in range(dqs)]).astype(jnp.int32)
    w_in_t = jnp.transpose(w_in[0], (1, 2, 0)).reshape(3 * channels, width)
    spectrum_t = jnp.transpose(spectrum[0], (0, 2, 1)).reshape(2 * channels, freqs)
    io_own = own_part(jnp.concatenate([w_in_t, w_out[0]], axis=0))
    sp_own = own_part(spectrum_t)
    per = 2 * width // dqs
    gu_own = lax.dynamic_slice(
        w_gate_up[0], (dq * per % width, dq * 2 // dqs, 0), (per, 1, hidden_cols)
    ).reshape(per, hidden_cols)
    dn_own = own_part(w_down[0])
    rows_in, io_part, sp_part, gu_own, dn_own = tie(
        transposed(own_slots(tokens)), transposed(io_own), transposed(sp_own), gu_own, dn_own
    )
    swapped = permute(segment_ids.astype(jnp.float32), ("core",), lambda c: (1 - c,))
    ids_both = jnp.stack([segment_ids, swapped.astype(jnp.int32)])
    segments = own_slots(ids_both[jnp.bitwise_xor(core, high_part)])
    first = section == 0
    own_taps = jnp.concatenate(
        [
            short_taps[0].reshape(9, channels),
            cond_taps[0],
            spectral_gain[0],
            jnp.zeros((2, channels), jnp.float32),
        ],
        axis=0,
    )
    own_taps = transposed(own_taps)
    own_gains = jnp.concatenate([norm_gain1, norm_gain2], axis=0)

    def both_layers(own):
        other = swap_section(own)
        return jnp.stack([jnp.where(first, own, other), jnp.where(first, other, own)])

    taps = both_layers(own_taps)
    gains = both_layers(own_gains)

    def columns(ids):
        prev, nxt = neighbours(ids)
        masks = [(ids == g).astype(jnp.float32) for g in range(SEGS)]
        return jnp.stack([prev, nxt] + masks + [jnp.zeros_like(prev)] * 2, axis=1)

    cols = [columns(segments[index]) for index in range(packs)]
    line = Line()

    def by_layer(part, other):
        return jnp.where(first, part, other), jnp.where(first, other, part)

    w_io, spectra, gate_up, down = [None, None], [None, None], [None, None], [None, None]
    results = [[], []]
    saved = [[], []]
    late = []
    for index in range(packs):
        state = rows_in[index].astype(jnp.float32)
        for layer in range(2):
            opening = index == 0 and layer == 0
            normed, norm_pull = jax.vjp(layer_norm, state, gains[layer, 0])
            blocks = gather_rows(low(normed))
            if opening:
                io_other, sp_other = swap_section(io_part), swap_section(sp_part)
                dn_moved = transposed(dn_own)
                gu_moved = transposed(gu_own)
                blocks, io_other, sp_other = tie(blocks, io_other, sp_other)
                sp_both = by_layer(sp_part, sp_other)
                spectra[0] = join_parts(sp_both[0])
                io_both = by_layer(io_part, io_other)
                w_io[0] = join_parts(io_both[0])
                line.mark(io_both[0], sp_both[0])
                dn_part = line.take(dn_moved)
                dn_other = swap_section(dn_part)
                line.mark(dn_part)
                gu_part = line.take(gu_moved)
                dn_both = by_layer(dn_part, after(dn_other, gu_part))
                blocks, gu_part, dn_first, cot_own = tie(blocks, gu_part, dn_both[0], own_slots(cotangent))
                cot_in = transposed(cot_own)
                gu_other = swap_section(gu_part)
                down[0] = join_parts(dn_first)
            parts, gathered, mix, kept = mixer_forward(
                blocks, w_io[layer], taps[layer : layer + 1], cols[index], spectra[layer], tables,
                order, places,
            )
            if opening:
                gu_both = by_layer(gu_part, after(gu_other, parts))
                parts, gu_first, cot_in = tie(parts, gu_both[0], cot_in)
            if layer == 1:
                parts, cot_chip = tie(parts, cot_chip)
            if index == 0 and layer == 1:
                parts, gate_up[1], down[1] = tie(parts, gate_up[1], down[1])
            sums_of = core_sums(parts)
            if opening:
                gate_up[0] = join_parts(gu_first)
            if layer == 1:
                cot_blocks = both_cores(cot_chip)
            hidden = state + chip_sums(sums_of)
            normed_two, norm_pull_two = jax.vjp(layer_norm, hidden, gains[layer, 1])
            blocks = gather_rows(low(normed_two))
            if opening:
                io_part, sp_part = after((io_both[1], sp_both[1]), blocks)
                w_io[1] = join_parts(io_part)
                spectra[1] = join_parts(sp_part)
            parts, (gathered_two, gate, up, act) = glu_forward(
                blocks, gate_up[layer], down[layer], places
            )
            saved[layer].append(
                (norm_pull, gathered, mix, kept, norm_pull_two, gathered_two, gate, up, act)
            )
            if layer == 0:
                sums_of = core_sums(parts)
                if opening:
                    gu_part, dn_part = after((gu_both[1], dn_both[1]), sums_of)
                    gate_up[1] = join_parts(gu_part)
                    down[1] = join_parts(dn_part)
                moved_sums = sent_sums(sums_of)
                state = hidden + add_sums(sums_of, moved_sums)
                results[0].append(state)
                cot_chip = chip_blocks(after(cot_in[index], state))
            else:
                late.append((hidden, parts, cot_blocks))

    def deliver(zero, one):
        keep = transposed(jnp.where(first, zero, one))
        given = permute(
            jnp.where(first, one, zero),
            ("section", "core", "th"),
            lambda s, c, h: (1 - s, h, c),
        )
        return keep, given

    def ordered(keep, given):
        lead = jnp.where(first, keep, given)
        trail = jnp.where(first, given, keep)
        return jnp.concatenate([lead, trail], axis=0).astype(jnp.float32)

    sums = [{}, {}]

    def collect(layer, terms, last):
        for name, term in terms.items():
            total = term if name not in sums[layer] else sums[layer][name] + term
            sums[layer][name] = low(total) if last else total.astype(jnp.float32)

    def glu_terms(layer, kept, sums_of, grad_rows, gate_grad, up_grad, last):
        act, rows_two, grad_rows, gate_grad, up_grad = after(
            (kept[8], kept[5], grad_rows, gate_grad, up_grad), sums_of
        )
        half = width // 2
        terms = {
            "down": dot32("lf,ld->fd", act, grad_rows),
            "gate_a": dot32("ld,lf->df", rows_two[:, :half], gate_grad),
            "gate_b": dot32("ld,lf->df", rows_two[:, half:], gate_grad),
            "up": dot32("ld,lf->df", rows_two, up_grad),
        }
        collect(layer, terms, last)

    def mix_terms(layer, kept, sums_of, mix_rows, proj_grad, spectrum_grad, last):
        mix, mix_rows, proj_grad, rows_one = after((kept[2], mix_rows, proj_grad, kept[1]), sums_of)
        terms = {
            "w_in": dot32("lc,ld->cd", proj_grad, rows_one),
            "w_out": dot32("lc,ld->cd", mix, mix_rows),
            "spectrum": spectrum_grad,
        }
        collect(layer, terms, last)

    contents = (("down", "gate_a"), ("gate_b", "up"), ("w_in", "w_out", "spectrum"))
    own = [{}, {}]
    moved = [{}, {}]
    crossed = [{}, {}]

    def send_dq(layer, m, *events):
            arrays = pack(after([sums[layer][name] for name in contents[m]], *events))
            sent = [exchange_dq(a) for a in arrays]
            own[layer][m] = [s[0] for s in sent]
            moved[layer][m] = [s[1] for s in sent]

    def add_own(layer, m, *events):
        terms = after(moved[layer][m], *events)
        own[layer][m] = [total_dq(o, t) for o, t in zip(own[layer][m], terms)]

    def cross(layer, m):
        crossed[layer][m] = [to_section(o, layer) for o in own[layer][m]]

    total = {}
    held = {}

    def add_total(m, *events):
        terms = after((crossed[0][m], crossed[1][m]), *events)
        total[m] = [
            jnp.where(first, o, p) + jnp.where(first, t, u).astype(jnp.float32)
            for o, p, t, u in zip(own[0][m], own[1][m], *terms)
        ]

    def hold(m):
        held[m] = [to_holder(t) for t in total[m]]

    small_sum = [None, None]
    gain_sum = [None, None]
    grads_in = [[], []]
    for index in range(packs):
        last = index == packs - 1
        state = cot_in[index].astype(jnp.float32)
        kept = saved[1][index]
        late_hidden, late_parts, cot_blocks = late[index]
        parts, (grad_rows, gate_grad, up_grad) = glu_backward(
            cot_blocks, kept[6], kept[7], gate_up[1], down[1], places
        )
        sums_of = core_sums(parts)
        glu_terms(1, kept, sums_of, grad_rows, gate_grad, up_grad, last)
        grad_part, gain_two = kept[4](chip_sums(sums_of))
        hidden_grad = state + grad_part
        if last:
            send_dq(1, 0)
            send_dq(1, 1, hidden_grad)
        blocks = gather_rows(low(hidden_grad))
        late_sums = core_sums(after(late_parts, hidden_grad))
        blocks, late_sums = tie(blocks, late_sums)
        late_moved = sent_sums(late_sums)
        parts, mix_rows, proj_grad, spectrum_grad, tap_grad = mixer_backward(
            blocks, w_io[1], taps[1:2], cols[index], kept[3], spectra[1], tables, order, places
        )
        parts, late_moved = tie(parts, late_moved)
        if last:
            parts, moved[1][0], moved[1][1] = tie(parts, moved[1][0], moved[1][1])
        sums_of = core_sums(parts)
        results[1].append(late_hidden + add_sums(late_sums, after(late_moved, sums_of)))
        moved_sums = sent_sums(sums_of)
        if last:
            add_own(1, 0, sums_of)
            add_own(1, 1, sums_of)
            moved_sums, own[1][0], own[1][1], results[1][-1] = tie(
                moved_sums, own[1][0], own[1][1], results[1][-1]
            )
            cross(1, 0)
            cross(1, 1)
            out_sent = deliver(low(jnp.stack(results[0])), low(jnp.stack(results[1])))
        grad_part, gain_one = kept[0](add_sums(sums_of, moved_sums))
        state = hidden_grad + grad_part
        small_sum[1] = add(small_sum[1], tap_grad)
        gain_sum[1] = add(gain_sum[1], jnp.stack([gain_one, gain_two]))
        grads_in[1].append(state)
        mix_terms(1, kept, state, mix_rows, proj_grad, spectrum_grad, last)
        if last:
            send_dq(1, 2)
        kept = saved[0][index]
        blocks = gather_rows(low(state))
        if last:
            blocks, own[1][2] = tie(blocks, own[1][2])
        parts, (grad_rows, gate_grad, up_grad) = glu_backward(
            blocks, kept[6], kept[7], gate_up[0], down[0], places
        )
        if last:
            parts, out_sent = tie(parts, out_sent)
        sums_of = core_sums(parts)
        glu_terms(0, kept, sums_of, grad_rows, gate_grad, up_grad, last)
        moved_sums = sent_sums(sums_of)
        if last:
            send_dq(0, 0)
            layer_out = ordered(*after(out_sent, sums_of))
            moved_sums, own[0][0], layer_out = tie(moved_sums, own[0][0], layer_out)
        grad_part, gain_two = kept[4](add_sums(sums_of, moved_sums))
        hidden_grad = state + grad_part
        blocks = gather_rows(low(hidden_grad))
        if last:
            send_dq(0, 1, hidden_grad)
            add_own(1, 2, blocks)
            blocks, own[0][1], own[1][2] = tie(blocks, own[0][1], own[1][2])
            cross(1, 2)
        parts, mix_rows, proj_grad, spectrum_grad, tap_grad = mixer_backward(
            blocks, w_io[0], taps[0:1], cols[index], kept[3], spectra[0], tables, order, places
        )
        if last:
            parts, moved[0][0], moved[0][1], crossed[1][2] = tie(
                parts, moved[0][0], moved[0][1], crossed[1][2]
            )
            add_own(0, 0, parts)
            parts, own[0][0] = tie(parts, own[0][0])
            cross(0, 0)
            mix_terms(0, kept, parts, mix_rows, proj_grad, spectrum_grad, last)
            send_dq(0, 2)
            parts, own[0][2] = tie(parts, own[0][2])
        sums_of = core_sums(parts)
        if last:
            add_own(0, 1, sums_of)
        else:
            mix_terms(0, kept, sums_of, mix_rows, proj_grad, spectrum_grad, last)
        moved_sums = sent_sums(sums_of)
        small_sum[0] = add(small_sum[0], tap_grad)
        if last:
            break
        grad_part, gain_one = kept[0](add_sums(sums_of, moved_sums))
        grads_in[0].append(hidden_grad + grad_part)
        gain_sum[0] = add(gain_sum[0], jnp.stack([gain_one, gain_two]))

    line.mark(own[0][1])
    add_total(0, line.events)
    (total[0], own[0][1]) = tie(total[0], own[0][1])
    hold(0)
    cross(0, 1)
    line.mark(total[0])
    joined = {}

    def send_joined(m):
        terms = [holder_total(t, o) for t, o in zip(total[m], line.take(held[m]))]
        line.mark(terms)
        joined[m] = [join_holders(t) for t in terms]

    grad_part, gain_one = kept[0](add_sums(sums_of, line.take(moved_sums)))
    state = hidden_grad + grad_part
    grads_in[0].append(state)
    gain_sum[0] = add(gain_sum[0], jnp.stack([gain_one, gain_two]))
    line.mark(state)
    small = [
        jnp.concatenate(
            [jnp.pad(small_sum[k], ((0, 0), (0, width - channels))), gain_sum[k]], axis=0
        )
        for k in range(2)
    ]
    small_other = swap_section(jnp.where(first, small[1], small[0]))
    add_own(0, 2, line.events)
    cross(0, 2)
    line.mark(own[0][2])
    add_total(1, line.events)
    hold(1)
    line.mark(total[1])
    send_joined(0)
    mine = jnp.where(first, small[0], small[1]) + line.take(small_other)
    moved_small = [shift(mine, "dq", k) for k in range(1, lax.axis_size("dq"))]
    line.mark(mine)
    add_total(2, line.events)
    hold(2)
    line.mark(total[2])
    grad_sent = deliver(
        *line.take((low(jnp.stack(grads_in[0])), low(jnp.stack(grads_in[1]))))
    )
    sum_dq = mine
    for term in line.take(moved_small):
        sum_dq = sum_dq + term
    moved_small = permute(sum_dq, ("th",), lambda h: (1 - h,))
    line.mark(sum_dq)
    mine = sum_dq + line.take(moved_small)
    rows_of = own_taps.shape[0]
    tap_grads = transposed(mine[:rows_of, :channels])
    gain_grads = mine[rows_of:]
    gain_other = swap_core(gain_grads)
    line.mark(mine)
    send_joined(1)
    gain_grads = gain_grads + line.take(gain_other)
    gain_moved = [shift(gain_grads, "tl", k) for k in range(1, peers)]
    line.mark(gain_grads)
    grad_in = ordered(*line.take(grad_sent))
    line.mark(grad_in)
    gain_total = gain_grads
    for term in line.take(gain_moved):
        gain_total = gain_total + term
    line.mark(gain_total)

    def finish_wide(buffers, outs):
        take = row_reader(buffers)
        outs[0][...] = take(hidden_cols)
        outs[1][: width // 2, 0, :] = take(width // 2)
        outs[1][width // 2 :, 0, :] = take(width // 2)
        outs[1][:, 1, :] = take(width)

    def finish_rest(buffers, outs):
        take = row_reader(buffers)
        outs[0][...] = take(3 * channels)
        outs[1][...] = take(channels)
        outs[2][...] = take(2 * channels)[:, :freqs]

    grad_down, grad_gate_up = assemble(
        line.take(joined[0] + joined[1]),
        places,
        finish_wide,
        [(hidden_cols, width), (width, 2, hidden_cols)],
    )
    line.mark(grad_down)
    send_joined(2)
    grad_w_in, grad_w_out, grad_spectrum = assemble(
        joined[2],
        places,
        finish_rest,
        [(3 * channels, width), (channels, width), (2 * channels, freqs)],
    )
    grad_spectrum = grad_spectrum.reshape(2, channels, freqs)
    return (
        layer_out[None],
        grad_in[None],
        gain_total[0:1],
        jnp.transpose(grad_w_in.reshape(3, channels, width), (2, 0, 1))[None],
        tap_grads[:9].reshape(1, 3, 3, channels),
        tap_grads[9:12][None],
        jnp.transpose(grad_spectrum, (0, 2, 1))[None],
        tap_grads[12:14][None],
        grad_w_out[None],
        gain_total[1:2],
        grad_gate_up[None],
        grad_down[None],
    )


def solution(mesh):
    sections, dps, tensors = (mesh.shape[a] for a in ("section", "dp", "tensor"))
    devices = mesh.devices.reshape(sections, dps // 2, 2, 2, tensors // 2)
    fine = Mesh(devices, ALL_AXES)
    dp = ("dq", "core")
    tensor = ("th", "tl")
    return jax.shard_map(
        per_device,
        mesh=fine,
        in_specs=(
            P(dp, tensor, None),
            P(dp, None),
            P(dp, tensor, None),
            P("section", None),
            P("section", None, None, tensor),
            P("section", None, None, tensor),
            P("section", None, tensor),
            P("section", None, None, tensor),
            P("section", None, tensor),
            P("section", tensor, None),
            P("section", None),
            P("section", None, None, tensor),
            P("section", tensor, None),
        ),
        out_specs=(
            P("section", dp, tensor, None),
            P("section", dp, tensor, None),
            P("section", None),
            P("section", None, None, tensor),
            P("section", None, None, tensor),
            P("section", None, tensor),
            P("section", None, None, tensor),
            P("section", None, tensor),
            P("section", tensor, None),
            P("section", None),
            P("section", None, None, tensor),
            P("section", tensor, None),
        ),
        check_vma=False,
    )
```

```python
from functools import partial
import math

import jax
import jax.numpy as jnp
import numpy as np
from jax import lax
from jax.experimental import pallas as pl
from jax.experimental.pallas import tpu as pltpu
from jax.sharding import Mesh
from jax.sharding import PartitionSpec as P

SEGS = 4

FTILE = 256
HTILE = 384
PEAK = 1.0e9
MIB = 1024 * 1024

ALL_AXES = ("section", "dq", "core", "th", "tl")


def permute(values, axes, mapping):
    sizes = [lax.axis_size(a) for a in axes]
    pairs = []
    total = math.prod(sizes)
    for source in range(total):
        place = []
        rest = source
        for size in reversed(sizes):
            place.append(rest % size)
            rest //= size
        place = tuple(reversed(place))
        target = mapping(*place)
        if target is None:
            continue
        flat = 0
        for size, at in zip(sizes, target):
            flat = flat * size + at
        pairs.append((source, flat))
    return lax.ppermute(values, axes if len(axes) > 1 else axes[0], pairs)


def swap_core(values):
    return permute(values, ("core",), lambda c: (1 - c,))


def swap_section(values):
    return permute(values, ("section",), lambda s: (1 - s,))


def shift(values, axis, by):
    size = lax.axis_size(axis)
    return permute(values, (axis,), lambda j: ((j + by) % size,))


def transposed(values):
    return permute(values, ("core", "th"), lambda c, h: (h, c))


def chip_blocks(rows):
    return [rows] + [shift(rows, "tl", k) for k in range(1, lax.axis_size("tl"))]


def both_cores(blocks):
    return blocks + [swap_core(block) for block in blocks]


def gather_rows(rows):
    return both_cores(chip_blocks(rows))


def core_sums(blocks):
    peers = lax.axis_size("tl")
    order = list(range(1, peers)) + [0]
    sums = {k: blocks[k] + swap_core(blocks[peers + k]) for k in order}
    return [sums[k] for k in range(peers)]


def sent_sums(sums):
    return [shift(sums[k], "tl", -k) for k in range(1, len(sums))]


def add_sums(sums, moved):
    total = sums[0]
    for term in moved:
        total = total + term.astype(jnp.float32)
    return total


def chip_sums(sums):
    return add_sums(sums, sent_sums(sums))


def after(values, *events):
    return lax.optimization_barrier((values, events))[0]


def tie(*values):
    return lax.optimization_barrier(values)


class Line:
    def __init__(self):
        self.events = ()

    def take(self, values):
        return after(values, self.events)

    def mark(self, *events):
        self.events = events


def layer_norm(values, gain):
    row_mean = jnp.mean(values, axis=-1, keepdims=True)
    centred = values - row_mean
    variance = jnp.mean(centred * centred, axis=-1, keepdims=True)
    return centred * lax.rsqrt(variance + 1e-05) * gain


def neighbours(segments):
    equal = (segments[1:] == segments[:-1]).astype(jnp.float32)
    blank = jnp.zeros((1,), jnp.float32)
    return (jnp.concatenate([blank, equal]), jnp.concatenate([equal, blank]))


def table_size(pack_len):
    return -(-(pack_len + 1) // FTILE) * FTILE


def split(values):
    upper = values.astype(jnp.bfloat16)
    lower = (values - upper.astype(jnp.float32)).astype(jnp.bfloat16)
    return upper, lower


def mm(a, b):
    return jnp.dot(a, b, preferred_element_type=jnp.float32)


def mm_t(a, b):
    return lax.dot_general(a, b, (((1,), (1,)), ((), ())), preferred_element_type=jnp.float32)


def mm3(upper, lower, b_upper, b_lower):
    return mm(upper, b_upper) + (mm(upper, b_lower) + mm(lower, b_upper))


STEP = 32


def tables_kernel(coarse_cos, coarse_sin, fine_cos, fine_sin, cos_hi, cos_lo, sin_hi, sin_lo):
    def body(p, carry):
        cc = coarse_cos[pl.ds(p, 1), :]
        cs = coarse_sin[pl.ds(p, 1), :]
        rows = pl.ds(pl.multiple_of(p * STEP, STEP), STEP)
        upper, lower = split(cc * fine_cos[...] - cs * fine_sin[...])
        cos_hi[rows, :] = upper
        cos_lo[rows, :] = lower
        upper, lower = split(cs * fine_cos[...] + cc * fine_sin[...])
        sin_hi[rows, :] = upper
        sin_lo[rows, :] = lower
        return carry

    lax.fori_loop(0, cos_hi.shape[0] // STEP, body, 0)


def spectral_tables(pack_len):
    size = table_size(pack_len)
    period = 2 * pack_len
    column = np.arange(size, dtype=np.int64)[None, :]
    coarse = (np.arange(size // STEP, dtype=np.int64)[:, None] * STEP * column) % period
    fine = (np.arange(STEP, dtype=np.int64)[:, None] * column) % period
    to_angle = 2.0 * np.pi / period
    small = [f(x * to_angle).astype(np.float32) for x in (coarse, fine) for f in (np.cos, np.sin)]
    return pl.pallas_call(
        tables_kernel,
        out_shape=[jax.ShapeDtypeStruct((size, size), jnp.bfloat16)] * 4,
        cost_estimate=pl.CostEstimate(flops=int(4 * PEAK), bytes_accessed=0, transcendentals=0),
        compiler_params=pltpu.CompilerParams(vmem_limit_bytes=12 * MIB),
        name="tables",
    )(*small)


def row_before(values):
    return pltpu.roll(values, 1, 0)


def row_after(values):
    return pltpu.roll(values, values.shape[0] - 1, 0)


def freq_weight(pack_len, step, shape):
    f = lax.broadcasted_iota(jnp.int32, shape, 0) + step * FTILE
    edge = (f == 0) | (f == pack_len)
    weight = jnp.where(edge, 1.0, 2.0) / (2.0 * pack_len)
    return f <= pack_len, jnp.where(f <= pack_len, weight, 0.0)


def join(whole_rows, parts, places):
    for k, part in enumerate(parts):
        count = part.shape[0]
        at = pl.ds(pl.multiple_of(places[k] * count, 8), count)
        whole_rows[at, :] = part[...]


def mixer_kernel(nb, np_, order, places, *refs):
    rows = refs[:nb]
    w_parts, s_parts = refs[nb : nb + np_], refs[nb + np_ : nb + 2 * np_]
    refs = refs[nb + 2 * np_ :]
    (taps, cols, ch_r, cl_r, sh_r, sl_r, ch_c, cl_c, sh_c, sl_c) = refs[:10]
    parts = refs[10 : nb + 10]
    (gathered, mix, proj, long, cond_hat, piece_hat) = refs[nb + 10 : nb + 16]
    x_hi, x_lo, acc, query, w_in_out, spectrum = refs[nb + 16 :]
    step = pl.program_id(0)
    count = rows[0].shape[0]
    pack_len = proj.shape[0]
    width = mix.shape[2]
    scale = 1.0 / math.sqrt(pack_len)

    @pl.when(step == 0)
    def _():
        join(w_in_out, w_parts, places)
        for j in range(nb):
            gathered[j] = rows[j][...]
            at = pl.ds(pl.multiple_of(order[j] * count, 8), count)
            proj[at, :] = mm_t(rows[j][...], w_in_out[: 3 * width, :])
        prev = cols[:, 0:1]
        nxt = cols[:, 1:2]

        def short(values, w0, w1, w2):
            return w0 * (row_before(values) * prev) + w1 * values + w2 * (row_after(values) * nxt)

        def one(k):
            return short(
                proj[:, k * width : (k + 1) * width],
                taps[0, k : k + 1, :],
                taps[0, 3 + k : 4 + k, :],
                taps[0, 6 + k : 7 + k, :],
            )

        query[...] = one(0)
        condition = short(one(1), taps[0, 9:10, :], taps[0, 10:11, :], taps[0, 11:12, :])
        value = one(2)
        x_hi[pack_len:, :] = jnp.zeros((x_hi.shape[0] - pack_len, x_hi.shape[1]), jnp.bfloat16)
        x_lo[pack_len:, :] = jnp.zeros((x_hi.shape[0] - pack_len, x_hi.shape[1]), jnp.bfloat16)
        pieces = [value * cols[:, 2 + g : 3 + g] for g in range(SEGS)] + [condition]
        for g, piece in enumerate(pieces):
            upper, lower = split(piece)
            x_hi[:pack_len, g * width : (g + 1) * width] = upper
            x_lo[:pack_len, g * width : (g + 1) * width] = lower
        acc[...] = jnp.zeros_like(acc)

    wide = SEGS * width
    hat_re = mm3(ch_r[...], cl_r[...], x_hi[...], x_lo[...])
    hat_im = -mm3(sh_r[...], sl_r[...], x_hi[...], x_lo[...])
    v_re, v_im = hat_re[:, :wide], hat_im[:, :wide]
    c_re, c_im = hat_re[:, wide:], hat_im[:, wide:]
    cond_hat[0] = c_re
    cond_hat[1] = c_im
    piece_hat[0] = v_re
    piece_hat[1] = v_im
    gain_in = taps[0, 12:13, :] * scale
    gain_out = taps[0, 13:14, :]
    inside, weight = freq_weight(pack_len, step, c_re.shape)
    join(spectrum, s_parts, places)
    s_re = jnp.transpose(spectrum[:width, :])
    s_im = jnp.transpose(spectrum[width:, :])
    f_re = jnp.where(inside, s_re + gain_out * jnp.tanh(gain_in * c_re), 0.0) * weight
    f_im = jnp.where(inside, s_im + gain_out * jnp.tanh(gain_in * c_im), 0.0) * weight
    f_re = jnp.concatenate([f_re] * SEGS, axis=1)
    f_im = jnp.concatenate([f_im] * SEGS, axis=1)
    p_hi, p_lo = split(v_re * f_re - v_im * f_im)
    m_hi, m_lo = split(-(v_re * f_im + v_im * f_re))
    acc[...] += mm3(ch_c[...], cl_c[...], p_hi, p_lo) + mm3(sh_c[...], sl_c[...], m_hi, m_lo)

    @pl.when(step == pl.num_programs(0) - 1)
    def _():
        total = acc[:, :width] * cols[:, 2:3]
        for g in range(1, SEGS):
            total = total + acc[:, g * width : (g + 1) * width] * cols[:, 2 + g : 3 + g]
        long[...] = total
        query[...] = query[...] * total
        for j in range(nb):
            at = pl.ds(pl.multiple_of(order[j] * count, 8), count)
            mixed = query[at, :].astype(jnp.bfloat16)
            mix[j] = mixed
            parts[j][...] = mm(mixed, w_in_out[3 * width :, :])


def table_specs(size, pack_len):
    row = pl.BlockSpec((FTILE, size), lambda i: (i, 0))
    col = pl.BlockSpec((pack_len, FTILE), lambda i: (0, i))
    return [row] * 4 + [col] * 4


def whole(shape):
    zeros = (0,) * len(shape)
    return pl.BlockSpec(shape, lambda i: zeros)


def of_layer(layer, shape):
    rest = (0,) * len(shape)
    return pl.BlockSpec((1,) + shape, lambda i: (layer,) + rest)


SMEM = pl.BlockSpec(memory_space=pltpu.SMEM)


def part_specs(w_in_out, spectra):
    return [whole(p.shape) for p in w_in_out] + [
        pl.BlockSpec((p.shape[0], FTILE), lambda i: (0, i)) for p in spectra
    ]


def part_scratch(w_in_out, spectra):
    peers = len(w_in_out)
    return [
        pltpu.VMEM((peers * w_in_out[0].shape[0], w_in_out[0].shape[1]), jnp.bfloat16),
        pltpu.VMEM((peers * spectra[0].shape[0], FTILE), jnp.float32),
    ]


def mixer_forward(blocks, w_in_out, taps, cols, spectra, tables, order, places):
    layer = 0
    pack_len = cols.shape[0]
    nb = len(blocks)
    count, model = blocks[0].shape
    width = taps.shape[2]
    size = tables[0].shape[0]
    f32, low = jnp.float32, jnp.bfloat16
    out = pl.pallas_call(
        partial(mixer_kernel, nb, len(w_in_out)),
        grid=(size // FTILE,),
        in_specs=[SMEM, SMEM]
        + [whole((count, model))] * nb
        + part_specs(w_in_out, spectra)
        + [of_layer(layer, taps.shape[1:]), whole(cols.shape)]
        + table_specs(size, pack_len),
        out_specs=[whole((count, model))] * nb
        + [
            whole((nb, count, model)),
            whole((nb, count, width)),
            whole((pack_len, 3 * width)),
            whole((pack_len, width)),
            pl.BlockSpec((2, FTILE, width), lambda i: (0, i, 0)),
            pl.BlockSpec((2, FTILE, SEGS * width), lambda i: (0, i, 0)),
        ],
        out_shape=[jax.ShapeDtypeStruct((count, model), f32)] * nb
        + [
            jax.ShapeDtypeStruct((nb, count, model), low),
            jax.ShapeDtypeStruct((nb, count, width), low),
            jax.ShapeDtypeStruct((pack_len, 3 * width), f32),
            jax.ShapeDtypeStruct((pack_len, width), f32),
            jax.ShapeDtypeStruct((2, size, width), f32),
            jax.ShapeDtypeStruct((2, size, SEGS * width), f32),
        ],
        scratch_shapes=[
            pltpu.VMEM((size, (SEGS + 1) * width), low),
            pltpu.VMEM((size, (SEGS + 1) * width), low),
            pltpu.VMEM((pack_len, SEGS * width), f32),
            pltpu.VMEM((pack_len, width), f32),
        ]
        + part_scratch(w_in_out, spectra),
        compiler_params=pltpu.CompilerParams(vmem_limit_bytes=36 * MIB),
        cost_estimate=pl.CostEstimate(flops=int(26 * PEAK), bytes_accessed=0, transcendentals=0),
        name="mixer_forward",
    )(order, places, *blocks, *w_in_out, *spectra, taps, cols, *tables, *tables)
    return out[:nb], out[nb].reshape(pack_len, model), out[nb + 1].reshape(pack_len, width), out[nb + 2 :]


def mixer_grad_kernel(nb, np_, order, places, *refs):
    grads = refs[:nb]
    w_parts, s_parts = refs[nb : nb + np_], refs[nb + np_ : nb + 2 * np_]
    refs = refs[nb + 2 * np_ :]
    (taps, cols, normed, gain, proj, long, cond_hat, piece_hat) = refs[:8]
    (ch_r, cl_r, sh_r, sl_r, ch_c, cl_c, sh_c, sl_c) = refs[8:16]
    partials = refs[16 : nb + 16]
    gathered, proj_grad, grad_spectrum, grad_taps, grad_gain = refs[nb + 16 : nb + 21]
    x_hi, x_lo, acc, query_grad, full, w_in_out, spectrum = refs[nb + 21 :]
    step = pl.program_id(0)
    count = grads[0].shape[0]
    pack_len = proj.shape[0]
    width = long.shape[1]
    wide = SEGS * width
    scale = 1.0 / math.sqrt(pack_len)

    def short(values, w0, w1, w2):
        return (
            w0 * (row_before(values) * cols[:, 0:1])
            + w1 * values
            + w2 * (row_after(values) * cols[:, 1:2])
        )

    @pl.when(step == 0)
    def _():
        join(w_in_out, w_parts, places)
        for j in range(nb):
            gathered[j] = grads[j][...]
            at = pl.ds(pl.multiple_of(order[j] * count, 8), count)
            query_grad[at, :] = mm_t(grads[j][...], w_in_out[3 * width :, :])
        query = short(proj[:, :width], taps[0, 0:1, :], taps[0, 3:4, :], taps[0, 6:7, :])
        mix_grad = query_grad[...]
        long_grad = mix_grad * query
        query_grad[...] = mix_grad * long[...]
        x_hi[pack_len:, :] = jnp.zeros((x_hi.shape[0] - pack_len, wide), jnp.bfloat16)
        x_lo[pack_len:, :] = jnp.zeros((x_hi.shape[0] - pack_len, wide), jnp.bfloat16)
        for g in range(SEGS):
            upper, lower = split(long_grad * cols[:, 2 + g : 3 + g])
            x_hi[:pack_len, g * width : (g + 1) * width] = upper
            x_lo[:pack_len, g * width : (g + 1) * width] = lower
        acc[...] = jnp.zeros_like(acc)
        grad_taps[...] = jnp.zeros_like(grad_taps)

    c_re, c_im = cond_hat[0], cond_hat[1]
    inside, weight = freq_weight(pack_len, step, c_re.shape)
    w4 = jnp.concatenate([weight] * SEGS, axis=1)
    b_re = mm3(ch_r[...], cl_r[...], x_hi[...], x_lo[...]) * w4
    b_im = mm3(sh_r[...], sl_r[...], x_hi[...], x_lo[...]) * (-w4)
    v_re, v_im = piece_hat[0], piece_hat[1]

    def over_segments(values):
        total = values[:, :width]
        for g in range(1, SEGS):
            total = total + values[:, g * width : (g + 1) * width]
        return total

    h_re = over_segments(v_re * b_re + v_im * b_im)
    h_im = over_segments(v_re * b_im - v_im * b_re)
    grad_spectrum[0] = jnp.transpose(h_re).astype(jnp.bfloat16)
    grad_spectrum[1] = jnp.transpose(h_im).astype(jnp.bfloat16)
    gain_in = taps[0, 12:13, :] * scale
    gain_out = taps[0, 13:14, :]
    t_re = jnp.tanh(gain_in * c_re)
    t_im = jnp.tanh(gain_in * c_im)
    join(spectrum, s_parts, places)
    f_re = jnp.where(inside, jnp.transpose(spectrum[:width, :]) + gain_out * t_re, 0.0)
    f_im = jnp.where(inside, jnp.transpose(spectrum[width:, :]) + gain_out * t_im, 0.0)
    a_re = h_re * gain_out * (1.0 - t_re * t_re)
    a_im = h_im * gain_out * (1.0 - t_im * t_im)
    grad_taps[12:13, :] += jnp.sum(a_re * c_re + a_im * c_im, axis=0, keepdims=True) * scale
    grad_taps[13:14, :] += jnp.sum(h_re * t_re + h_im * t_im, axis=0, keepdims=True)
    f_re = jnp.concatenate([f_re] * SEGS, axis=1)
    f_im = jnp.concatenate([f_im] * SEGS, axis=1)
    p = jnp.concatenate([f_re * b_re + f_im * b_im, a_re * gain_in], axis=1)
    m = jnp.concatenate([f_im * b_re - f_re * b_im, -(a_im * gain_in)], axis=1)
    p_hi, p_lo = split(p)
    m_hi, m_lo = split(m)
    acc[...] += mm3(ch_c[...], cl_c[...], p_hi, p_lo) + mm3(sh_c[...], sl_c[...], m_hi, m_lo)

    @pl.when(step == pl.num_programs(0) - 1)
    def _():
        prev = cols[:, 0:1]
        nxt = cols[:, 1:2]
        value_grad = acc[:, :width] * cols[:, 2:3]
        for g in range(1, SEGS):
            value_grad = value_grad + acc[:, g * width : (g + 1) * width] * cols[:, 2 + g : 3 + g]

        def column_sum(values):
            return jnp.sum(values, axis=0, keepdims=True)

        def adjoint(values, grad, row, stride):
            w0 = taps[0, row : row + 1, :]
            w1 = taps[0, row + stride : row + stride + 1, :]
            w2 = taps[0, row + 2 * stride : row + 2 * stride + 1, :]
            from_prev = prev * grad
            from_next = nxt * grad
            grad_taps[row : row + 1, :] = column_sum(row_before(values) * from_prev)
            grad_taps[row + stride : row + stride + 1, :] = column_sum(values * grad)
            grad_taps[row + 2 * stride : row + 2 * stride + 1, :] = column_sum(
                row_after(values) * from_next
            )
            return w1 * grad + w0 * row_after(from_prev) + w2 * row_before(from_next)

        key_proj = proj[:, width : 2 * width]
        key_part = short(key_proj, taps[0, 1:2, :], taps[0, 4:5, :], taps[0, 7:8, :])
        key_grad = adjoint(key_part, acc[:, wide:], 9, 1)
        parts = [query_grad[...], key_grad, value_grad]
        for j in range(3):
            full[:, j * width : (j + 1) * width] = adjoint(
                proj[:, j * width : (j + 1) * width], parts[j], j, 3
            )
        for j in range(nb):
            at = pl.ds(pl.multiple_of(order[j] * count, 8), count)
            low = full[at, :].astype(jnp.bfloat16)
            proj_grad[j] = low
            rows_grad = mm(low, w_in_out[: 3 * width, :])
            partials[j][...] = rows_grad
            seen = normed[j * count : (j + 1) * count, :].astype(jnp.float32)
            term = jnp.sum(rows_grad * seen, axis=0, keepdims=True)
            gain_sum = term if j == 0 else gain_sum + term
        grad_gain[...] = gain_sum / gain[...]


def mixer_backward(blocks, w_in_out, taps, cols, normed, gain, kept, spectra, tables, order, places):
    layer = 0
    proj, long, cond_hat, piece_hat = kept
    pack_len = cols.shape[0]
    nb = len(blocks)
    count, model = blocks[0].shape
    width = taps.shape[2]
    size = tables[0].shape[0]
    f32, low = jnp.float32, jnp.bfloat16
    freq = pl.BlockSpec((2, FTILE, width), lambda i: (0, i, 0))
    out = pl.pallas_call(
        partial(mixer_grad_kernel, nb, len(w_in_out)),
        grid=(size // FTILE,),
        in_specs=[SMEM, SMEM]
        + [whole((count, model))] * nb
        + part_specs(w_in_out, spectra)
        + [
            of_layer(layer, taps.shape[1:]),
            whole(cols.shape),
            whole(normed.shape),
            whole(gain.shape),
            whole(proj.shape),
            whole(long.shape),
            freq,
            pl.BlockSpec((2, FTILE, SEGS * width), lambda i: (0, i, 0)),
        ]
        + table_specs(size, pack_len),
        out_specs=[whole((count, model))] * nb
        + [
            whole((nb, count, model)),
            whole((nb, count, 3 * width)),
            pl.BlockSpec((2, width, FTILE), lambda i: (0, 0, i)),
            whole(taps.shape[1:]),
            whole(gain.shape),
        ],
        out_shape=[jax.ShapeDtypeStruct((count, model), f32)] * nb
        + [
            jax.ShapeDtypeStruct((nb, count, model), low),
            jax.ShapeDtypeStruct((nb, count, 3 * width), low),
            jax.ShapeDtypeStruct((2, width, size), low),
            jax.ShapeDtypeStruct(taps.shape[1:], f32),
            jax.ShapeDtypeStruct(gain.shape, f32),
        ],
        scratch_shapes=[
            pltpu.VMEM((size, SEGS * width), low),
            pltpu.VMEM((size, SEGS * width), low),
            pltpu.VMEM((pack_len, (SEGS + 1) * width), f32),
            pltpu.VMEM((pack_len, width), f32),
            pltpu.VMEM((pack_len, 3 * width), f32),
        ]
        + part_scratch(w_in_out, spectra),
        compiler_params=pltpu.CompilerParams(vmem_limit_bytes=40 * MIB),
        cost_estimate=pl.CostEstimate(flops=int(30 * PEAK), bytes_accessed=0, transcendentals=0),
        name="mixer_backward",
    )(
        order, places, *blocks, *w_in_out, *spectra, taps, cols, normed, gain, proj, long, cond_hat,
        piece_hat,
        *tables, *tables,
    )
    rows, proj_grad, grad_spectrum, grad_taps, grad_gain = out[nb:]
    return (
        out[:nb],
        rows.reshape(pack_len, model),
        proj_grad.reshape(pack_len, 3 * width),
        grad_spectrum.reshape(2 * width, size),
        grad_taps,
        grad_gain,
    )


def glu_kernel(nb, np_, places, *refs):
    rows = refs[:nb]
    gu_parts, down_parts = refs[nb : nb + np_], refs[nb + np_ : nb + 2 * np_]
    refs = refs[nb + 2 * np_ :]
    parts = refs[:nb]
    gathered, gate, up, act, total, gate_up, down_w = refs[nb:]
    step = pl.program_id(0)
    count, model = rows[0].shape
    tile = gate.shape[1]
    join(gate_up, gu_parts, places)

    @pl.when(step == 0)
    def _():
        join(down_w, down_parts, places)
        for j in range(nb):
            gathered[j * count : (j + 1) * count, :] = rows[j][...]

    gates = mm(gathered[...], gate_up[:model, :])
    ups = mm(gathered[...], gate_up[model:, :])
    gate[...] = gates
    up[...] = ups
    low = (gates * jax.nn.sigmoid(gates) * ups).astype(jnp.bfloat16)
    act[...] = low
    grown = mm(low, down_w[pl.ds(pl.multiple_of(step * tile, tile), tile), :])

    @pl.when(step == 0)
    def _():
        total[...] = grown

    @pl.when(step > 0)
    def _():
        total[...] += grown

    @pl.when(step == pl.num_programs(0) - 1)
    def _():
        for j in range(nb):
            parts[j][...] = total[j * count : (j + 1) * count, :]


def glu_specs(gate_up, down, tile):
    return [pl.BlockSpec((p.shape[0], tile), lambda i: (0, i)) for p in gate_up] + [
        whole(p.shape) for p in down
    ]


def glu_scratch(gate_up, down, tile):
    peers = len(down)
    return [
        pltpu.VMEM((peers * gate_up[0].shape[0], tile), jnp.bfloat16),
        pltpu.VMEM((peers * down[0].shape[0], down[0].shape[1]), jnp.bfloat16),
    ]


def glu_forward(blocks, gate_up, down, places):
    nb = len(blocks)
    count, model = blocks[0].shape
    hidden = len(down) * down[0].shape[0]
    tile = min(HTILE, hidden)
    length = nb * count
    f32, low = jnp.float32, jnp.bfloat16
    column = pl.BlockSpec((length, tile), lambda i: (0, i))
    out = pl.pallas_call(
        partial(glu_kernel, nb, len(down)),
        grid=(hidden // tile,),
        in_specs=[SMEM] + [whole((count, model))] * nb + glu_specs(gate_up, down, tile),
        out_specs=[whole((count, model))] * nb + [whole((length, model))] + [column] * 3,
        out_shape=[jax.ShapeDtypeStruct((count, model), f32)] * nb
        + [
            jax.ShapeDtypeStruct((length, model), low),
            jax.ShapeDtypeStruct((length, hidden), f32),
            jax.ShapeDtypeStruct((length, hidden), f32),
            jax.ShapeDtypeStruct((length, hidden), low),
        ],
        scratch_shapes=[pltpu.VMEM((length, model), f32)] + glu_scratch(gate_up, down, tile),
        compiler_params=pltpu.CompilerParams(vmem_limit_bytes=28 * MIB),
        cost_estimate=pl.CostEstimate(flops=int(9 * PEAK), bytes_accessed=0, transcendentals=0),
        name="glu_forward",
    )(places, *blocks, *gate_up, *down)
    return out[:nb], out[nb:]


def glu_grad_kernel(nb, np_, places, *refs):
    rows = refs[:nb]
    gate, up = refs[nb : nb + 2]
    gu_parts, down_parts = refs[nb + 2 : nb + 2 + np_], refs[nb + 2 + np_ : nb + 2 + 2 * np_]
    refs = refs[nb + 2 + 2 * np_ :]
    parts = refs[:nb]
    gathered, gate_grad, up_grad, total, gate_up, down_w = refs[nb:]
    step = pl.program_id(0)
    count, model = rows[0].shape
    tile = gate.shape[1]
    join(gate_up, gu_parts, places)

    @pl.when(step == 0)
    def _():
        join(down_w, down_parts, places)
        for j in range(nb):
            gathered[j * count : (j + 1) * count, :] = rows[j][...]

    act_grad = mm_t(gathered[...], down_w[pl.ds(pl.multiple_of(step * tile, tile), tile), :])
    gates = gate[...]
    s = jax.nn.sigmoid(gates)
    low_gate = (act_grad * up[...] * (s * (1.0 + gates * (1.0 - s)))).astype(jnp.bfloat16)
    low_up = (act_grad * (gates * s)).astype(jnp.bfloat16)
    gate_grad[...] = low_gate
    up_grad[...] = low_up
    grown = mm_t(low_gate, gate_up[:model, :]) + mm_t(low_up, gate_up[model:, :])

    @pl.when(step == 0)
    def _():
        total[...] = grown

    @pl.when(step > 0)
    def _():
        total[...] += grown

    @pl.when(step == pl.num_programs(0) - 1)
    def _():
        for j in range(nb):
            parts[j][...] = total[j * count : (j + 1) * count, :]


def glu_backward(blocks, gate, up, gate_up, down, places):
    nb = len(blocks)
    count, model = blocks[0].shape
    hidden = len(down) * down[0].shape[0]
    tile = min(HTILE, hidden)
    length = nb * count
    f32, low = jnp.float32, jnp.bfloat16
    column = pl.BlockSpec((length, tile), lambda i: (0, i))
    out = pl.pallas_call(
        partial(glu_grad_kernel, nb, len(down)),
        grid=(hidden // tile,),
        in_specs=[SMEM] + [whole((count, model))] * nb + [column] * 2 + glu_specs(gate_up, down, tile),
        out_specs=[whole((count, model))] * nb + [whole((length, model))] + [column] * 2,
        out_shape=[jax.ShapeDtypeStruct((count, model), f32)] * nb
        + [
            jax.ShapeDtypeStruct((length, model), low),
            jax.ShapeDtypeStruct((length, hidden), low),
            jax.ShapeDtypeStruct((length, hidden), low),
        ],
        scratch_shapes=[pltpu.VMEM((length, model), f32)] + glu_scratch(gate_up, down, tile),
        compiler_params=pltpu.CompilerParams(vmem_limit_bytes=28 * MIB),
        cost_estimate=pl.CostEstimate(flops=int(9.5 * PEAK), bytes_accessed=0, transcendentals=0),
        name="glu_backward",
    )(places, *blocks, gate, up, *gate_up, *down)
    return out[:nb], out[nb:]


def dot32(spec, a, b):
    return jnp.einsum(spec, a, b, preferred_element_type=jnp.float32)


def low(values):
    return values.astype(jnp.bfloat16)


def add(old, new):
    return new if old is None else old + new


def exchange_dq(grad):
    peers = lax.axis_size("dq")
    dq = lax.axis_index("dq")
    parts = low(grad).reshape(peers, grad.shape[0] // peers, grad.shape[1])
    moved = [shift(parts[(dq + k) % peers], "dq", k) for k in range(1, peers)]
    return parts[dq], moved


def total_dq(own, moved):
    total = own.astype(jnp.float32)
    for term in moved:
        total = total + term.astype(jnp.float32)
    return total


def to_section(total, target):
    source = 1 - target
    return permute(low(total), ("section",), lambda s: (target,) if s == source else None)


def own_part(own):
    count = own.shape[0] // lax.axis_size("dq")
    return lax.dynamic_slice_in_dim(own, lax.axis_index("dq") * count, count, 0)


def join_parts(part):
    return [part] + [shift(part, "dq", k) for k in range(1, lax.axis_size("dq"))]


def to_holder(total):
    return permute(low(total), ("core", "th"), lambda c, h: (c, 1 - h) if c != h else None)


def holder_total(total, other):
    return low(total + other.astype(jnp.float32))


def from_holder(values):
    return permute(values, ("core", "th"), lambda c, h: (1 - c, h) if c == h else None)


def join_holders(total):
    peers = lax.axis_size("dq")
    held = [total]
    for k in range(1, peers):
        held.append(
            permute(
                total,
                ("dq", "core", "th"),
                lambda d, c, h: ((d + k) % peers, c, h) if c == h else None,
            )
        )
    return held, [from_holder(part) for part in held]


def assemble_kernel(counts, finish, places, *refs):
    taken = 0
    n_in = 2 * sum(counts)
    n_out = len(refs) - n_in - len(counts)
    outs = refs[n_in : n_in + n_out]
    joined = refs[n_in + n_out :]
    holds = places[len(places) - 1] == 1
    for buffer, nb in zip(joined, counts):
        for j in range(nb):
            held, given = refs[taken + j], refs[taken + nb + j]
            rows = held.shape[0]
            at = pl.ds(pl.multiple_of(places[j] * rows, 8), rows)
            buffer[at, :] = jnp.where(
                holds, held[...].astype(jnp.float32), given[...].astype(jnp.float32)
            )
        taken += 2 * nb
    finish(joined, outs)


def assemble(messages, places, finish, out_shapes):
    counts = [len(held) for held, given in messages]
    vmem = pl.BlockSpec(memory_space=pltpu.VMEM)
    holds = (lax.axis_index("core") == lax.axis_index("th")).astype(jnp.int32)
    return pl.pallas_call(
        partial(assemble_kernel, counts, finish),
        in_specs=[SMEM] + [vmem] * (2 * sum(counts)),
        out_specs=[vmem] * len(out_shapes),
        out_shape=[jax.ShapeDtypeStruct(s, jnp.float32) for s in out_shapes],
        scratch_shapes=[
            pltpu.VMEM((len(held) * held[0].shape[0], held[0].shape[1]), jnp.float32)
            for held, given in messages
        ],
        compiler_params=pltpu.CompilerParams(vmem_limit_bytes=40 * MIB),
        cost_estimate=pl.CostEstimate(flops=int(4 * PEAK), bytes_accessed=0, transcendentals=0),
        name="assemble",
    )(jnp.append(places, holds), *[p for held, given in messages for p in held + given])


def pack(arrays):
    if len({a.shape[1] for a in arrays}) == 1:
        return [jnp.concatenate(arrays, axis=0)]
    return list(arrays)


def row_reader(buffers):
    state = [0, 0]

    def take(rows):
        at, offset = state
        if offset + rows > buffers[at].shape[0]:
            at, offset = at + 1, 0
        state[0], state[1] = at, offset + rows
        return buffers[at][offset : offset + rows, :]

    return take


def per_device(
    tokens,
    segment_ids,
    cotangent,
    norm_gain1,
    w_in,
    short_taps,
    cond_taps,
    spectrum,
    spectral_gain,
    w_out,
    norm_gain2,
    w_gate_up,
    w_down,
):
    slots, row_count, width = tokens.shape
    pack_len = segment_ids.shape[1]
    channels = w_in.shape[3]
    hidden_cols = w_gate_up.shape[3]
    place5 = tuple(lax.axis_index(a) for a in ALL_AXES)
    section, dq, core, high_part, along = place5
    packs = slots // 2
    peers = lax.axis_size("tl")
    order = jnp.stack(
        [jnp.bitwise_xor(core, c) * peers + (along - t) % peers for c in range(2) for t in range(peers)]
    ).astype(jnp.int32)

    tables = spectral_tables(pack_len)

    def own_slots(array):
        return lax.dynamic_slice_in_dim(array, section * packs, packs, 0)

    freqs = spectrum.shape[2]
    dqs = lax.axis_size("dq")
    places = jnp.stack([(dq - k) % dqs for k in range(dqs)]).astype(jnp.int32)
    w_in_t = jnp.transpose(w_in[0], (1, 2, 0)).reshape(3 * channels, width)
    spectrum_t = jnp.transpose(spectrum[0], (0, 2, 1)).reshape(2 * channels, freqs)
    io_own = own_part(jnp.concatenate([w_in_t, w_out[0]], axis=0))
    sp_own = own_part(spectrum_t)
    per = 2 * width // dqs
    gu_own = lax.dynamic_slice(
        w_gate_up[0], (dq * per % width, dq * 2 // dqs, 0), (per, 1, hidden_cols)
    ).reshape(per, hidden_cols)
    dn_own = own_part(w_down[0])
    rows_in, io_part, sp_part, gu_own, dn_own = tie(
        transposed(own_slots(tokens)), transposed(io_own), transposed(sp_own), gu_own, dn_own
    )
    swapped = permute(segment_ids.astype(jnp.float32), ("core",), lambda c: (1 - c,))
    ids_both = jnp.stack([segment_ids, swapped.astype(jnp.int32)])
    segments = own_slots(ids_both[jnp.bitwise_xor(core, high_part)])
    first = section == 0
    own_taps = jnp.concatenate(
        [
            short_taps[0].reshape(9, channels),
            cond_taps[0],
            spectral_gain[0],
            jnp.zeros((2, channels), jnp.float32),
        ],
        axis=0,
    )
    own_taps = transposed(own_taps)
    own_gains = jnp.concatenate([norm_gain1, norm_gain2], axis=0)

    def both_layers(own):
        other = swap_section(own)
        return jnp.stack([jnp.where(first, own, other), jnp.where(first, other, own)])

    taps = both_layers(own_taps)
    gains = both_layers(own_gains)

    def columns(ids):
        prev, nxt = neighbours(ids)
        masks = [(ids == g).astype(jnp.float32) for g in range(SEGS)]
        return jnp.stack([prev, nxt] + masks + [jnp.zeros_like(prev)] * 2, axis=1)

    cols = [columns(segments[index]) for index in range(packs)]
    line = Line()

    def by_layer(part, other):
        return jnp.where(first, part, other), jnp.where(first, other, part)

    w_io, spectra, gate_up, down = [None, None], [None, None], [None, None], [None, None]
    results = [[], []]
    saved = [[], []]
    late = []
    for index in range(packs):
        state = rows_in[index].astype(jnp.float32)
        for layer in range(2):
            opening = index == 0 and layer == 0
            normed, norm_pull = jax.vjp(layer_norm, state, gains[layer, 0])
            blocks = gather_rows(low(normed))
            if opening:
                io_other, sp_other = swap_section(io_part), swap_section(sp_part)
                dn_moved = transposed(dn_own)
                gu_moved = transposed(gu_own)
                blocks, io_other, sp_other = tie(blocks, io_other, sp_other)
                sp_both = by_layer(sp_part, sp_other)
                spectra[0] = join_parts(sp_both[0])
                io_both = by_layer(io_part, io_other)
                w_io[0] = join_parts(io_both[0])
                line.mark(io_both[0], sp_both[0])
                dn_part = line.take(dn_moved)
                dn_other = swap_section(dn_part)
                line.mark(dn_part)
                gu_part = line.take(gu_moved)
                dn_both = by_layer(dn_part, after(dn_other, gu_part))
                blocks, gu_part, dn_first, cot_own = tie(blocks, gu_part, dn_both[0], own_slots(cotangent))
                cot_in = transposed(cot_own)
                gu_other = swap_section(gu_part)
                down[0] = join_parts(dn_first)
            parts, gathered, mix, kept = mixer_forward(
                blocks, w_io[layer], taps[layer : layer + 1], cols[index], spectra[layer], tables,
                order, places,
            )
            if opening:
                gu_both = by_layer(gu_part, after(gu_other, parts))
                parts, gu_first, cot_in, down[0] = tie(parts, gu_both[0], cot_in, down[0])
            if layer == 1:
                parts, cot_chip = tie(parts, cot_chip)
            if index == 0 and layer == 1:
                parts, gate_up[1] = tie(parts, gate_up[1])
            sums_of = core_sums(parts)
            if opening:
                gate_up[0] = join_parts(gu_first)
            if layer == 1:
                cot_blocks = both_cores(cot_chip)
            moved_sums = sent_sums(sums_of)
            if index == 0 and layer == 1:
                moved_sums, down[1] = tie(moved_sums, down[1])
            hidden = state + add_sums(sums_of, moved_sums)
            normed_two, norm_pull_two = jax.vjp(layer_norm, hidden, gains[layer, 1])
            blocks = gather_rows(low(normed_two))
            if opening:
                io_part, sp_part = after((io_both[1], sp_both[1]), blocks)
                w_io[1] = join_parts(io_part)
                spectra[1] = join_parts(sp_part)
            parts, (gathered_two, gate, up, act) = glu_forward(
                blocks, gate_up[layer], down[layer], places
            )
            saved[layer].append(
                (norm_pull, gathered, mix, kept, norm_pull_two, gathered_two, gate, up, act)
            )
            if layer == 0:
                sums_of = core_sums(parts)
                if opening:
                    gu_part, dn_part = after((gu_both[1], dn_both[1]), sums_of)
                    gate_up[1] = join_parts(gu_part)
                    down[1] = join_parts(dn_part)
                moved_sums = sent_sums(sums_of)
                state = hidden + add_sums(sums_of, moved_sums)
                results[0].append(state)
                cot_chip = chip_blocks(after(cot_in[index], state))
            else:
                late.append((hidden, parts, cot_blocks))

    def deliver(zero, one):
        keep = transposed(jnp.where(first, zero, one))
        given = permute(
            jnp.where(first, one, zero),
            ("section", "core", "th"),
            lambda s, c, h: (1 - s, h, c),
        )
        return keep, given

    def ordered(keep, given):
        lead = jnp.where(first, keep, given)
        trail = jnp.where(first, given, keep)
        return jnp.concatenate([lead, trail], axis=0).astype(jnp.float32)

    sums = [{}, {}]

    def collect(layer, terms, last):
        for name, term in terms.items():
            total = term if name not in sums[layer] else sums[layer][name] + term
            sums[layer][name] = low(total) if last else total.astype(jnp.float32)

    def glu_terms(layer, kept, sums_of, grad_rows, gate_grad, up_grad, last):
        act, rows_two, grad_rows, gate_grad, up_grad = after(
            (kept[8], kept[5], grad_rows, gate_grad, up_grad), sums_of
        )
        half = width // 2
        terms = {
            "down": dot32("lf,ld->fd", act, grad_rows),
            "gate_a": dot32("ld,lf->df", rows_two[:, :half], gate_grad),
            "gate_b": dot32("ld,lf->df", rows_two[:, half:], gate_grad),
            "up": dot32("ld,lf->df", rows_two, up_grad),
        }
        collect(layer, terms, last)

    def small_rows(tap_grad, gain_one, gain_two):
        rows_of = jnp.pad(tap_grad, ((0, 0), (0, width - channels)))
        filled = rows_of.shape[0] + 2
        return jnp.concatenate(
            [rows_of, gain_one, gain_two[None], jnp.zeros((-filled % 64, width), jnp.float32)], axis=0
        )

    def mix_terms(layer, kept, sums_of, mix_rows, proj_grad, spectrum_grad, small, last):
        mix, mix_rows, proj_grad, rows_one = after((kept[2], mix_rows, proj_grad, kept[1]), sums_of)
        terms = {
            "w_in": dot32("lc,ld->cd", proj_grad, rows_one),
            "w_out": dot32("lc,ld->cd", mix, mix_rows),
            "spectrum": spectrum_grad,
            "small": small,
        }
        collect(layer, terms, last)

    contents = (("down", "gate_a"), ("gate_b", "up"), ("w_in", "w_out", "spectrum", "small"))
    own = [{}, {}]
    moved = [{}, {}]
    crossed = [{}, {}]

    def send_dq(layer, m, *events):
            arrays = pack(after([sums[layer][name] for name in contents[m]], *events))
            sent = [exchange_dq(a) for a in arrays]
            own[layer][m] = [s[0] for s in sent]
            moved[layer][m] = [s[1] for s in sent]

    def add_own(layer, m, *events):
        terms = after(moved[layer][m], *events)
        own[layer][m] = [total_dq(o, t) for o, t in zip(own[layer][m], terms)]

    def cross(layer, m):
        crossed[layer][m] = [to_section(o, layer) for o in own[layer][m]]

    total = {}
    held = {}

    def add_total(m, *events):
        terms = after((crossed[0][m], crossed[1][m]), *events)
        total[m] = [
            jnp.where(first, o, p) + jnp.where(first, t, u).astype(jnp.float32)
            for o, p, t, u in zip(own[0][m], own[1][m], *terms)
        ]

    def hold(m):
        held[m] = [to_holder(t) for t in total[m]]

    grads_in = [[], []]
    for index in range(packs):
        last = index == packs - 1
        state = cot_in[index].astype(jnp.float32)
        kept = saved[1][index]
        late_hidden, late_parts, cot_blocks = late[index]
        parts, (grad_rows, gate_grad, up_grad) = glu_backward(
            cot_blocks, kept[6], kept[7], gate_up[1], down[1], places
        )
        sums_of = core_sums(parts)
        glu_terms(1, kept, sums_of, grad_rows, gate_grad, up_grad, last)
        grad_part, gain_two = kept[4](chip_sums(sums_of))
        hidden_grad = state + grad_part
        if last:
            send_dq(1, 0)
            send_dq(1, 1, hidden_grad)
        blocks = gather_rows(low(hidden_grad))
        late_sums = core_sums(after(late_parts, hidden_grad))
        blocks, late_sums = tie(blocks, late_sums)
        late_moved = sent_sums(late_sums)
        parts, mix_rows, proj_grad, spectrum_grad, tap_grad, gain_one = mixer_backward(
            blocks, w_io[1], taps[1:2], cols[index], kept[1], gains[1, 0:1], kept[3], spectra[1],
            tables, order, places,
        )
        parts, late_moved = tie(parts, late_moved)
        if last:
            parts, moved[1][0], moved[1][1] = tie(parts, moved[1][0], moved[1][1])
        sums_of = core_sums(parts)
        results[1].append(late_hidden + add_sums(late_sums, after(late_moved, sums_of)))
        moved_sums = sent_sums(sums_of)
        if last:
            add_own(1, 0, sums_of)
            add_own(1, 1, sums_of)
            moved_sums, own[1][0], own[1][1], results[1][-1] = tie(
                moved_sums, own[1][0], own[1][1], results[1][-1]
            )
            cross(1, 0)
            cross(1, 1)
            out_sent = deliver(low(jnp.stack(results[0])), low(jnp.stack(results[1])))
        state = hidden_grad + kept[0](add_sums(sums_of, moved_sums))[0]
        grads_in[1].append(state)
        small = small_rows(tap_grad, gain_one, gain_two)
        mix_terms(1, kept, state, mix_rows, proj_grad, spectrum_grad, small, last)
        if last:
            send_dq(1, 2)
        kept = saved[0][index]
        blocks = gather_rows(low(state))
        if last:
            blocks, own[1][2] = tie(blocks, own[1][2])
        parts, (grad_rows, gate_grad, up_grad) = glu_backward(
            blocks, kept[6], kept[7], gate_up[0], down[0], places
        )
        if last:
            parts, out_sent = tie(parts, out_sent)
        sums_of = core_sums(parts)
        glu_terms(0, kept, sums_of, grad_rows, gate_grad, up_grad, last)
        moved_sums = sent_sums(sums_of)
        if last:
            send_dq(0, 0)
            layer_out = ordered(*after(out_sent, sums_of))
            moved_sums, own[0][0], layer_out = tie(moved_sums, own[0][0], layer_out)
        grad_part, gain_two = kept[4](add_sums(sums_of, moved_sums))
        hidden_grad = state + grad_part
        blocks = gather_rows(low(hidden_grad))
        if last:
            send_dq(0, 1, hidden_grad)
            add_own(1, 2, blocks)
            blocks, own[0][1], own[1][2] = tie(blocks, own[0][1], own[1][2])
            cross(1, 2)
        parts, mix_rows, proj_grad, spectrum_grad, tap_grad, gain_one = mixer_backward(
            blocks, w_io[0], taps[0:1], cols[index], kept[1], gains[0, 0:1], kept[3], spectra[0],
            tables, order, places,
        )
        small = small_rows(tap_grad, gain_one, gain_two)
        if last:
            parts, moved[0][0], moved[0][1], crossed[1][2] = tie(
                parts, moved[0][0], moved[0][1], crossed[1][2]
            )
            add_own(0, 0, parts)
            parts, own[0][0] = tie(parts, own[0][0])
            cross(0, 0)
            mix_terms(0, kept, parts, mix_rows, proj_grad, spectrum_grad, small, last)
            send_dq(0, 2)
            parts, own[0][2] = tie(parts, own[0][2])
        sums_of = core_sums(parts)
        if last:
            add_own(0, 1, sums_of)
        else:
            mix_terms(0, kept, sums_of, mix_rows, proj_grad, spectrum_grad, small, last)
        moved_sums = sent_sums(sums_of)
        if last:
            break
        grads_in[0].append(hidden_grad + kept[0](add_sums(sums_of, moved_sums))[0])

    line.mark(own[0][1])
    add_total(0, line.events)
    (total[0], own[0][1]) = tie(total[0], own[0][1])
    hold(0)
    cross(0, 1)
    line.mark(total[0])
    joined = {}

    def send_joined(m):
        terms = [holder_total(t, o) for t, o in zip(total[m], line.take(held[m]))]
        line.mark(terms)
        joined[m] = [join_holders(t) for t in terms]

    state = hidden_grad + kept[0](add_sums(sums_of, line.take(moved_sums)))[0]
    grads_in[0].append(state)
    line.mark(state)
    add_own(0, 2, line.events)
    cross(0, 2)
    line.mark(own[0][2])
    grad_sent = deliver(low(jnp.stack(grads_in[0])), low(jnp.stack(grads_in[1])))
    crossed[0][1], grad_sent = tie(crossed[0][1], grad_sent)
    add_total(1, line.events)
    hold(1)
    line.mark(total[1])
    send_joined(0)
    crossed[0][2], held[1] = tie(crossed[0][2], held[1])
    add_total(2)
    hold(2)
    line.mark(total[2])
    send_joined(1)
    held[2], joined[0], joined[1] = tie(held[2], joined[0], joined[1])
    line.mark(held[2])
    send_joined(2)
    grad_in = ordered(*line.take(grad_sent))

    small_count = small.shape[0]

    def finish_wide(buffers, outs):
        take = row_reader(buffers)
        outs[0][...] = take(hidden_cols)
        outs[1][: width // 2, 0, :] = take(width // 2)
        outs[1][width // 2 :, 0, :] = take(width // 2)
        outs[1][:, 1, :] = take(width)

    def finish_rest(buffers, outs):
        take = row_reader(buffers)
        outs[0][...] = take(3 * channels)
        outs[1][...] = take(channels)
        outs[2][...] = take(2 * channels)[:, :freqs]
        outs[3][...] = take(small_count)

    grad_down, grad_gate_up = assemble(
        line.take(joined[0] + joined[1]),
        places,
        finish_wide,
        [(hidden_cols, width), (width, 2, hidden_cols)],
    )
    grad_down, joined[2] = tie(grad_down, joined[2])
    send_joined(2)
    grad_w_in, grad_w_out, grad_spectrum, small_total = assemble(
        joined[2],
        places,
        finish_rest,
        [
            (3 * channels, width),
            (channels, width),
            (2 * channels, freqs),
            (small_count, width),
        ],
    )
    grad_spectrum = grad_spectrum.reshape(2, channels, freqs)
    rows_of = own_taps.shape[0]
    tap_grads = small_total[:rows_of, :channels]
    gain_total = small_total[rows_of : rows_of + 2]
    gain_total = gain_total + permute(gain_total, ("th",), lambda h: (1 - h,))
    gain_moved = [shift(gain_total, "tl", k) for k in range(1, peers)]
    for term in gain_moved:
        gain_total = gain_total + term
    return (
        layer_out[None],
        grad_in[None],
        gain_total[0:1],
        jnp.transpose(grad_w_in.reshape(3, channels, width), (2, 0, 1))[None],
        tap_grads[:9].reshape(1, 3, 3, channels),
        tap_grads[9:12][None],
        jnp.transpose(grad_spectrum, (0, 2, 1))[None],
        tap_grads[12:14][None],
        grad_w_out[None],
        gain_total[1:2],
        grad_gate_up[None],
        grad_down[None],
    )


def solution(mesh):
    sections, dps, tensors = (mesh.shape[a] for a in ("section", "dp", "tensor"))
    devices = mesh.devices.reshape(sections, dps // 2, 2, 2, tensors // 2)
    fine = Mesh(devices, ALL_AXES)
    dp = ("dq", "core")
    tensor = ("th", "tl")
    return jax.shard_map(
        per_device,
        mesh=fine,
        in_specs=(
            P(dp, tensor, None),
            P(dp, None),
            P(dp, tensor, None),
            P("section", None),
            P("section", None, None, tensor),
            P("section", None, None, tensor),
            P("section", None, tensor),
            P("section", None, None, tensor),
            P("section", None, tensor),
            P("section", tensor, None),
            P("section", None),
            P("section", None, None, tensor),
            P("section", tensor, None),
        ),
        out_specs=(
            P("section", dp, tensor, None),
            P("section", dp, tensor, None),
            P("section", None),
            P("section", None, None, tensor),
            P("section", None, None, tensor),
            P("section", None, tensor),
            P("section", None, None, tensor),
            P("section", None, tensor),
            P("section", tensor, None),
            P("section", None),
            P("section", None, None, tensor),
            P("section", tensor, None),
        ),
        check_vma=False,
    )
```

```python
from functools import partial
import math

import jax
import jax.numpy as jnp
import numpy as np
from jax import lax
from jax.experimental import pallas as pl
from jax.experimental.pallas import tpu as pltpu
from jax.sharding import Mesh
from jax.sharding import PartitionSpec as P

SEGS = 4

FTILE = 256
HTILE = 384
PEAK = 1.0e9
MIB = 1024 * 1024

ALL_AXES = ("section", "dq", "core", "th", "tl")


def permute(values, axes, mapping):
    sizes = [lax.axis_size(a) for a in axes]
    pairs = []
    total = math.prod(sizes)
    for source in range(total):
        place = []
        rest = source
        for size in reversed(sizes):
            place.append(rest % size)
            rest //= size
        place = tuple(reversed(place))
        target = mapping(*place)
        if target is None:
            continue
        flat = 0
        for size, at in zip(sizes, target):
            flat = flat * size + at
        pairs.append((source, flat))
    return lax.ppermute(values, axes if len(axes) > 1 else axes[0], pairs)


def swap_core(values):
    return permute(values, ("core",), lambda c: (1 - c,))


def swap_section(values):
    return permute(values, ("section",), lambda s: (1 - s,))


def shift(values, axis, by):
    size = lax.axis_size(axis)
    return permute(values, (axis,), lambda j: ((j + by) % size,))


def transposed(values):
    return permute(values, ("core", "th"), lambda c, h: (h, c))


def chip_blocks(rows):
    return [rows] + [shift(rows, "tl", k) for k in range(1, lax.axis_size("tl"))]


def both_cores(blocks):
    return blocks + [swap_core(block) for block in blocks]


def gather_rows(rows):
    return both_cores(chip_blocks(rows))


def core_sums(blocks):
    peers = lax.axis_size("tl")
    order = list(range(1, peers)) + [0]
    sums = {k: blocks[k] + swap_core(blocks[peers + k]) for k in order}
    return [sums[k] for k in range(peers)]


def sent_sums(sums):
    return [shift(sums[k], "tl", -k) for k in range(1, len(sums))]


def add_sums(sums, moved):
    total = sums[0]
    for term in moved:
        total = total + term.astype(jnp.float32)
    return total


def chip_sums(sums):
    return add_sums(sums, sent_sums(sums))


def after(values, *events):
    return lax.optimization_barrier((values, events))[0]


def tie(*values):
    return lax.optimization_barrier(values)


class Line:
    def __init__(self):
        self.events = ()

    def take(self, values):
        return after(values, self.events)

    def mark(self, *events):
        self.events = events


def layer_norm(values, gain):
    row_mean = jnp.mean(values, axis=-1, keepdims=True)
    centred = values - row_mean
    variance = jnp.mean(centred * centred, axis=-1, keepdims=True)
    return centred * lax.rsqrt(variance + 1e-05) * gain


def neighbours(segments):
    equal = (segments[1:] == segments[:-1]).astype(jnp.float32)
    blank = jnp.zeros((1,), jnp.float32)
    return (jnp.concatenate([blank, equal]), jnp.concatenate([equal, blank]))


def table_size(pack_len):
    return -(-(pack_len + 1) // FTILE) * FTILE


def split(values):
    upper = values.astype(jnp.bfloat16)
    lower = (values - upper.astype(jnp.float32)).astype(jnp.bfloat16)
    return upper, lower


def mm(a, b):
    return jnp.dot(a, b, preferred_element_type=jnp.float32)


def mm_t(a, b):
    return lax.dot_general(a, b, (((1,), (1,)), ((), ())), preferred_element_type=jnp.float32)


def mm3(upper, lower, b_upper, b_lower):
    return mm(upper, b_upper) + (mm(upper, b_lower) + mm(lower, b_upper))


STEP = 32


def tables_kernel(coarse_cos, coarse_sin, fine_cos, fine_sin, cos_hi, cos_lo, sin_hi, sin_lo):
    def body(p, carry):
        cc = coarse_cos[pl.ds(p, 1), :]
        cs = coarse_sin[pl.ds(p, 1), :]
        rows = pl.ds(pl.multiple_of(p * STEP, STEP), STEP)
        upper, lower = split(cc * fine_cos[...] - cs * fine_sin[...])
        cos_hi[rows, :] = upper
        cos_lo[rows, :] = lower
        upper, lower = split(cs * fine_cos[...] + cc * fine_sin[...])
        sin_hi[rows, :] = upper
        sin_lo[rows, :] = lower
        return carry

    lax.fori_loop(0, cos_hi.shape[0] // STEP, body, 0)


def spectral_tables(pack_len):
    size = table_size(pack_len)
    period = 2 * pack_len
    column = np.arange(size, dtype=np.int64)[None, :]
    coarse = (np.arange(size // STEP, dtype=np.int64)[:, None] * STEP * column) % period
    fine = (np.arange(STEP, dtype=np.int64)[:, None] * column) % period
    to_angle = 2.0 * np.pi / period
    small = [f(x * to_angle).astype(np.float32) for x in (coarse, fine) for f in (np.cos, np.sin)]
    return pl.pallas_call(
        tables_kernel,
        out_shape=[jax.ShapeDtypeStruct((size, size), jnp.bfloat16)] * 4,
        cost_estimate=pl.CostEstimate(flops=int(4 * PEAK), bytes_accessed=0, transcendentals=0),
        compiler_params=pltpu.CompilerParams(vmem_limit_bytes=12 * MIB),
        name="tables",
    )(*small)


def row_before(values):
    return pltpu.roll(values, 1, 0)


def row_after(values):
    return pltpu.roll(values, values.shape[0] - 1, 0)


def freq_weight(pack_len, step, shape):
    f = lax.broadcasted_iota(jnp.int32, shape, 0) + step * FTILE
    edge = (f == 0) | (f == pack_len)
    weight = jnp.where(edge, 1.0, 2.0) / (2.0 * pack_len)
    return f <= pack_len, jnp.where(f <= pack_len, weight, 0.0)


def join(whole_rows, parts, places):
    for k, part in enumerate(parts):
        count = part.shape[0]
        at = pl.ds(pl.multiple_of(places[k] * count, 8), count)
        whole_rows[at, :] = part[...]


def mixer_kernel(nb, np_, order, places, *refs):
    rows = refs[:nb]
    w_parts, s_parts = refs[nb : nb + np_], refs[nb + np_ : nb + 2 * np_]
    refs = refs[nb + 2 * np_ :]
    (taps, cols, ch_r, cl_r, sh_r, sl_r, ch_c, cl_c, sh_c, sl_c) = refs[:10]
    parts = refs[10 : nb + 10]
    (gathered, mix, proj, long, cond_hat, piece_hat) = refs[nb + 10 : nb + 16]
    x_hi, x_lo, acc, query, w_in_out, spectrum = refs[nb + 16 :]
    step = pl.program_id(0)
    count = rows[0].shape[0]
    pack_len = proj.shape[0]
    width = mix.shape[2]
    scale = 1.0 / math.sqrt(pack_len)

    @pl.when(step == 0)
    def _():
        join(w_in_out, w_parts, places)
        for j in range(nb):
            gathered[j] = rows[j][...]
            at = pl.ds(pl.multiple_of(order[j] * count, 8), count)
            proj[at, :] = mm_t(rows[j][...], w_in_out[: 3 * width, :])
        prev = cols[:, 0:1]
        nxt = cols[:, 1:2]

        def short(values, w0, w1, w2):
            return w0 * (row_before(values) * prev) + w1 * values + w2 * (row_after(values) * nxt)

        def one(k):
            return short(
                proj[:, k * width : (k + 1) * width],
                taps[0, k : k + 1, :],
                taps[0, 3 + k : 4 + k, :],
                taps[0, 6 + k : 7 + k, :],
            )

        query[...] = one(0)
        condition = short(one(1), taps[0, 9:10, :], taps[0, 10:11, :], taps[0, 11:12, :])
        value = one(2)
        x_hi[pack_len:, :] = jnp.zeros((x_hi.shape[0] - pack_len, x_hi.shape[1]), jnp.bfloat16)
        x_lo[pack_len:, :] = jnp.zeros((x_hi.shape[0] - pack_len, x_hi.shape[1]), jnp.bfloat16)
        pieces = [value * cols[:, 2 + g : 3 + g] for g in range(SEGS)] + [condition]
        for g, piece in enumerate(pieces):
            upper, lower = split(piece)
            x_hi[:pack_len, g * width : (g + 1) * width] = upper
            x_lo[:pack_len, g * width : (g + 1) * width] = lower
        acc[...] = jnp.zeros_like(acc)

    wide = SEGS * width
    hat_re = mm3(ch_r[...], cl_r[...], x_hi[...], x_lo[...])
    hat_im = -mm3(sh_r[...], sl_r[...], x_hi[...], x_lo[...])
    v_re, v_im = hat_re[:, :wide], hat_im[:, :wide]
    c_re, c_im = hat_re[:, wide:], hat_im[:, wide:]
    cond_hat[0] = c_re
    cond_hat[1] = c_im
    piece_hat[0] = v_re
    piece_hat[1] = v_im
    gain_in = taps[0, 12:13, :] * scale
    gain_out = taps[0, 13:14, :]
    inside, weight = freq_weight(pack_len, step, c_re.shape)
    join(spectrum, s_parts, places)
    s_re = jnp.transpose(spectrum[:width, :])
    s_im = jnp.transpose(spectrum[width:, :])
    f_re = jnp.where(inside, s_re + gain_out * jnp.tanh(gain_in * c_re), 0.0) * weight
    f_im = jnp.where(inside, s_im + gain_out * jnp.tanh(gain_in * c_im), 0.0) * weight
    f_re = jnp.concatenate([f_re] * SEGS, axis=1)
    f_im = jnp.concatenate([f_im] * SEGS, axis=1)
    p_hi, p_lo = split(v_re * f_re - v_im * f_im)
    m_hi, m_lo = split(-(v_re * f_im + v_im * f_re))
    acc[...] += mm3(ch_c[...], cl_c[...], p_hi, p_lo) + mm3(sh_c[...], sl_c[...], m_hi, m_lo)

    @pl.when(step == pl.num_programs(0) - 1)
    def _():
        total = acc[:, :width] * cols[:, 2:3]
        for g in range(1, SEGS):
            total = total + acc[:, g * width : (g + 1) * width] * cols[:, 2 + g : 3 + g]
        long[...] = total
        query[...] = query[...] * total
        for j in range(nb):
            at = pl.ds(pl.multiple_of(order[j] * count, 8), count)
            mixed = query[at, :].astype(jnp.bfloat16)
            mix[j] = mixed
            parts[j][...] = mm(mixed, w_in_out[3 * width :, :])


def table_specs(size, pack_len):
    row = pl.BlockSpec((FTILE, size), lambda i: (i, 0))
    col = pl.BlockSpec((pack_len, FTILE), lambda i: (0, i))
    return [row] * 4 + [col] * 4


def whole(shape):
    zeros = (0,) * len(shape)
    return pl.BlockSpec(shape, lambda i: zeros)


def of_layer(layer, shape):
    rest = (0,) * len(shape)
    return pl.BlockSpec((1,) + shape, lambda i: (layer,) + rest)


SMEM = pl.BlockSpec(memory_space=pltpu.SMEM)


def part_specs(w_in_out, spectra):
    return [whole(p.shape) for p in w_in_out] + [
        pl.BlockSpec((p.shape[0], FTILE), lambda i: (0, i)) for p in spectra
    ]


def part_scratch(w_in_out, spectra):
    peers = len(w_in_out)
    return [
        pltpu.VMEM((peers * w_in_out[0].shape[0], w_in_out[0].shape[1]), jnp.bfloat16),
        pltpu.VMEM((peers * spectra[0].shape[0], FTILE), jnp.float32),
    ]


def mixer_forward(blocks, w_in_out, taps, cols, spectra, tables, order, places, mib):
    layer = 0
    pack_len = cols.shape[0]
    nb = len(blocks)
    count, model = blocks[0].shape
    width = taps.shape[2]
    size = tables[0].shape[0]
    f32, low = jnp.float32, jnp.bfloat16
    out = pl.pallas_call(
        partial(mixer_kernel, nb, len(w_in_out)),
        grid=(size // FTILE,),
        in_specs=[SMEM, SMEM]
        + [whole((count, model))] * nb
        + part_specs(w_in_out, spectra)
        + [of_layer(layer, taps.shape[1:]), whole(cols.shape)]
        + table_specs(size, pack_len),
        out_specs=[whole((count, model))] * nb
        + [
            whole((nb, count, model)),
            whole((nb, count, width)),
            whole((pack_len, 3 * width)),
            whole((pack_len, width)),
            pl.BlockSpec((2, FTILE, width), lambda i: (0, i, 0)),
            pl.BlockSpec((2, FTILE, SEGS * width), lambda i: (0, i, 0)),
        ],
        out_shape=[jax.ShapeDtypeStruct((count, model), f32)] * nb
        + [
            jax.ShapeDtypeStruct((nb, count, model), low),
            jax.ShapeDtypeStruct((nb, count, width), low),
            jax.ShapeDtypeStruct((pack_len, 3 * width), f32),
            jax.ShapeDtypeStruct((pack_len, width), f32),
            jax.ShapeDtypeStruct((2, size, width), f32),
            jax.ShapeDtypeStruct((2, size, SEGS * width), f32),
        ],
        scratch_shapes=[
            pltpu.VMEM((size, (SEGS + 1) * width), low),
            pltpu.VMEM((size, (SEGS + 1) * width), low),
            pltpu.VMEM((pack_len, SEGS * width), f32),
            pltpu.VMEM((pack_len, width), f32),
        ]
        + part_scratch(w_in_out, spectra),
        compiler_params=pltpu.CompilerParams(vmem_limit_bytes=mib * MIB),
        cost_estimate=pl.CostEstimate(flops=int(26 * PEAK), bytes_accessed=0, transcendentals=0),
        name="mixer_forward",
    )(order, places, *blocks, *w_in_out, *spectra, taps, cols, *tables, *tables)
    return out[:nb], out[nb].reshape(pack_len, model), out[nb + 1].reshape(pack_len, width), out[nb + 2 :]


def mixer_grad_kernel(nb, np_, order, places, *refs):
    grads = refs[:nb]
    w_parts, s_parts = refs[nb : nb + np_], refs[nb + np_ : nb + 2 * np_]
    refs = refs[nb + 2 * np_ :]
    (taps, cols, normed, gain, proj, long, cond_hat, piece_hat) = refs[:8]
    (ch_r, cl_r, sh_r, sl_r, ch_c, cl_c, sh_c, sl_c) = refs[8:16]
    partials = refs[16 : nb + 16]
    gathered, proj_grad, grad_spectrum, grad_taps, grad_gain = refs[nb + 16 : nb + 21]
    x_hi, x_lo, acc, query_grad, full, w_in_out, spectrum = refs[nb + 21 :]
    step = pl.program_id(0)
    count = grads[0].shape[0]
    pack_len = proj.shape[0]
    width = long.shape[1]
    wide = SEGS * width
    scale = 1.0 / math.sqrt(pack_len)

    def short(values, w0, w1, w2):
        return (
            w0 * (row_before(values) * cols[:, 0:1])
            + w1 * values
            + w2 * (row_after(values) * cols[:, 1:2])
        )

    @pl.when(step == 0)
    def _():
        join(w_in_out, w_parts, places)
        for j in range(nb):
            gathered[j] = grads[j][...]
            at = pl.ds(pl.multiple_of(order[j] * count, 8), count)
            query_grad[at, :] = mm_t(grads[j][...], w_in_out[3 * width :, :])
        query = short(proj[:, :width], taps[0, 0:1, :], taps[0, 3:4, :], taps[0, 6:7, :])
        mix_grad = query_grad[...]
        long_grad = mix_grad * query
        query_grad[...] = mix_grad * long[...]
        x_hi[pack_len:, :] = jnp.zeros((x_hi.shape[0] - pack_len, wide), jnp.bfloat16)
        x_lo[pack_len:, :] = jnp.zeros((x_hi.shape[0] - pack_len, wide), jnp.bfloat16)
        for g in range(SEGS):
            upper, lower = split(long_grad * cols[:, 2 + g : 3 + g])
            x_hi[:pack_len, g * width : (g + 1) * width] = upper
            x_lo[:pack_len, g * width : (g + 1) * width] = lower
        acc[...] = jnp.zeros_like(acc)
        grad_taps[...] = jnp.zeros_like(grad_taps)

    c_re, c_im = cond_hat[0], cond_hat[1]
    inside, weight = freq_weight(pack_len, step, c_re.shape)
    w4 = jnp.concatenate([weight] * SEGS, axis=1)
    b_re = mm3(ch_r[...], cl_r[...], x_hi[...], x_lo[...]) * w4
    b_im = mm3(sh_r[...], sl_r[...], x_hi[...], x_lo[...]) * (-w4)
    v_re, v_im = piece_hat[0], piece_hat[1]

    def over_segments(values):
        total = values[:, :width]
        for g in range(1, SEGS):
            total = total + values[:, g * width : (g + 1) * width]
        return total

    h_re = over_segments(v_re * b_re + v_im * b_im)
    h_im = over_segments(v_re * b_im - v_im * b_re)
    grad_spectrum[0] = jnp.transpose(h_re).astype(jnp.bfloat16)
    grad_spectrum[1] = jnp.transpose(h_im).astype(jnp.bfloat16)
    gain_in = taps[0, 12:13, :] * scale
    gain_out = taps[0, 13:14, :]
    t_re = jnp.tanh(gain_in * c_re)
    t_im = jnp.tanh(gain_in * c_im)
    join(spectrum, s_parts, places)
    f_re = jnp.where(inside, jnp.transpose(spectrum[:width, :]) + gain_out * t_re, 0.0)
    f_im = jnp.where(inside, jnp.transpose(spectrum[width:, :]) + gain_out * t_im, 0.0)
    a_re = h_re * gain_out * (1.0 - t_re * t_re)
    a_im = h_im * gain_out * (1.0 - t_im * t_im)
    grad_taps[12:13, :] += jnp.sum(a_re * c_re + a_im * c_im, axis=0, keepdims=True) * scale
    grad_taps[13:14, :] += jnp.sum(h_re * t_re + h_im * t_im, axis=0, keepdims=True)
    f_re = jnp.concatenate([f_re] * SEGS, axis=1)
    f_im = jnp.concatenate([f_im] * SEGS, axis=1)
    p = jnp.concatenate([f_re * b_re + f_im * b_im, a_re * gain_in], axis=1)
    m = jnp.concatenate([f_im * b_re - f_re * b_im, -(a_im * gain_in)], axis=1)
    p_hi, p_lo = split(p)
    m_hi, m_lo = split(m)
    acc[...] += mm3(ch_c[...], cl_c[...], p_hi, p_lo) + mm3(sh_c[...], sl_c[...], m_hi, m_lo)

    @pl.when(step == pl.num_programs(0) - 1)
    def _():
        prev = cols[:, 0:1]
        nxt = cols[:, 1:2]
        value_grad = acc[:, :width] * cols[:, 2:3]
        for g in range(1, SEGS):
            value_grad = value_grad + acc[:, g * width : (g + 1) * width] * cols[:, 2 + g : 3 + g]

        def column_sum(values):
            return jnp.sum(values, axis=0, keepdims=True)

        def adjoint(values, grad, row, stride):
            w0 = taps[0, row : row + 1, :]
            w1 = taps[0, row + stride : row + stride + 1, :]
            w2 = taps[0, row + 2 * stride : row + 2 * stride + 1, :]
            from_prev = prev * grad
            from_next = nxt * grad
            grad_taps[row : row + 1, :] = column_sum(row_before(values) * from_prev)
            grad_taps[row + stride : row + stride + 1, :] = column_sum(values * grad)
            grad_taps[row + 2 * stride : row + 2 * stride + 1, :] = column_sum(
                row_after(values) * from_next
            )
            return w1 * grad + w0 * row_after(from_prev) + w2 * row_before(from_next)

        key_proj = proj[:, width : 2 * width]
        key_part = short(key_proj, taps[0, 1:2, :], taps[0, 4:5, :], taps[0, 7:8, :])
        key_grad = adjoint(key_part, acc[:, wide:], 9, 1)
        parts = [query_grad[...], key_grad, value_grad]
        for j in range(3):
            full[:, j * width : (j + 1) * width] = adjoint(
                proj[:, j * width : (j + 1) * width], parts[j], j, 3
            )
        for j in range(nb):
            at = pl.ds(pl.multiple_of(order[j] * count, 8), count)
            low = full[at, :].astype(jnp.bfloat16)
            proj_grad[j] = low
            rows_grad = mm(low, w_in_out[: 3 * width, :])
            partials[j][...] = rows_grad
            seen = normed[j * count : (j + 1) * count, :].astype(jnp.float32)
            term = jnp.sum(rows_grad * seen, axis=0, keepdims=True)
            gain_sum = term if j == 0 else gain_sum + term
        grad_gain[...] = gain_sum / gain[...]


def mixer_backward(blocks, w_in_out, taps, cols, normed, gain, kept, spectra, tables, order, places):
    layer = 0
    proj, long, cond_hat, piece_hat = kept
    pack_len = cols.shape[0]
    nb = len(blocks)
    count, model = blocks[0].shape
    width = taps.shape[2]
    size = tables[0].shape[0]
    f32, low = jnp.float32, jnp.bfloat16
    freq = pl.BlockSpec((2, FTILE, width), lambda i: (0, i, 0))
    out = pl.pallas_call(
        partial(mixer_grad_kernel, nb, len(w_in_out)),
        grid=(size // FTILE,),
        in_specs=[SMEM, SMEM]
        + [whole((count, model))] * nb
        + part_specs(w_in_out, spectra)
        + [
            of_layer(layer, taps.shape[1:]),
            whole(cols.shape),
            whole(normed.shape),
            whole(gain.shape),
            whole(proj.shape),
            whole(long.shape),
            freq,
            pl.BlockSpec((2, FTILE, SEGS * width), lambda i: (0, i, 0)),
        ]
        + table_specs(size, pack_len),
        out_specs=[whole((count, model))] * nb
        + [
            whole((nb, count, model)),
            whole((nb, count, 3 * width)),
            pl.BlockSpec((2, width, FTILE), lambda i: (0, 0, i)),
            whole(taps.shape[1:]),
            whole(gain.shape),
        ],
        out_shape=[jax.ShapeDtypeStruct((count, model), f32)] * nb
        + [
            jax.ShapeDtypeStruct((nb, count, model), low),
            jax.ShapeDtypeStruct((nb, count, 3 * width), low),
            jax.ShapeDtypeStruct((2, width, size), low),
            jax.ShapeDtypeStruct(taps.shape[1:], f32),
            jax.ShapeDtypeStruct(gain.shape, f32),
        ],
        scratch_shapes=[
            pltpu.VMEM((size, SEGS * width), low),
            pltpu.VMEM((size, SEGS * width), low),
            pltpu.VMEM((pack_len, (SEGS + 1) * width), f32),
            pltpu.VMEM((pack_len, width), f32),
            pltpu.VMEM((pack_len, 3 * width), f32),
        ]
        + part_scratch(w_in_out, spectra),
        compiler_params=pltpu.CompilerParams(vmem_limit_bytes=40 * MIB),
        cost_estimate=pl.CostEstimate(flops=int(30 * PEAK), bytes_accessed=0, transcendentals=0),
        name="mixer_backward",
    )(
        order, places, *blocks, *w_in_out, *spectra, taps, cols, normed, gain, proj, long, cond_hat,
        piece_hat,
        *tables, *tables,
    )
    rows, proj_grad, grad_spectrum, grad_taps, grad_gain = out[nb:]
    return (
        out[:nb],
        rows.reshape(pack_len, model),
        proj_grad.reshape(pack_len, 3 * width),
        grad_spectrum.reshape(2 * width, size),
        grad_taps,
        grad_gain,
    )


def glu_kernel(nb, np_, places, *refs):
    rows = refs[:nb]
    gu_parts, down_parts = refs[nb : nb + np_], refs[nb + np_ : nb + 2 * np_]
    refs = refs[nb + 2 * np_ :]
    parts = refs[:nb]
    gathered, gate, up, act, total, gate_up, down_w = refs[nb:]
    step = pl.program_id(0)
    count, model = rows[0].shape
    tile = gate.shape[1]
    join(gate_up, gu_parts, places)

    @pl.when(step == 0)
    def _():
        join(down_w, down_parts, places)
        for j in range(nb):
            gathered[j * count : (j + 1) * count, :] = rows[j][...]

    gates = mm(gathered[...], gate_up[:model, :])
    ups = mm(gathered[...], gate_up[model:, :])
    gate[...] = gates
    up[...] = ups
    low = (gates * jax.nn.sigmoid(gates) * ups).astype(jnp.bfloat16)
    act[...] = low
    grown = mm(low, down_w[pl.ds(pl.multiple_of(step * tile, tile), tile), :])

    @pl.when(step == 0)
    def _():
        total[...] = grown

    @pl.when(step > 0)
    def _():
        total[...] += grown

    @pl.when(step == pl.num_programs(0) - 1)
    def _():
        for j in range(nb):
            parts[j][...] = total[j * count : (j + 1) * count, :]


def glu_specs(gate_up, down, tile):
    return [pl.BlockSpec((p.shape[0], tile), lambda i: (0, i)) for p in gate_up] + [
        whole(p.shape) for p in down
    ]


def glu_scratch(gate_up, down, tile):
    peers = len(down)
    return [
        pltpu.VMEM((peers * gate_up[0].shape[0], tile), jnp.bfloat16),
        pltpu.VMEM((peers * down[0].shape[0], down[0].shape[1]), jnp.bfloat16),
    ]


def glu_forward(blocks, gate_up, down, places):
    nb = len(blocks)
    count, model = blocks[0].shape
    hidden = len(down) * down[0].shape[0]
    tile = min(HTILE, hidden)
    length = nb * count
    f32, low = jnp.float32, jnp.bfloat16
    column = pl.BlockSpec((length, tile), lambda i: (0, i))
    out = pl.pallas_call(
        partial(glu_kernel, nb, len(down)),
        grid=(hidden // tile,),
        in_specs=[SMEM] + [whole((count, model))] * nb + glu_specs(gate_up, down, tile),
        out_specs=[whole((count, model))] * nb + [whole((length, model))] + [column] * 3,
        out_shape=[jax.ShapeDtypeStruct((count, model), f32)] * nb
        + [
            jax.ShapeDtypeStruct((length, model), low),
            jax.ShapeDtypeStruct((length, hidden), f32),
            jax.ShapeDtypeStruct((length, hidden), f32),
            jax.ShapeDtypeStruct((length, hidden), low),
        ],
        scratch_shapes=[pltpu.VMEM((length, model), f32)] + glu_scratch(gate_up, down, tile),
        compiler_params=pltpu.CompilerParams(vmem_limit_bytes=28 * MIB),
        cost_estimate=pl.CostEstimate(flops=int(9 * PEAK), bytes_accessed=0, transcendentals=0),
        name="glu_forward",
    )(places, *blocks, *gate_up, *down)
    return out[:nb], out[nb:]


def glu_grad_kernel(nb, np_, places, *refs):
    rows = refs[:nb]
    gate, up = refs[nb : nb + 2]
    gu_parts, down_parts = refs[nb + 2 : nb + 2 + np_], refs[nb + 2 + np_ : nb + 2 + 2 * np_]
    refs = refs[nb + 2 + 2 * np_ :]
    parts = refs[:nb]
    gathered, gate_grad, up_grad, total, gate_up, down_w = refs[nb:]
    step = pl.program_id(0)
    count, model = rows[0].shape
    tile = gate.shape[1]
    join(gate_up, gu_parts, places)

    @pl.when(step == 0)
    def _():
        join(down_w, down_parts, places)
        for j in range(nb):
            gathered[j * count : (j + 1) * count, :] = rows[j][...]

    act_grad = mm_t(gathered[...], down_w[pl.ds(pl.multiple_of(step * tile, tile), tile), :])
    gates = gate[...]
    s = jax.nn.sigmoid(gates)
    low_gate = (act_grad * up[...] * (s * (1.0 + gates * (1.0 - s)))).astype(jnp.bfloat16)
    low_up = (act_grad * (gates * s)).astype(jnp.bfloat16)
    gate_grad[...] = low_gate
    up_grad[...] = low_up
    grown = mm_t(low_gate, gate_up[:model, :]) + mm_t(low_up, gate_up[model:, :])

    @pl.when(step == 0)
    def _():
        total[...] = grown

    @pl.when(step > 0)
    def _():
        total[...] += grown

    @pl.when(step == pl.num_programs(0) - 1)
    def _():
        for j in range(nb):
            parts[j][...] = total[j * count : (j + 1) * count, :]


def glu_backward(blocks, gate, up, gate_up, down, places):
    nb = len(blocks)
    count, model = blocks[0].shape
    hidden = len(down) * down[0].shape[0]
    tile = min(HTILE, hidden)
    length = nb * count
    f32, low = jnp.float32, jnp.bfloat16
    column = pl.BlockSpec((length, tile), lambda i: (0, i))
    out = pl.pallas_call(
        partial(glu_grad_kernel, nb, len(down)),
        grid=(hidden // tile,),
        in_specs=[SMEM] + [whole((count, model))] * nb + [column] * 2 + glu_specs(gate_up, down, tile),
        out_specs=[whole((count, model))] * nb + [whole((length, model))] + [column] * 2,
        out_shape=[jax.ShapeDtypeStruct((count, model), f32)] * nb
        + [
            jax.ShapeDtypeStruct((length, model), low),
            jax.ShapeDtypeStruct((length, hidden), low),
            jax.ShapeDtypeStruct((length, hidden), low),
        ],
        scratch_shapes=[pltpu.VMEM((length, model), f32)] + glu_scratch(gate_up, down, tile),
        compiler_params=pltpu.CompilerParams(vmem_limit_bytes=28 * MIB),
        cost_estimate=pl.CostEstimate(flops=int(9.5 * PEAK), bytes_accessed=0, transcendentals=0),
        name="glu_backward",
    )(places, *blocks, gate, up, *gate_up, *down)
    return out[:nb], out[nb:]


def dot32(spec, a, b):
    return jnp.einsum(spec, a, b, preferred_element_type=jnp.float32)


def low(values):
    return values.astype(jnp.bfloat16)


def add(old, new):
    return new if old is None else old + new


def exchange_dq(grad):
    peers = lax.axis_size("dq")
    dq = lax.axis_index("dq")
    parts = low(grad).reshape(peers, grad.shape[0] // peers, grad.shape[1])
    moved = [shift(parts[(dq + k) % peers], "dq", k) for k in range(1, peers)]
    return parts[dq], moved


def total_dq(own, moved):
    total = own.astype(jnp.float32)
    for term in moved:
        total = total + term.astype(jnp.float32)
    return total


def to_section(total, target):
    source = 1 - target
    return permute(low(total), ("section",), lambda s: (target,) if s == source else None)


def own_part(own):
    count = own.shape[0] // lax.axis_size("dq")
    return lax.dynamic_slice_in_dim(own, lax.axis_index("dq") * count, count, 0)


def join_parts(part):
    return [part] + [shift(part, "dq", k) for k in range(1, lax.axis_size("dq"))]


def to_holder(total):
    return permute(low(total), ("core", "th"), lambda c, h: (c, 1 - h) if c != h else None)


def holder_total(total, other):
    return low(total + other.astype(jnp.float32))


def from_holder(values):
    return permute(values, ("core", "th"), lambda c, h: (1 - c, h) if c == h else None)


def join_holders(total):
    peers = lax.axis_size("dq")
    held = [total]
    for k in range(1, peers):
        held.append(
            permute(
                total,
                ("dq", "core", "th"),
                lambda d, c, h: ((d + k) % peers, c, h) if c == h else None,
            )
        )
    return held, [from_holder(part) for part in held]


def assemble_kernel(counts, finish, places, *refs):
    taken = 0
    n_in = 2 * sum(counts)
    n_out = len(refs) - n_in - len(counts)
    outs = refs[n_in : n_in + n_out]
    joined = refs[n_in + n_out :]
    holds = places[len(places) - 1] == 1
    for buffer, nb in zip(joined, counts):
        for j in range(nb):
            held, given = refs[taken + j], refs[taken + nb + j]
            rows = held.shape[0]
            at = pl.ds(pl.multiple_of(places[j] * rows, 8), rows)
            buffer[at, :] = jnp.where(
                holds, held[...].astype(jnp.float32), given[...].astype(jnp.float32)
            )
        taken += 2 * nb
    finish(joined, outs)


def assemble(messages, places, finish, out_shapes):
    counts = [len(held) for held, given in messages]
    vmem = pl.BlockSpec(memory_space=pltpu.VMEM)
    holds = (lax.axis_index("core") == lax.axis_index("th")).astype(jnp.int32)
    return pl.pallas_call(
        partial(assemble_kernel, counts, finish),
        in_specs=[SMEM] + [vmem] * (2 * sum(counts)),
        out_specs=[vmem] * len(out_shapes),
        out_shape=[jax.ShapeDtypeStruct(s, jnp.float32) for s in out_shapes],
        scratch_shapes=[
            pltpu.VMEM((len(held) * held[0].shape[0], held[0].shape[1]), jnp.float32)
            for held, given in messages
        ],
        compiler_params=pltpu.CompilerParams(vmem_limit_bytes=40 * MIB),
        cost_estimate=pl.CostEstimate(flops=int(4 * PEAK), bytes_accessed=0, transcendentals=0),
        name="assemble",
    )(jnp.append(places, holds), *[p for held, given in messages for p in held + given])


def pack(arrays):
    if len({a.shape[1] for a in arrays}) == 1:
        return [jnp.concatenate(arrays, axis=0)]
    return list(arrays)


def row_reader(buffers):
    state = [0, 0]

    def take(rows):
        at, offset = state
        if offset + rows > buffers[at].shape[0]:
            at, offset = at + 1, 0
        state[0], state[1] = at, offset + rows
        return buffers[at][offset : offset + rows, :]

    return take


def per_device(
    tokens,
    segment_ids,
    cotangent,
    norm_gain1,
    w_in,
    short_taps,
    cond_taps,
    spectrum,
    spectral_gain,
    w_out,
    norm_gain2,
    w_gate_up,
    w_down,
):
    slots, row_count, width = tokens.shape
    pack_len = segment_ids.shape[1]
    channels = w_in.shape[3]
    hidden_cols = w_gate_up.shape[3]
    place5 = tuple(lax.axis_index(a) for a in ALL_AXES)
    section, dq, core, high_part, along = place5
    packs = slots // 2
    peers = lax.axis_size("tl")
    order = jnp.stack(
        [jnp.bitwise_xor(core, c) * peers + (along - t) % peers for c in range(2) for t in range(peers)]
    ).astype(jnp.int32)

    tables = spectral_tables(pack_len)

    def own_slots(array):
        return lax.dynamic_slice_in_dim(array, section * packs, packs, 0)

    freqs = spectrum.shape[2]
    dqs = lax.axis_size("dq")
    places = jnp.stack([(dq - k) % dqs for k in range(dqs)]).astype(jnp.int32)
    w_in_t = jnp.transpose(w_in[0], (1, 2, 0)).reshape(3 * channels, width)
    spectrum_t = jnp.transpose(spectrum[0], (0, 2, 1)).reshape(2 * channels, freqs)
    io_own = own_part(jnp.concatenate([w_in_t, w_out[0]], axis=0))
    sp_own = own_part(spectrum_t)
    per = 2 * width // dqs
    gu_own = lax.dynamic_slice(
        w_gate_up[0], (dq * per % width, dq * 2 // dqs, 0), (per, 1, hidden_cols)
    ).reshape(per, hidden_cols)
    dn_own = own_part(w_down[0])
    rows_in, io_part, sp_part, gu_own, dn_own = tie(
        transposed(own_slots(tokens)), transposed(io_own), transposed(sp_own), gu_own, dn_own
    )
    swapped = permute(segment_ids.astype(jnp.float32), ("core",), lambda c: (1 - c,))
    ids_both = jnp.stack([segment_ids, swapped.astype(jnp.int32)])
    segments = own_slots(ids_both[jnp.bitwise_xor(core, high_part)])
    first = section == 0
    own_taps = jnp.concatenate(
        [
            short_taps[0].reshape(9, channels),
            cond_taps[0],
            spectral_gain[0],
            jnp.zeros((2, channels), jnp.float32),
        ],
        axis=0,
    )
    own_taps = transposed(own_taps)
    own_gains = jnp.concatenate([norm_gain1, norm_gain2], axis=0)

    def both_layers(own):
        other = swap_section(own)
        return jnp.stack([jnp.where(first, own, other), jnp.where(first, other, own)])

    taps = both_layers(own_taps)
    gains = both_layers(own_gains)

    def columns(ids):
        prev, nxt = neighbours(ids)
        masks = [(ids == g).astype(jnp.float32) for g in range(SEGS)]
        return jnp.stack([prev, nxt] + masks + [jnp.zeros_like(prev)] * 2, axis=1)

    cols = [columns(segments[index]) for index in range(packs)]
    line = Line()

    def by_layer(part, other):
        return jnp.where(first, part, other), jnp.where(first, other, part)

    w_io, spectra, gate_up, down = [None, None], [None, None], [None, None], [None, None]
    results = [[], []]
    saved = [[], []]
    late = []
    for index in range(packs):
        state = rows_in[index].astype(jnp.float32)
        for layer in range(2):
            opening = index == 0 and layer == 0
            normed, norm_pull = jax.vjp(layer_norm, state, gains[layer, 0])
            blocks = gather_rows(low(normed))
            if opening:
                io_other, sp_other = swap_section(io_part), swap_section(sp_part)
                dn_moved = transposed(dn_own)
                gu_moved = transposed(gu_own)
                blocks, io_other, sp_other = tie(blocks, io_other, sp_other)
                sp_both = by_layer(sp_part, sp_other)
                spectra[0] = join_parts(sp_both[0])
                io_both = by_layer(io_part, io_other)
                w_io[0] = join_parts(io_both[0])
                line.mark(io_both[0], sp_both[0])
                dn_part = line.take(dn_moved)
                dn_other = swap_section(dn_part)
                line.mark(dn_part)
                gu_part = line.take(gu_moved)
                dn_both = by_layer(dn_part, after(dn_other, gu_part))
                blocks, gu_part, dn_first, cot_own = tie(blocks, gu_part, dn_both[0], own_slots(cotangent))
                cot_in = transposed(cot_own)
                gu_other = swap_section(gu_part)
                down[0] = join_parts(dn_first)
            parts, gathered, mix, kept = mixer_forward(
                blocks, w_io[layer], taps[layer : layer + 1], cols[index], spectra[layer], tables,
                order, places, 56 if opening else 36,
            )
            if opening:
                gu_both = by_layer(gu_part, after(gu_other, parts))
                parts, gu_first, cot_in, down[0] = tie(parts, gu_both[0], cot_in, down[0])
            if layer == 1:
                parts, cot_chip = tie(parts, cot_chip)
            if index == 0 and layer == 1:
                parts, gate_up[1] = tie(parts, gate_up[1])
            sums_of = core_sums(parts)
            if opening:
                gate_up[0] = join_parts(gu_first)
            if layer == 1:
                cot_blocks = both_cores(cot_chip)
            moved_sums = sent_sums(sums_of)
            if index == 0 and layer == 1:
                moved_sums, down[1] = tie(moved_sums, down[1])
            hidden = state + add_sums(sums_of, moved_sums)
            normed_two, norm_pull_two = jax.vjp(layer_norm, hidden, gains[layer, 1])
            blocks = gather_rows(low(normed_two))
            if opening:
                io_part, sp_part = after((io_both[1], sp_both[1]), blocks)
                w_io[1] = join_parts(io_part)
                spectra[1] = join_parts(sp_part)
            parts, (gathered_two, gate, up, act) = glu_forward(
                blocks, gate_up[layer], down[layer], places
            )
            saved[layer].append(
                (norm_pull, gathered, mix, kept, norm_pull_two, gathered_two, gate, up, act)
            )
            if layer == 0:
                sums_of = core_sums(parts)
                if opening:
                    gu_part, dn_part = after((gu_both[1], dn_both[1]), sums_of)
                    gate_up[1] = join_parts(gu_part)
                    down[1] = join_parts(dn_part)
                moved_sums = sent_sums(sums_of)
                state = hidden + add_sums(sums_of, moved_sums)
                results[0].append(state)
                cot_chip = chip_blocks(after(cot_in[index], state))
            else:
                late.append((hidden, parts, cot_blocks))

    def deliver(zero, one):
        keep = transposed(jnp.where(first, zero, one))
        given = permute(
            jnp.where(first, one, zero),
            ("section", "core", "th"),
            lambda s, c, h: (1 - s, h, c),
        )
        return keep, given

    def ordered(keep, given):
        lead = jnp.where(first, keep, given)
        trail = jnp.where(first, given, keep)
        return jnp.concatenate([lead, trail], axis=0).astype(jnp.float32)

    sums = [{}, {}]

    def collect(layer, terms, last):
        for name, term in terms.items():
            total = term if name not in sums[layer] else sums[layer][name] + term
            sums[layer][name] = low(total) if last else total.astype(jnp.float32)

    def glu_terms(layer, kept, sums_of, grad_rows, gate_grad, up_grad, last):
        act, rows_two, grad_rows, gate_grad, up_grad = after(
            (kept[8], kept[5], grad_rows, gate_grad, up_grad), sums_of
        )
        half = width // 2
        terms = {
            "down": dot32("lf,ld->fd", act, grad_rows),
            "gate_a": dot32("ld,lf->df", rows_two[:, :half], gate_grad),
            "gate_b": dot32("ld,lf->df", rows_two[:, half:], gate_grad),
            "up": dot32("ld,lf->df", rows_two, up_grad),
        }
        collect(layer, terms, last)

    def small_rows(tap_grad, gain_one, gain_two):
        rows_of = jnp.pad(tap_grad, ((0, 0), (0, width - channels)))
        filled = rows_of.shape[0] + 2
        return jnp.concatenate(
            [rows_of, gain_one, gain_two[None], jnp.zeros((-filled % 64, width), jnp.float32)], axis=0
        )

    def mix_terms(layer, kept, sums_of, mix_rows, proj_grad, spectrum_grad, small, last):
        mix, mix_rows, proj_grad, rows_one = after((kept[2], mix_rows, proj_grad, kept[1]), sums_of)
        terms = {
            "w_in": dot32("lc,ld->cd", proj_grad, rows_one),
            "w_out": dot32("lc,ld->cd", mix, mix_rows),
            "spectrum": spectrum_grad,
            "small": small,
        }
        collect(layer, terms, last)

    contents = (("down", "gate_a"), ("gate_b", "up"), ("w_in", "w_out", "spectrum", "small"))
    own = [{}, {}]
    moved = [{}, {}]
    crossed = [{}, {}]

    def send_dq(layer, m, *events):
            arrays = pack(after([sums[layer][name] for name in contents[m]], *events))
            sent = [exchange_dq(a) for a in arrays]
            own[layer][m] = [s[0] for s in sent]
            moved[layer][m] = [s[1] for s in sent]

    def add_own(layer, m, *events):
        terms = after(moved[layer][m], *events)
        own[layer][m] = [total_dq(o, t) for o, t in zip(own[layer][m], terms)]

    def cross(layer, m):
        crossed[layer][m] = [to_section(o, layer) for o in own[layer][m]]

    total = {}
    held = {}

    def add_total(m, *events):
        terms = after((crossed[0][m], crossed[1][m]), *events)
        total[m] = [
            jnp.where(first, o, p) + jnp.where(first, t, u).astype(jnp.float32)
            for o, p, t, u in zip(own[0][m], own[1][m], *terms)
        ]

    def hold(m):
        held[m] = [to_holder(t) for t in total[m]]

    grads_in = [[], []]
    for index in range(packs):
        last = index == packs - 1
        state = cot_in[index].astype(jnp.float32)
        kept = saved[1][index]
        late_hidden, late_parts, cot_blocks = late[index]
        parts, (grad_rows, gate_grad, up_grad) = glu_backward(
            cot_blocks, kept[6], kept[7], gate_up[1], down[1], places
        )
        sums_of = core_sums(parts)
        glu_terms(1, kept, sums_of, grad_rows, gate_grad, up_grad, last)
        grad_part, gain_two = kept[4](chip_sums(sums_of))
        hidden_grad = state + grad_part
        if last:
            send_dq(1, 0)
            send_dq(1, 1, hidden_grad)
        blocks = gather_rows(low(hidden_grad))
        late_sums = core_sums(after(late_parts, hidden_grad))
        blocks, late_sums = tie(blocks, late_sums)
        late_moved = sent_sums(late_sums)
        parts, mix_rows, proj_grad, spectrum_grad, tap_grad, gain_one = mixer_backward(
            blocks, w_io[1], taps[1:2], cols[index], kept[1], gains[1, 0:1], kept[3], spectra[1],
            tables, order, places,
        )
        parts, late_moved = tie(parts, late_moved)
        if last:
            parts, moved[1][0], moved[1][1] = tie(parts, moved[1][0], moved[1][1])
        sums_of = core_sums(parts)
        results[1].append(late_hidden + add_sums(late_sums, after(late_moved, sums_of)))
        moved_sums = sent_sums(sums_of)
        if last:
            add_own(1, 0, sums_of)
            add_own(1, 1, sums_of)
            moved_sums, own[1][0], own[1][1], results[1][-1] = tie(
                moved_sums, own[1][0], own[1][1], results[1][-1]
            )
            cross(1, 0)
            cross(1, 1)
            out_sent = deliver(low(jnp.stack(results[0])), low(jnp.stack(results[1])))
        state = hidden_grad + kept[0](add_sums(sums_of, moved_sums))[0]
        grads_in[1].append(state)
        small = small_rows(tap_grad, gain_one, gain_two)
        mix_terms(1, kept, state, mix_rows, proj_grad, spectrum_grad, small, last)
        if last:
            send_dq(1, 2)
        kept = saved[0][index]
        blocks = gather_rows(low(state))
        if last:
            blocks, own[1][2] = tie(blocks, own[1][2])
        parts, (grad_rows, gate_grad, up_grad) = glu_backward(
            blocks, kept[6], kept[7], gate_up[0], down[0], places
        )
        if last:
            parts, out_sent = tie(parts, out_sent)
        sums_of = core_sums(parts)
        glu_terms(0, kept, sums_of, grad_rows, gate_grad, up_grad, last)
        moved_sums = sent_sums(sums_of)
        if last:
            send_dq(0, 0)
            layer_out = ordered(*after(out_sent, sums_of))
            moved_sums, own[0][0], layer_out = tie(moved_sums, own[0][0], layer_out)
        grad_part, gain_two = kept[4](add_sums(sums_of, moved_sums))
        hidden_grad = state + grad_part
        blocks = gather_rows(low(hidden_grad))
        if last:
            send_dq(0, 1, hidden_grad)
            add_own(1, 2, blocks)
            blocks, own[0][1], own[1][2] = tie(blocks, own[0][1], own[1][2])
            cross(1, 2)
        parts, mix_rows, proj_grad, spectrum_grad, tap_grad, gain_one = mixer_backward(
            blocks, w_io[0], taps[0:1], cols[index], kept[1], gains[0, 0:1], kept[3], spectra[0],
            tables, order, places,
        )
        small = small_rows(tap_grad, gain_one, gain_two)
        if last:
            parts, moved[0][0], moved[0][1], crossed[1][2] = tie(
                parts, moved[0][0], moved[0][1], crossed[1][2]
            )
            add_own(0, 0, parts)
            parts, own[0][0] = tie(parts, own[0][0])
            cross(0, 0)
            mix_terms(0, kept, parts, mix_rows, proj_grad, spectrum_grad, small, last)
            send_dq(0, 2)
            parts, own[0][2] = tie(parts, own[0][2])
        sums_of = core_sums(parts)
        if last:
            add_own(0, 1, sums_of)
        else:
            mix_terms(0, kept, sums_of, mix_rows, proj_grad, spectrum_grad, small, last)
        moved_sums = sent_sums(sums_of)
        if last:
            break
        grads_in[0].append(hidden_grad + kept[0](add_sums(sums_of, moved_sums))[0])

    line.mark(own[0][1])
    add_total(0, line.events)
    (total[0], own[0][1]) = tie(total[0], own[0][1])
    hold(0)
    cross(0, 1)
    line.mark(total[0])
    joined = {}

    def send_joined(m):
        terms = [holder_total(t, o) for t, o in zip(total[m], line.take(held[m]))]
        line.mark(terms)
        joined[m] = [join_holders(t) for t in terms]

    state = hidden_grad + kept[0](add_sums(sums_of, line.take(moved_sums)))[0]
    grads_in[0].append(state)
    line.mark(state)
    add_own(0, 2, line.events)
    cross(0, 2)
    line.mark(own[0][2])
    grad_sent = deliver(low(jnp.stack(grads_in[0])), low(jnp.stack(grads_in[1])))
    crossed[0][1], grad_sent = tie(crossed[0][1], grad_sent)
    add_total(1, line.events)
    hold(1)
    line.mark(total[1])
    send_joined(0)
    crossed[0][2], held[1] = tie(crossed[0][2], held[1])
    add_total(2)
    hold(2)
    line.mark(total[2])
    send_joined(1)
    held[2], joined[0], joined[1] = tie(held[2], joined[0], joined[1])
    line.mark(held[2])
    send_joined(2)
    grad_in = ordered(*line.take(grad_sent))

    small_count = small.shape[0]

    def finish_wide(buffers, outs):
        take = row_reader(buffers)
        outs[0][...] = take(hidden_cols)
        outs[1][: width // 2, 0, :] = take(width // 2)
        outs[1][width // 2 :, 0, :] = take(width // 2)
        outs[1][:, 1, :] = take(width)

    def finish_rest(buffers, outs):
        take = row_reader(buffers)
        outs[0][...] = take(3 * channels)
        outs[1][...] = take(channels)
        outs[2][...] = take(2 * channels)[:, :freqs]
        outs[3][...] = take(small_count)

    grad_down, grad_gate_up = assemble(
        line.take(joined[0] + joined[1]),
        places,
        finish_wide,
        [(hidden_cols, width), (width, 2, hidden_cols)],
    )
    grad_down, joined[2] = tie(grad_down, joined[2])
    send_joined(2)
    grad_w_in, grad_w_out, grad_spectrum, small_total = assemble(
        joined[2],
        places,
        finish_rest,
        [
            (3 * channels, width),
            (channels, width),
            (2 * channels, freqs),
            (small_count, width),
        ],
    )
    grad_spectrum = grad_spectrum.reshape(2, channels, freqs)
    rows_of = own_taps.shape[0]
    tap_grads = small_total[:rows_of, :channels]
    gain_total = small_total[rows_of : rows_of + 2]
    gain_total = gain_total + permute(gain_total, ("th",), lambda h: (1 - h,))
    gain_moved = [shift(gain_total, "tl", k) for k in range(1, peers)]
    for term in gain_moved:
        gain_total = gain_total + term
    return (
        layer_out[None],
        grad_in[None],
        gain_total[0:1],
        jnp.transpose(grad_w_in.reshape(3, channels, width), (2, 0, 1))[None],
        tap_grads[:9].reshape(1, 3, 3, channels),
        tap_grads[9:12][None],
        jnp.transpose(grad_spectrum, (0, 2, 1))[None],
        tap_grads[12:14][None],
        grad_w_out[None],
        gain_total[1:2],
        grad_gate_up[None],
        grad_down[None],
    )


def solution(mesh):
    sections, dps, tensors = (mesh.shape[a] for a in ("section", "dp", "tensor"))
    devices = mesh.devices.reshape(sections, dps // 2, 2, 2, tensors // 2)
    fine = Mesh(devices, ALL_AXES)
    dp = ("dq", "core")
    tensor = ("th", "tl")
    return jax.shard_map(
        per_device,
        mesh=fine,
        in_specs=(
            P(dp, tensor, None),
            P(dp, None),
            P(dp, tensor, None),
            P("section", None),
            P("section", None, None, tensor),
            P("section", None, None, tensor),
            P("section", None, tensor),
            P("section", None, None, tensor),
            P("section", None, tensor),
            P("section", tensor, None),
            P("section", None),
            P("section", None, None, tensor),
            P("section", tensor, None),
        ),
        out_specs=(
            P("section", dp, tensor, None),
            P("section", dp, tensor, None),
            P("section", None),
            P("section", None, None, tensor),
            P("section", None, None, tensor),
            P("section", None, tensor),
            P("section", None, None, tensor),
            P("section", None, tensor),
            P("section", tensor, None),
            P("section", None),
            P("section", None, None, tensor),
            P("section", tensor, None),
        ),
        check_vma=False,
    )
```

```python
from functools import partial
import math

import jax
import jax.numpy as jnp
import numpy as np
from jax import lax
from jax.experimental import pallas as pl
from jax.experimental.pallas import tpu as pltpu
from jax.sharding import Mesh
from jax.sharding import PartitionSpec as P

SEGS = 4

FTILE = 256
HTILE = 768
PEAK = 1.0e9
MIB = 1024 * 1024

ALL_AXES = ("section", "dq", "core", "th", "tl")


def permute(values, axes, mapping):
    sizes = [lax.axis_size(a) for a in axes]
    pairs = []
    total = math.prod(sizes)
    for source in range(total):
        place = []
        rest = source
        for size in reversed(sizes):
            place.append(rest % size)
            rest //= size
        place = tuple(reversed(place))
        target = mapping(*place)
        if target is None:
            continue
        flat = 0
        for size, at in zip(sizes, target):
            flat = flat * size + at
        pairs.append((source, flat))
    return lax.ppermute(values, axes if len(axes) > 1 else axes[0], pairs)


def swap_core(values):
    return permute(values, ("core",), lambda c: (1 - c,))


def swap_section(values):
    return permute(values, ("section",), lambda s: (1 - s,))


def shift(values, axis, by):
    size = lax.axis_size(axis)
    return permute(values, (axis,), lambda j: ((j + by) % size,))


def transposed(values):
    return permute(values, ("core", "th"), lambda c, h: (h, c))


def chip_blocks(rows):
    return [rows] + [shift(rows, "tl", k) for k in range(1, lax.axis_size("tl"))]


def both_cores(blocks):
    return blocks + [swap_core(block) for block in blocks]


def gather_rows(rows):
    return both_cores(chip_blocks(rows))


def core_sums(blocks):
    peers = lax.axis_size("tl")
    order = list(range(1, peers)) + [0]
    sums = {k: blocks[k] + swap_core(blocks[peers + k]) for k in order}
    return [sums[k] for k in range(peers)]


def sent_sums(sums):
    return [shift(sums[k], "tl", -k) for k in range(1, len(sums))]


def add_sums(sums, moved):
    total = sums[0]
    for term in moved:
        total = total + term.astype(jnp.float32)
    return total


def chip_sums(sums):
    return add_sums(sums, sent_sums(sums))


def after(values, *events):
    return lax.optimization_barrier((values, events))[0]


def tie(*values):
    return lax.optimization_barrier(values)


class Line:
    def __init__(self):
        self.events = ()

    def take(self, values):
        return after(values, self.events)

    def mark(self, *events):
        self.events = events


def layer_norm(values, gain):
    row_mean = jnp.mean(values, axis=-1, keepdims=True)
    centred = values - row_mean
    variance = jnp.mean(centred * centred, axis=-1, keepdims=True)
    return centred * lax.rsqrt(variance + 1e-05) * gain


def neighbours(segments):
    equal = (segments[1:] == segments[:-1]).astype(jnp.float32)
    blank = jnp.zeros((1,), jnp.float32)
    return (jnp.concatenate([blank, equal]), jnp.concatenate([equal, blank]))


def table_size(pack_len):
    return -(-(pack_len + 1) // FTILE) * FTILE


def split(values):
    upper = values.astype(jnp.bfloat16)
    lower = (values - upper.astype(jnp.float32)).astype(jnp.bfloat16)
    return upper, lower


def mm(a, b):
    return jnp.dot(a, b, preferred_element_type=jnp.float32)


def mm_t(a, b):
    return lax.dot_general(a, b, (((1,), (1,)), ((), ())), preferred_element_type=jnp.float32)


def mm3(upper, lower, b_upper, b_lower):
    return mm(upper, b_upper) + (mm(upper, b_lower) + mm(lower, b_upper))


STEP = 32


def tables_kernel(coarse_cos, coarse_sin, fine_cos, fine_sin, cos_hi, cos_lo, sin_hi, sin_lo):
    def body(p, carry):
        cc = coarse_cos[pl.ds(p, 1), :]
        cs = coarse_sin[pl.ds(p, 1), :]
        rows = pl.ds(pl.multiple_of(p * STEP, STEP), STEP)
        upper, lower = split(cc * fine_cos[...] - cs * fine_sin[...])
        cos_hi[rows, :] = upper
        cos_lo[rows, :] = lower
        upper, lower = split(cs * fine_cos[...] + cc * fine_sin[...])
        sin_hi[rows, :] = upper
        sin_lo[rows, :] = lower
        return carry

    lax.fori_loop(0, cos_hi.shape[0] // STEP, body, 0)


def spectral_tables(pack_len):
    size = table_size(pack_len)
    period = 2 * pack_len
    column = np.arange(size, dtype=np.int64)[None, :]
    coarse = (np.arange(size // STEP, dtype=np.int64)[:, None] * STEP * column) % period
    fine = (np.arange(STEP, dtype=np.int64)[:, None] * column) % period
    to_angle = 2.0 * np.pi / period
    small = [f(x * to_angle).astype(np.float32) for x in (coarse, fine) for f in (np.cos, np.sin)]
    return pl.pallas_call(
        tables_kernel,
        out_shape=[jax.ShapeDtypeStruct((size, size), jnp.bfloat16)] * 4,
        cost_estimate=pl.CostEstimate(flops=int(4 * PEAK), bytes_accessed=0, transcendentals=0),
        compiler_params=pltpu.CompilerParams(vmem_limit_bytes=12 * MIB),
        name="tables",
    )(*small)


def row_before(values):
    return pltpu.roll(values, 1, 0)


def row_after(values):
    return pltpu.roll(values, values.shape[0] - 1, 0)


def freq_weight(pack_len, step, shape):
    f = lax.broadcasted_iota(jnp.int32, shape, 0) + step * FTILE
    edge = (f == 0) | (f == pack_len)
    weight = jnp.where(edge, 1.0, 2.0) / (2.0 * pack_len)
    return f <= pack_len, jnp.where(f <= pack_len, weight, 0.0)


def join(whole_rows, parts, places):
    for k, part in enumerate(parts):
        count = part.shape[0]
        at = pl.ds(pl.multiple_of(places[k] * count, 8), count)
        whole_rows[at, :] = part[...]


def mixer_kernel(nb, np_, order, places, *refs):
    rows = refs[:nb]
    w_parts, s_parts = refs[nb : nb + np_], refs[nb + np_ : nb + 2 * np_]
    refs = refs[nb + 2 * np_ :]
    (taps, cols, ch_r, cl_r, sh_r, sl_r, ch_c, cl_c, sh_c, sl_c) = refs[:10]
    parts = refs[10 : nb + 10]
    (gathered, mix, proj, long, cond_hat, piece_hat) = refs[nb + 10 : nb + 16]
    x_hi, x_lo, acc, query, w_in_out, spectrum = refs[nb + 16 :]
    step = pl.program_id(0)
    count = rows[0].shape[0]
    pack_len = proj.shape[0]
    width = mix.shape[2]
    scale = 1.0 / math.sqrt(pack_len)

    @pl.when(step == 0)
    def _():
        join(w_in_out, w_parts, places)
        for j in range(nb):
            gathered[j] = rows[j][...]
            at = pl.ds(pl.multiple_of(order[j] * count, 8), count)
            proj[at, :] = mm_t(rows[j][...], w_in_out[: 3 * width, :])
        prev = cols[:, 0:1]
        nxt = cols[:, 1:2]

        def short(values, w0, w1, w2):
            return w0 * (row_before(values) * prev) + w1 * values + w2 * (row_after(values) * nxt)

        def one(k):
            return short(
                proj[:, k * width : (k + 1) * width],
                taps[0, k : k + 1, :],
                taps[0, 3 + k : 4 + k, :],
                taps[0, 6 + k : 7 + k, :],
            )

        query[...] = one(0)
        condition = short(one(1), taps[0, 9:10, :], taps[0, 10:11, :], taps[0, 11:12, :])
        value = one(2)
        x_hi[pack_len:, :] = jnp.zeros((x_hi.shape[0] - pack_len, x_hi.shape[1]), jnp.bfloat16)
        x_lo[pack_len:, :] = jnp.zeros((x_hi.shape[0] - pack_len, x_hi.shape[1]), jnp.bfloat16)
        pieces = [value * cols[:, 2 + g : 3 + g] for g in range(SEGS)] + [condition]
        for g, piece in enumerate(pieces):
            upper, lower = split(piece)
            x_hi[:pack_len, g * width : (g + 1) * width] = upper
            x_lo[:pack_len, g * width : (g + 1) * width] = lower
        acc[...] = jnp.zeros_like(acc)

    wide = SEGS * width
    hat_re = mm3(ch_r[...], cl_r[...], x_hi[...], x_lo[...])
    hat_im = -mm3(sh_r[...], sl_r[...], x_hi[...], x_lo[...])
    v_re, v_im = hat_re[:, :wide], hat_im[:, :wide]
    c_re, c_im = hat_re[:, wide:], hat_im[:, wide:]
    cond_hat[0] = c_re
    cond_hat[1] = c_im
    piece_hat[0] = v_re
    piece_hat[1] = v_im
    gain_in = taps[0, 12:13, :] * scale
    gain_out = taps[0, 13:14, :]
    inside, weight = freq_weight(pack_len, step, c_re.shape)
    join(spectrum, s_parts, places)
    s_re = jnp.transpose(spectrum[:width, :])
    s_im = jnp.transpose(spectrum[width:, :])
    f_re = jnp.where(inside, s_re + gain_out * jnp.tanh(gain_in * c_re), 0.0) * weight
    f_im = jnp.where(inside, s_im + gain_out * jnp.tanh(gain_in * c_im), 0.0) * weight
    f_re = jnp.concatenate([f_re] * SEGS, axis=1)
    f_im = jnp.concatenate([f_im] * SEGS, axis=1)
    p_hi, p_lo = split(v_re * f_re - v_im * f_im)
    m_hi, m_lo = split(-(v_re * f_im + v_im * f_re))
    acc[...] += mm3(ch_c[...], cl_c[...], p_hi, p_lo) + mm3(sh_c[...], sl_c[...], m_hi, m_lo)

    @pl.when(step == pl.num_programs(0) - 1)
    def _():
        total = acc[:, :width] * cols[:, 2:3]
        for g in range(1, SEGS):
            total = total + acc[:, g * width : (g + 1) * width] * cols[:, 2 + g : 3 + g]
        long[...] = total
        query[...] = query[...] * total
        for j in range(nb):
            at = pl.ds(pl.multiple_of(order[j] * count, 8), count)
            mixed = query[at, :].astype(jnp.bfloat16)
            mix[j] = mixed
            parts[j][...] = mm(mixed, w_in_out[3 * width :, :])


def table_specs(size, pack_len):
    row = pl.BlockSpec((FTILE, size), lambda i: (i, 0))
    col = pl.BlockSpec((pack_len, FTILE), lambda i: (0, i))
    return [row] * 4 + [col] * 4


def whole(shape):
    zeros = (0,) * len(shape)
    return pl.BlockSpec(shape, lambda i: zeros)


def of_layer(layer, shape):
    rest = (0,) * len(shape)
    return pl.BlockSpec((1,) + shape, lambda i: (layer,) + rest)


SMEM = pl.BlockSpec(memory_space=pltpu.SMEM)


def part_specs(w_in_out, spectra):
    return [whole(p.shape) for p in w_in_out] + [
        pl.BlockSpec((p.shape[0], FTILE), lambda i: (0, i)) for p in spectra
    ]


def part_scratch(w_in_out, spectra):
    peers = len(w_in_out)
    return [
        pltpu.VMEM((peers * w_in_out[0].shape[0], w_in_out[0].shape[1]), jnp.bfloat16),
        pltpu.VMEM((peers * spectra[0].shape[0], FTILE), jnp.float32),
    ]


def mixer_forward(blocks, w_in_out, taps, cols, spectra, tables, order, places, mib):
    layer = 0
    pack_len = cols.shape[0]
    nb = len(blocks)
    count, model = blocks[0].shape
    width = taps.shape[2]
    size = tables[0].shape[0]
    f32, low = jnp.float32, jnp.bfloat16
    out = pl.pallas_call(
        partial(mixer_kernel, nb, len(w_in_out)),
        grid=(size // FTILE,),
        in_specs=[SMEM, SMEM]
        + [whole((count, model))] * nb
        + part_specs(w_in_out, spectra)
        + [of_layer(layer, taps.shape[1:]), whole(cols.shape)]
        + table_specs(size, pack_len),
        out_specs=[whole((count, model))] * nb
        + [
            whole((nb, count, model)),
            whole((nb, count, width)),
            whole((pack_len, 3 * width)),
            whole((pack_len, width)),
            pl.BlockSpec((2, FTILE, width), lambda i: (0, i, 0)),
            pl.BlockSpec((2, FTILE, SEGS * width), lambda i: (0, i, 0)),
        ],
        out_shape=[jax.ShapeDtypeStruct((count, model), f32)] * nb
        + [
            jax.ShapeDtypeStruct((nb, count, model), low),
            jax.ShapeDtypeStruct((nb, count, width), low),
            jax.ShapeDtypeStruct((pack_len, 3 * width), f32),
            jax.ShapeDtypeStruct((pack_len, width), f32),
            jax.ShapeDtypeStruct((2, size, width), f32),
            jax.ShapeDtypeStruct((2, size, SEGS * width), f32),
        ],
        scratch_shapes=[
            pltpu.VMEM((size, (SEGS + 1) * width), low),
            pltpu.VMEM((size, (SEGS + 1) * width), low),
            pltpu.VMEM((pack_len, SEGS * width), f32),
            pltpu.VMEM((pack_len, width), f32),
        ]
        + part_scratch(w_in_out, spectra),
        compiler_params=pltpu.CompilerParams(vmem_limit_bytes=mib * MIB),
        cost_estimate=pl.CostEstimate(flops=int(26 * PEAK), bytes_accessed=0, transcendentals=0),
        name="mixer_forward",
    )(order, places, *blocks, *w_in_out, *spectra, taps, cols, *tables, *tables)
    return out[:nb], out[nb].reshape(pack_len, model), out[nb + 1].reshape(pack_len, width), out[nb + 2 :]


def mixer_grad_kernel(nb, np_, order, places, *refs):
    grads = refs[:nb]
    w_parts, s_parts = refs[nb : nb + np_], refs[nb + np_ : nb + 2 * np_]
    refs = refs[nb + 2 * np_ :]
    (taps, cols, normed, gain, proj, long, cond_hat, piece_hat) = refs[:8]
    (ch_r, cl_r, sh_r, sl_r, ch_c, cl_c, sh_c, sl_c) = refs[8:16]
    partials = refs[16 : nb + 16]
    gathered, proj_grad, grad_spectrum, grad_taps, grad_gain = refs[nb + 16 : nb + 21]
    x_hi, x_lo, acc, query_grad, full, w_in_out, spectrum = refs[nb + 21 :]
    step = pl.program_id(0)
    count = grads[0].shape[0]
    pack_len = proj.shape[0]
    width = long.shape[1]
    wide = SEGS * width
    scale = 1.0 / math.sqrt(pack_len)

    def short(values, w0, w1, w2):
        return (
            w0 * (row_before(values) * cols[:, 0:1])
            + w1 * values
            + w2 * (row_after(values) * cols[:, 1:2])
        )

    @pl.when(step == 0)
    def _():
        join(w_in_out, w_parts, places)
        for j in range(nb):
            gathered[j] = grads[j][...]
            at = pl.ds(pl.multiple_of(order[j] * count, 8), count)
            query_grad[at, :] = mm_t(grads[j][...], w_in_out[3 * width :, :])
        query = short(proj[:, :width], taps[0, 0:1, :], taps[0, 3:4, :], taps[0, 6:7, :])
        mix_grad = query_grad[...]
        long_grad = mix_grad * query
        query_grad[...] = mix_grad * long[...]
        x_hi[pack_len:, :] = jnp.zeros((x_hi.shape[0] - pack_len, wide), jnp.bfloat16)
        x_lo[pack_len:, :] = jnp.zeros((x_hi.shape[0] - pack_len, wide), jnp.bfloat16)
        for g in range(SEGS):
            upper, lower = split(long_grad * cols[:, 2 + g : 3 + g])
            x_hi[:pack_len, g * width : (g + 1) * width] = upper
            x_lo[:pack_len, g * width : (g + 1) * width] = lower
        acc[...] = jnp.zeros_like(acc)
        grad_taps[...] = jnp.zeros_like(grad_taps)

    c_re, c_im = cond_hat[0], cond_hat[1]
    inside, weight = freq_weight(pack_len, step, c_re.shape)
    w4 = jnp.concatenate([weight] * SEGS, axis=1)
    b_re = mm3(ch_r[...], cl_r[...], x_hi[...], x_lo[...]) * w4
    b_im = mm3(sh_r[...], sl_r[...], x_hi[...], x_lo[...]) * (-w4)
    v_re, v_im = piece_hat[0], piece_hat[1]

    def over_segments(values):
        total = values[:, :width]
        for g in range(1, SEGS):
            total = total + values[:, g * width : (g + 1) * width]
        return total

    h_re = over_segments(v_re * b_re + v_im * b_im)
    h_im = over_segments(v_re * b_im - v_im * b_re)
    grad_spectrum[0] = jnp.transpose(h_re).astype(jnp.bfloat16)
    grad_spectrum[1] = jnp.transpose(h_im).astype(jnp.bfloat16)
    gain_in = taps[0, 12:13, :] * scale
    gain_out = taps[0, 13:14, :]
    t_re = jnp.tanh(gain_in * c_re)
    t_im = jnp.tanh(gain_in * c_im)
    join(spectrum, s_parts, places)
    f_re = jnp.where(inside, jnp.transpose(spectrum[:width, :]) + gain_out * t_re, 0.0)
    f_im = jnp.where(inside, jnp.transpose(spectrum[width:, :]) + gain_out * t_im, 0.0)
    a_re = h_re * gain_out * (1.0 - t_re * t_re)
    a_im = h_im * gain_out * (1.0 - t_im * t_im)
    grad_taps[12:13, :] += jnp.sum(a_re * c_re + a_im * c_im, axis=0, keepdims=True) * scale
    grad_taps[13:14, :] += jnp.sum(h_re * t_re + h_im * t_im, axis=0, keepdims=True)
    f_re = jnp.concatenate([f_re] * SEGS, axis=1)
    f_im = jnp.concatenate([f_im] * SEGS, axis=1)
    p = jnp.concatenate([f_re * b_re + f_im * b_im, a_re * gain_in], axis=1)
    m = jnp.concatenate([f_im * b_re - f_re * b_im, -(a_im * gain_in)], axis=1)
    p_hi, p_lo = split(p)
    m_hi, m_lo = split(m)
    acc[...] += mm3(ch_c[...], cl_c[...], p_hi, p_lo) + mm3(sh_c[...], sl_c[...], m_hi, m_lo)

    @pl.when(step == pl.num_programs(0) - 1)
    def _():
        prev = cols[:, 0:1]
        nxt = cols[:, 1:2]
        value_grad = acc[:, :width] * cols[:, 2:3]
        for g in range(1, SEGS):
            value_grad = value_grad + acc[:, g * width : (g + 1) * width] * cols[:, 2 + g : 3 + g]

        def column_sum(values):
            return jnp.sum(values, axis=0, keepdims=True)

        def adjoint(values, grad, row, stride):
            w0 = taps[0, row : row + 1, :]
            w1 = taps[0, row + stride : row + stride + 1, :]
            w2 = taps[0, row + 2 * stride : row + 2 * stride + 1, :]
            from_prev = prev * grad
            from_next = nxt * grad
            grad_taps[row : row + 1, :] = column_sum(row_before(values) * from_prev)
            grad_taps[row + stride : row + stride + 1, :] = column_sum(values * grad)
            grad_taps[row + 2 * stride : row + 2 * stride + 1, :] = column_sum(
                row_after(values) * from_next
            )
            return w1 * grad + w0 * row_after(from_prev) + w2 * row_before(from_next)

        key_proj = proj[:, width : 2 * width]
        key_part = short(key_proj, taps[0, 1:2, :], taps[0, 4:5, :], taps[0, 7:8, :])
        key_grad = adjoint(key_part, acc[:, wide:], 9, 1)
        parts = [query_grad[...], key_grad, value_grad]
        for j in range(3):
            full[:, j * width : (j + 1) * width] = adjoint(
                proj[:, j * width : (j + 1) * width], parts[j], j, 3
            )
        for j in range(nb):
            at = pl.ds(pl.multiple_of(order[j] * count, 8), count)
            low = full[at, :].astype(jnp.bfloat16)
            proj_grad[j] = low
            rows_grad = mm(low, w_in_out[: 3 * width, :])
            partials[j][...] = rows_grad
            seen = normed[j * count : (j + 1) * count, :].astype(jnp.float32)
            term = jnp.sum(rows_grad * seen, axis=0, keepdims=True)
            gain_sum = term if j == 0 else gain_sum + term
        grad_gain[...] = gain_sum / gain[...]


def mixer_backward(blocks, w_in_out, taps, cols, normed, gain, kept, spectra, tables, order, places):
    layer = 0
    proj, long, cond_hat, piece_hat = kept
    pack_len = cols.shape[0]
    nb = len(blocks)
    count, model = blocks[0].shape
    width = taps.shape[2]
    size = tables[0].shape[0]
    f32, low = jnp.float32, jnp.bfloat16
    freq = pl.BlockSpec((2, FTILE, width), lambda i: (0, i, 0))
    out = pl.pallas_call(
        partial(mixer_grad_kernel, nb, len(w_in_out)),
        grid=(size // FTILE,),
        in_specs=[SMEM, SMEM]
        + [whole((count, model))] * nb
        + part_specs(w_in_out, spectra)
        + [
            of_layer(layer, taps.shape[1:]),
            whole(cols.shape),
            whole(normed.shape),
            whole(gain.shape),
            whole(proj.shape),
            whole(long.shape),
            freq,
            pl.BlockSpec((2, FTILE, SEGS * width), lambda i: (0, i, 0)),
        ]
        + table_specs(size, pack_len),
        out_specs=[whole((count, model))] * nb
        + [
            whole((nb, count, model)),
            whole((nb, count, 3 * width)),
            pl.BlockSpec((2, width, FTILE), lambda i: (0, 0, i)),
            whole(taps.shape[1:]),
            whole(gain.shape),
        ],
        out_shape=[jax.ShapeDtypeStruct((count, model), f32)] * nb
        + [
            jax.ShapeDtypeStruct((nb, count, model), low),
            jax.ShapeDtypeStruct((nb, count, 3 * width), low),
            jax.ShapeDtypeStruct((2, width, size), low),
            jax.ShapeDtypeStruct(taps.shape[1:], f32),
            jax.ShapeDtypeStruct(gain.shape, f32),
        ],
        scratch_shapes=[
            pltpu.VMEM((size, SEGS * width), low),
            pltpu.VMEM((size, SEGS * width), low),
            pltpu.VMEM((pack_len, (SEGS + 1) * width), f32),
            pltpu.VMEM((pack_len, width), f32),
            pltpu.VMEM((pack_len, 3 * width), f32),
        ]
        + part_scratch(w_in_out, spectra),
        compiler_params=pltpu.CompilerParams(vmem_limit_bytes=40 * MIB),
        cost_estimate=pl.CostEstimate(flops=int(30 * PEAK), bytes_accessed=0, transcendentals=0),
        name="mixer_backward",
    )(
        order, places, *blocks, *w_in_out, *spectra, taps, cols, normed, gain, proj, long, cond_hat,
        piece_hat,
        *tables, *tables,
    )
    rows, proj_grad, grad_spectrum, grad_taps, grad_gain = out[nb:]
    return (
        out[:nb],
        rows.reshape(pack_len, model),
        proj_grad.reshape(pack_len, 3 * width),
        grad_spectrum.reshape(2 * width, size),
        grad_taps,
        grad_gain,
    )


def glu_kernel(nb, np_, places, *refs):
    rows = refs[:nb]
    gu_parts, down_parts = refs[nb : nb + np_], refs[nb + np_ : nb + 2 * np_]
    refs = refs[nb + 2 * np_ :]
    parts = refs[:nb]
    gathered, gate, up, act, total, gate_up, down_w = refs[nb:]
    step = pl.program_id(0)
    count, model = rows[0].shape
    tile = gate.shape[1]
    join(gate_up, gu_parts, places)

    @pl.when(step == 0)
    def _():
        join(down_w, down_parts, places)
        for j in range(nb):
            gathered[j * count : (j + 1) * count, :] = rows[j][...]

    gates = mm(gathered[...], gate_up[:model, :])
    ups = mm(gathered[...], gate_up[model:, :])
    gate[...] = gates
    up[...] = ups
    low = (gates * jax.nn.sigmoid(gates) * ups).astype(jnp.bfloat16)
    act[...] = low
    grown = mm(low, down_w[pl.ds(pl.multiple_of(step * tile, tile), tile), :])

    @pl.when(step == 0)
    def _():
        total[...] = grown

    @pl.when(step > 0)
    def _():
        total[...] += grown

    @pl.when(step == pl.num_programs(0) - 1)
    def _():
        for j in range(nb):
            parts[j][...] = total[j * count : (j + 1) * count, :]


def glu_specs(gate_up, down, tile):
    return [pl.BlockSpec((p.shape[0], tile), lambda i: (0, i)) for p in gate_up] + [
        whole(p.shape) for p in down
    ]


def glu_scratch(gate_up, down, tile):
    peers = len(down)
    return [
        pltpu.VMEM((peers * gate_up[0].shape[0], tile), jnp.bfloat16),
        pltpu.VMEM((peers * down[0].shape[0], down[0].shape[1]), jnp.bfloat16),
    ]


def glu_forward(blocks, gate_up, down, places):
    nb = len(blocks)
    count, model = blocks[0].shape
    hidden = len(down) * down[0].shape[0]
    tile = min(HTILE, hidden)
    length = nb * count
    f32, low = jnp.float32, jnp.bfloat16
    column = pl.BlockSpec((length, tile), lambda i: (0, i))
    out = pl.pallas_call(
        partial(glu_kernel, nb, len(down)),
        grid=(hidden // tile,),
        in_specs=[SMEM] + [whole((count, model))] * nb + glu_specs(gate_up, down, tile),
        out_specs=[whole((count, model))] * nb + [whole((length, model))] + [column] * 3,
        out_shape=[jax.ShapeDtypeStruct((count, model), f32)] * nb
        + [
            jax.ShapeDtypeStruct((length, model), low),
            jax.ShapeDtypeStruct((length, hidden), f32),
            jax.ShapeDtypeStruct((length, hidden), f32),
            jax.ShapeDtypeStruct((length, hidden), low),
        ],
        scratch_shapes=[pltpu.VMEM((length, model), f32)] + glu_scratch(gate_up, down, tile),
        compiler_params=pltpu.CompilerParams(vmem_limit_bytes=34 * MIB),
        cost_estimate=pl.CostEstimate(flops=int(9 * PEAK), bytes_accessed=0, transcendentals=0),
        name="glu_forward",
    )(places, *blocks, *gate_up, *down)
    return out[:nb], out[nb:]


def glu_grad_kernel(nb, np_, places, *refs):
    rows = refs[:nb]
    gate, up = refs[nb : nb + 2]
    gu_parts, down_parts = refs[nb + 2 : nb + 2 + np_], refs[nb + 2 + np_ : nb + 2 + 2 * np_]
    refs = refs[nb + 2 + 2 * np_ :]
    parts = refs[:nb]
    gathered, gate_grad, up_grad, total, gate_up, down_w = refs[nb:]
    step = pl.program_id(0)
    count, model = rows[0].shape
    tile = gate.shape[1]
    join(gate_up, gu_parts, places)

    @pl.when(step == 0)
    def _():
        join(down_w, down_parts, places)
        for j in range(nb):
            gathered[j * count : (j + 1) * count, :] = rows[j][...]

    act_grad = mm_t(gathered[...], down_w[pl.ds(pl.multiple_of(step * tile, tile), tile), :])
    gates = gate[...]
    s = jax.nn.sigmoid(gates)
    low_gate = (act_grad * up[...] * (s * (1.0 + gates * (1.0 - s)))).astype(jnp.bfloat16)
    low_up = (act_grad * (gates * s)).astype(jnp.bfloat16)
    gate_grad[...] = low_gate
    up_grad[...] = low_up
    grown = mm_t(low_gate, gate_up[:model, :]) + mm_t(low_up, gate_up[model:, :])

    @pl.when(step == 0)
    def _():
        total[...] = grown

    @pl.when(step > 0)
    def _():
        total[...] += grown

    @pl.when(step == pl.num_programs(0) - 1)
    def _():
        for j in range(nb):
            parts[j][...] = total[j * count : (j + 1) * count, :]


def glu_backward(blocks, gate, up, gate_up, down, places):
    nb = len(blocks)
    count, model = blocks[0].shape
    hidden = len(down) * down[0].shape[0]
    tile = min(HTILE, hidden)
    length = nb * count
    f32, low = jnp.float32, jnp.bfloat16
    column = pl.BlockSpec((length, tile), lambda i: (0, i))
    out = pl.pallas_call(
        partial(glu_grad_kernel, nb, len(down)),
        grid=(hidden // tile,),
        in_specs=[SMEM] + [whole((count, model))] * nb + [column] * 2 + glu_specs(gate_up, down, tile),
        out_specs=[whole((count, model))] * nb + [whole((length, model))] + [column] * 2,
        out_shape=[jax.ShapeDtypeStruct((count, model), f32)] * nb
        + [
            jax.ShapeDtypeStruct((length, model), low),
            jax.ShapeDtypeStruct((length, hidden), low),
            jax.ShapeDtypeStruct((length, hidden), low),
        ],
        scratch_shapes=[pltpu.VMEM((length, model), f32)] + glu_scratch(gate_up, down, tile),
        compiler_params=pltpu.CompilerParams(vmem_limit_bytes=34 * MIB),
        cost_estimate=pl.CostEstimate(flops=int(9.5 * PEAK), bytes_accessed=0, transcendentals=0),
        name="glu_backward",
    )(places, *blocks, gate, up, *gate_up, *down)
    return out[:nb], out[nb:]


def dot32(spec, a, b):
    return jnp.einsum(spec, a, b, preferred_element_type=jnp.float32)


def low(values):
    return values.astype(jnp.bfloat16)


def add(old, new):
    return new if old is None else old + new


def exchange_dq(grad):
    peers = lax.axis_size("dq")
    dq = lax.axis_index("dq")
    parts = low(grad).reshape(peers, grad.shape[0] // peers, grad.shape[1])
    moved = [shift(parts[(dq + k) % peers], "dq", k) for k in range(1, peers)]
    return parts[dq], moved


def total_dq(own, moved):
    total = own.astype(jnp.float32)
    for term in moved:
        total = total + term.astype(jnp.float32)
    return total


def to_section(total, target):
    source = 1 - target
    return permute(low(total), ("section",), lambda s: (target,) if s == source else None)


def own_part(own):
    count = own.shape[0] // lax.axis_size("dq")
    return lax.dynamic_slice_in_dim(own, lax.axis_index("dq") * count, count, 0)


def join_parts(part):
    return [part] + [shift(part, "dq", k) for k in range(1, lax.axis_size("dq"))]


def to_holder(total):
    return permute(low(total), ("core", "th"), lambda c, h: (c, 1 - h) if c != h else None)


def holder_total(total, other):
    return low(total + other.astype(jnp.float32))


def from_holder(values):
    return permute(values, ("core", "th"), lambda c, h: (1 - c, h) if c == h else None)


def join_holders(total):
    peers = lax.axis_size("dq")
    held = [total]
    for k in range(1, peers):
        held.append(
            permute(
                total,
                ("dq", "core", "th"),
                lambda d, c, h: ((d + k) % peers, c, h) if c == h else None,
            )
        )
    return held, [from_holder(part) for part in held]


def assemble_kernel(counts, finish, places, *refs):
    taken = 0
    n_in = 2 * sum(counts)
    n_out = len(refs) - n_in - len(counts)
    outs = refs[n_in : n_in + n_out]
    joined = refs[n_in + n_out :]
    holds = places[len(places) - 1] == 1
    for buffer, nb in zip(joined, counts):
        for j in range(nb):
            held, given = refs[taken + j], refs[taken + nb + j]
            rows = held.shape[0]
            at = pl.ds(pl.multiple_of(places[j] * rows, 8), rows)
            buffer[at, :] = jnp.where(
                holds, held[...].astype(jnp.float32), given[...].astype(jnp.float32)
            )
        taken += 2 * nb
    finish(joined, outs)


def assemble(messages, places, finish, out_shapes):
    counts = [len(held) for held, given in messages]
    vmem = pl.BlockSpec(memory_space=pltpu.VMEM)
    holds = (lax.axis_index("core") == lax.axis_index("th")).astype(jnp.int32)
    return pl.pallas_call(
        partial(assemble_kernel, counts, finish),
        in_specs=[SMEM] + [vmem] * (2 * sum(counts)),
        out_specs=[vmem] * len(out_shapes),
        out_shape=[jax.ShapeDtypeStruct(s, jnp.float32) for s in out_shapes],
        scratch_shapes=[
            pltpu.VMEM((len(held) * held[0].shape[0], held[0].shape[1]), jnp.float32)
            for held, given in messages
        ],
        compiler_params=pltpu.CompilerParams(vmem_limit_bytes=40 * MIB),
        cost_estimate=pl.CostEstimate(flops=int(4 * PEAK), bytes_accessed=0, transcendentals=0),
        name="assemble",
    )(jnp.append(places, holds), *[p for held, given in messages for p in held + given])


def pack(arrays):
    if len({a.shape[1] for a in arrays}) == 1:
        return [jnp.concatenate(arrays, axis=0)]
    return list(arrays)


def row_reader(buffers):
    state = [0, 0]

    def take(rows):
        at, offset = state
        if offset + rows > buffers[at].shape[0]:
            at, offset = at + 1, 0
        state[0], state[1] = at, offset + rows
        return buffers[at][offset : offset + rows, :]

    return take


def per_device(
    tokens,
    segment_ids,
    cotangent,
    norm_gain1,
    w_in,
    short_taps,
    cond_taps,
    spectrum,
    spectral_gain,
    w_out,
    norm_gain2,
    w_gate_up,
    w_down,
):
    slots, row_count, width = tokens.shape
    pack_len = segment_ids.shape[1]
    channels = w_in.shape[3]
    hidden_cols = w_gate_up.shape[3]
    place5 = tuple(lax.axis_index(a) for a in ALL_AXES)
    section, dq, core, high_part, along = place5
    packs = slots // 2
    peers = lax.axis_size("tl")
    order = jnp.stack(
        [jnp.bitwise_xor(core, c) * peers + (along - t) % peers for c in range(2) for t in range(peers)]
    ).astype(jnp.int32)

    tables = spectral_tables(pack_len)

    def own_slots(array):
        return lax.dynamic_slice_in_dim(array, section * packs, packs, 0)

    freqs = spectrum.shape[2]
    dqs = lax.axis_size("dq")
    places = jnp.stack([(dq - k) % dqs for k in range(dqs)]).astype(jnp.int32)
    w_in_t = jnp.transpose(w_in[0], (1, 2, 0)).reshape(3 * channels, width)
    spectrum_t = jnp.transpose(spectrum[0], (0, 2, 1)).reshape(2 * channels, freqs)
    io_own = own_part(jnp.concatenate([w_in_t, w_out[0]], axis=0))
    sp_own = own_part(spectrum_t)
    per = 2 * width // dqs
    gu_own = lax.dynamic_slice(
        w_gate_up[0], (dq * per % width, dq * 2 // dqs, 0), (per, 1, hidden_cols)
    ).reshape(per, hidden_cols)
    dn_own = own_part(w_down[0])
    rows_in, io_part, sp_part, gu_own, dn_own = tie(
        transposed(own_slots(tokens)), transposed(io_own), transposed(sp_own), gu_own, dn_own
    )
    swapped = permute(segment_ids.astype(jnp.float32), ("core",), lambda c: (1 - c,))
    ids_both = jnp.stack([segment_ids, swapped.astype(jnp.int32)])
    segments = own_slots(ids_both[jnp.bitwise_xor(core, high_part)])
    first = section == 0
    own_taps = jnp.concatenate(
        [
            short_taps[0].reshape(9, channels),
            cond_taps[0],
            spectral_gain[0],
            jnp.zeros((2, channels), jnp.float32),
        ],
        axis=0,
    )
    own_taps = transposed(own_taps)
    own_gains = jnp.concatenate([norm_gain1, norm_gain2], axis=0)

    def both_layers(own):
        other = swap_section(own)
        return jnp.stack([jnp.where(first, own, other), jnp.where(first, other, own)])

    taps = both_layers(own_taps)
    gains = both_layers(own_gains)

    def columns(ids):
        prev, nxt = neighbours(ids)
        masks = [(ids == g).astype(jnp.float32) for g in range(SEGS)]
        return jnp.stack([prev, nxt] + masks + [jnp.zeros_like(prev)] * 2, axis=1)

    cols = [columns(segments[index]) for index in range(packs)]
    line = Line()

    def by_layer(part, other):
        return jnp.where(first, part, other), jnp.where(first, other, part)

    w_io, spectra, gate_up, down = [None, None], [None, None], [None, None], [None, None]
    results = [[], []]
    saved = [[], []]
    late = []
    for index in range(packs):
        state = rows_in[index].astype(jnp.float32)
        for layer in range(2):
            opening = index == 0 and layer == 0
            normed, norm_pull = jax.vjp(layer_norm, state, gains[layer, 0])
            blocks = gather_rows(low(normed))
            if opening:
                io_other, sp_other = swap_section(io_part), swap_section(sp_part)
                dn_moved = transposed(dn_own)
                gu_moved = transposed(gu_own)
                blocks, io_other, sp_other = tie(blocks, io_other, sp_other)
                sp_both = by_layer(sp_part, sp_other)
                spectra[0] = join_parts(sp_both[0])
                io_both = by_layer(io_part, io_other)
                w_io[0] = join_parts(io_both[0])
                line.mark(io_both[0], sp_both[0])
                dn_part = line.take(dn_moved)
                dn_other = swap_section(dn_part)
                line.mark(dn_part)
                gu_part = line.take(gu_moved)
                dn_both = by_layer(dn_part, after(dn_other, gu_part))
                blocks, gu_part, dn_first, cot_own = tie(blocks, gu_part, dn_both[0], own_slots(cotangent))
                cot_in = transposed(cot_own)
                gu_other = swap_section(gu_part)
                down[0] = join_parts(dn_first)
            parts, gathered, mix, kept = mixer_forward(
                blocks, w_io[layer], taps[layer : layer + 1], cols[index], spectra[layer], tables,
                order, places, 56 if opening else 36,
            )
            if opening:
                gu_both = by_layer(gu_part, after(gu_other, parts))
                parts, gu_first, cot_in, down[0] = tie(parts, gu_both[0], cot_in, down[0])
            if layer == 1:
                parts, cot_chip = tie(parts, cot_chip)
            if index == 0 and layer == 1:
                parts, gate_up[1] = tie(parts, gate_up[1])
            sums_of = core_sums(parts)
            if opening:
                gate_up[0] = join_parts(gu_first)
            if layer == 1:
                cot_blocks = both_cores(cot_chip)
            moved_sums = sent_sums(sums_of)
            if index == 0 and layer == 1:
                moved_sums, down[1] = tie(moved_sums, down[1])
            hidden = state + add_sums(sums_of, moved_sums)
            normed_two, norm_pull_two = jax.vjp(layer_norm, hidden, gains[layer, 1])
            blocks = gather_rows(low(normed_two))
            if opening:
                io_part, sp_part = after((io_both[1], sp_both[1]), blocks)
                w_io[1] = join_parts(io_part)
                spectra[1] = join_parts(sp_part)
            parts, (gathered_two, gate, up, act) = glu_forward(
                blocks, gate_up[layer], down[layer], places
            )
            saved[layer].append(
                (norm_pull, gathered, mix, kept, norm_pull_two, gathered_two, gate, up, act)
            )
            if layer == 0:
                sums_of = core_sums(parts)
                if opening:
                    gu_part, dn_part = after((gu_both[1], dn_both[1]), sums_of)
                    gate_up[1] = join_parts(gu_part)
                    down[1] = join_parts(dn_part)
                moved_sums = sent_sums(sums_of)
                state = hidden + add_sums(sums_of, moved_sums)
                results[0].append(state)
                cot_chip = chip_blocks(after(cot_in[index], state))
            else:
                late.append((hidden, parts, cot_blocks))

    def deliver(zero, one):
        keep = transposed(jnp.where(first, zero, one))
        given = permute(
            jnp.where(first, one, zero),
            ("section", "core", "th"),
            lambda s, c, h: (1 - s, h, c),
        )
        return keep, given

    def ordered(keep, given):
        lead = jnp.where(first, keep, given)
        trail = jnp.where(first, given, keep)
        return jnp.concatenate([lead, trail], axis=0).astype(jnp.float32)

    sums = [{}, {}]

    def collect(layer, terms, last):
        for name, term in terms.items():
            total = term if name not in sums[layer] else sums[layer][name] + term
            sums[layer][name] = low(total) if last else total.astype(jnp.float32)

    def glu_terms(layer, kept, sums_of, grad_rows, gate_grad, up_grad, last):
        act, rows_two, grad_rows, gate_grad, up_grad = after(
            (kept[8], kept[5], grad_rows, gate_grad, up_grad), sums_of
        )
        half = width // 2
        terms = {
            "down": dot32("lf,ld->fd", act, grad_rows),
            "gate_a": dot32("ld,lf->df", rows_two[:, :half], gate_grad),
            "gate_b": dot32("ld,lf->df", rows_two[:, half:], gate_grad),
            "up": dot32("ld,lf->df", rows_two, up_grad),
        }
        collect(layer, terms, last)

    def small_rows(tap_grad, gain_one, gain_two):
        rows_of = jnp.pad(tap_grad, ((0, 0), (0, width - channels)))
        filled = rows_of.shape[0] + 2
        return jnp.concatenate(
            [rows_of, gain_one, gain_two[None], jnp.zeros((-filled % 64, width), jnp.float32)], axis=0
        )

    def mix_terms(layer, kept, sums_of, mix_rows, proj_grad, spectrum_grad, small, last):
        mix, mix_rows, proj_grad, rows_one = after((kept[2], mix_rows, proj_grad, kept[1]), sums_of)
        terms = {
            "w_in": dot32("lc,ld->cd", proj_grad, rows_one),
            "w_out": dot32("lc,ld->cd", mix, mix_rows),
            "spectrum": spectrum_grad,
            "small": small,
        }
        collect(layer, terms, last)

    contents = (("down", "gate_a"), ("gate_b", "up"), ("w_in", "w_out", "spectrum", "small"))
    own = [{}, {}]
    moved = [{}, {}]
    crossed = [{}, {}]

    def send_dq(layer, m, *events):
            arrays = pack(after([sums[layer][name] for name in contents[m]], *events))
            sent = [exchange_dq(a) for a in arrays]
            own[layer][m] = [s[0] for s in sent]
            moved[layer][m] = [s[1] for s in sent]

    def add_own(layer, m, *events):
        terms = after(moved[layer][m], *events)
        own[layer][m] = [total_dq(o, t) for o, t in zip(own[layer][m], terms)]

    def cross(layer, m):
        crossed[layer][m] = [to_section(o, layer) for o in own[layer][m]]

    total = {}
    held = {}

    def add_total(m, *events):
        terms = after((crossed[0][m], crossed[1][m]), *events)
        total[m] = [
            jnp.where(first, o, p) + jnp.where(first, t, u).astype(jnp.float32)
            for o, p, t, u in zip(own[0][m], own[1][m], *terms)
        ]

    def hold(m):
        held[m] = [to_holder(t) for t in total[m]]

    grads_in = [[], []]
    for index in range(packs):
        last = index == packs - 1
        state = cot_in[index].astype(jnp.float32)
        kept = saved[1][index]
        late_hidden, late_parts, cot_blocks = late[index]
        parts, (grad_rows, gate_grad, up_grad) = glu_backward(
            cot_blocks, kept[6], kept[7], gate_up[1], down[1], places
        )
        sums_of = core_sums(parts)
        glu_terms(1, kept, sums_of, grad_rows, gate_grad, up_grad, last)
        grad_part, gain_two = kept[4](chip_sums(sums_of))
        hidden_grad = state + grad_part
        if last:
            send_dq(1, 0)
            send_dq(1, 1, hidden_grad)
        blocks = gather_rows(low(hidden_grad))
        late_sums = core_sums(after(late_parts, hidden_grad))
        blocks, late_sums = tie(blocks, late_sums)
        late_moved = sent_sums(late_sums)
        parts, mix_rows, proj_grad, spectrum_grad, tap_grad, gain_one = mixer_backward(
            blocks, w_io[1], taps[1:2], cols[index], kept[1], gains[1, 0:1], kept[3], spectra[1],
            tables, order, places,
        )
        parts, late_moved = tie(parts, late_moved)
        if last:
            parts, moved[1][0], moved[1][1] = tie(parts, moved[1][0], moved[1][1])
        sums_of = core_sums(parts)
        results[1].append(late_hidden + add_sums(late_sums, after(late_moved, sums_of)))
        moved_sums = sent_sums(sums_of)
        if last:
            add_own(1, 0, sums_of)
            add_own(1, 1, sums_of)
            moved_sums, own[1][0], own[1][1], results[1][-1] = tie(
                moved_sums, own[1][0], own[1][1], results[1][-1]
            )
            cross(1, 0)
            cross(1, 1)
            out_sent = deliver(low(jnp.stack(results[0])), low(jnp.stack(results[1])))
        state = hidden_grad + kept[0](add_sums(sums_of, moved_sums))[0]
        grads_in[1].append(state)
        small = small_rows(tap_grad, gain_one, gain_two)
        mix_terms(1, kept, state, mix_rows, proj_grad, spectrum_grad, small, last)
        if last:
            send_dq(1, 2)
        kept = saved[0][index]
        blocks = gather_rows(low(state))
        if last:
            blocks, own[1][2] = tie(blocks, own[1][2])
        parts, (grad_rows, gate_grad, up_grad) = glu_backward(
            blocks, kept[6], kept[7], gate_up[0], down[0], places
        )
        if last:
            parts, out_sent = tie(parts, out_sent)
        sums_of = core_sums(parts)
        glu_terms(0, kept, sums_of, grad_rows, gate_grad, up_grad, last)
        moved_sums = sent_sums(sums_of)
        if last:
            send_dq(0, 0)
            layer_out = ordered(*after(out_sent, sums_of))
            moved_sums, own[0][0], layer_out = tie(moved_sums, own[0][0], layer_out)
        grad_part, gain_two = kept[4](add_sums(sums_of, moved_sums))
        hidden_grad = state + grad_part
        blocks = gather_rows(low(hidden_grad))
        if last:
            send_dq(0, 1, hidden_grad)
            add_own(1, 2, blocks)
            blocks, own[0][1], own[1][2] = tie(blocks, own[0][1], own[1][2])
            cross(1, 2)
        parts, mix_rows, proj_grad, spectrum_grad, tap_grad, gain_one = mixer_backward(
            blocks, w_io[0], taps[0:1], cols[index], kept[1], gains[0, 0:1], kept[3], spectra[0],
            tables, order, places,
        )
        small = small_rows(tap_grad, gain_one, gain_two)
        if last:
            parts, moved[0][0], moved[0][1], crossed[1][2] = tie(
                parts, moved[0][0], moved[0][1], crossed[1][2]
            )
            add_own(0, 0, parts)
            parts, own[0][0] = tie(parts, own[0][0])
            cross(0, 0)
            mix_terms(0, kept, parts, mix_rows, proj_grad, spectrum_grad, small, last)
            send_dq(0, 2)
            parts, own[0][2] = tie(parts, own[0][2])
        sums_of = core_sums(parts)
        if last:
            add_own(0, 1, sums_of)
        else:
            mix_terms(0, kept, sums_of, mix_rows, proj_grad, spectrum_grad, small, last)
        moved_sums = sent_sums(sums_of)
        if last:
            break
        grads_in[0].append(hidden_grad + kept[0](add_sums(sums_of, moved_sums))[0])

    line.mark(own[0][1])
    add_total(0, line.events)
    (total[0], own[0][1]) = tie(total[0], own[0][1])
    hold(0)
    cross(0, 1)
    line.mark(total[0])
    joined = {}

    def send_joined(m):
        terms = [holder_total(t, o) for t, o in zip(total[m], line.take(held[m]))]
        line.mark(terms)
        joined[m] = [join_holders(t) for t in terms]

    state = hidden_grad + kept[0](add_sums(sums_of, line.take(moved_sums)))[0]
    grads_in[0].append(state)
    line.mark(state)
    add_own(0, 2, line.events)
    cross(0, 2)
    line.mark(own[0][2])
    grad_sent = deliver(low(jnp.stack(grads_in[0])), low(jnp.stack(grads_in[1])))
    crossed[0][1], grad_sent = tie(crossed[0][1], grad_sent)
    add_total(1, line.events)
    hold(1)
    line.mark(total[1])
    send_joined(0)
    crossed[0][2], held[1] = tie(crossed[0][2], held[1])
    add_total(2)
    hold(2)
    line.mark(total[2])
    send_joined(1)
    held[2], joined[0], joined[1] = tie(held[2], joined[0], joined[1])
    line.mark(held[2])
    send_joined(2)
    grad_in = ordered(*line.take(grad_sent))

    small_count = small.shape[0]

    def finish_wide(buffers, outs):
        take = row_reader(buffers)
        outs[0][...] = take(hidden_cols)
        outs[1][: width // 2, 0, :] = take(width // 2)
        outs[1][width // 2 :, 0, :] = take(width // 2)
        outs[1][:, 1, :] = take(width)

    def finish_rest(buffers, outs):
        take = row_reader(buffers)
        outs[0][...] = take(3 * channels)
        outs[1][...] = take(channels)
        outs[2][...] = take(2 * channels)[:, :freqs]
        outs[3][...] = take(small_count)

    grad_down, grad_gate_up = assemble(
        line.take(joined[0] + joined[1]),
        places,
        finish_wide,
        [(hidden_cols, width), (width, 2, hidden_cols)],
    )
    grad_down, joined[2] = tie(grad_down, joined[2])
    send_joined(2)
    grad_w_in, grad_w_out, grad_spectrum, small_total = assemble(
        joined[2],
        places,
        finish_rest,
        [
            (3 * channels, width),
            (channels, width),
            (2 * channels, freqs),
            (small_count, width),
        ],
    )
    grad_spectrum = grad_spectrum.reshape(2, channels, freqs)
    rows_of = own_taps.shape[0]
    tap_grads = small_total[:rows_of, :channels]
    gain_total = small_total[rows_of : rows_of + 2]
    gain_total = gain_total + permute(gain_total, ("th",), lambda h: (1 - h,))
    gain_moved = [shift(gain_total, "tl", k) for k in range(1, peers)]
    for term in gain_moved:
        gain_total = gain_total + term
    return (
        layer_out[None],
        grad_in[None],
        gain_total[0:1],
        jnp.transpose(grad_w_in.reshape(3, channels, width), (2, 0, 1))[None],
        tap_grads[:9].reshape(1, 3, 3, channels),
        tap_grads[9:12][None],
        jnp.transpose(grad_spectrum, (0, 2, 1))[None],
        tap_grads[12:14][None],
        grad_w_out[None],
        gain_total[1:2],
        grad_gate_up[None],
        grad_down[None],
    )


def solution(mesh):
    sections, dps, tensors = (mesh.shape[a] for a in ("section", "dp", "tensor"))
    devices = mesh.devices.reshape(sections, dps // 2, 2, 2, tensors // 2)
    fine = Mesh(devices, ALL_AXES)
    dp = ("dq", "core")
    tensor = ("th", "tl")
    return jax.shard_map(
        per_device,
        mesh=fine,
        in_specs=(
            P(dp, tensor, None),
            P(dp, None),
            P(dp, tensor, None),
            P("section", None),
            P("section", None, None, tensor),
            P("section", None, None, tensor),
            P("section", None, tensor),
            P("section", None, None, tensor),
            P("section", None, tensor),
            P("section", tensor, None),
            P("section", None),
            P("section", None, None, tensor),
            P("section", tensor, None),
        ),
        out_specs=(
            P("section", dp, tensor, None),
            P("section", dp, tensor, None),
            P("section", None),
            P("section", None, None, tensor),
            P("section", None, None, tensor),
            P("section", None, tensor),
            P("section", None, None, tensor),
            P("section", None, tensor),
            P("section", tensor, None),
            P("section", None),
            P("section", None, None, tensor),
            P("section", tensor, None),
        ),
        check_vma=False,
    )
```
